512 devices in a mesh: grid: 64 (over y, z), state: 8 (over x, core).
Axes of the slice: x: 4, y: 4, z: 16, core: 2. Of those that a mesh axis runs over, the one named last changes fastest.
Arguments:
- orbitals: float32 [8, 512, 64, 128], P('state', 'grid'), may hold values from -6 to 6
- potential: float32 [512, 64, 128], P('grid'), may hold values from 0 to 2
Outputs:
- corrections: float32 [8, 512, 64, 128], P('state', 'grid')
- correlation_gram: float32 [8, 8], P('state')
The draws below stay inside these ranges and needn't reach their ends.
All inputs are finite; a program needn't handle non-finite values.
Results may differ from the reference program's by a relative error of at most 0.00095.
Values may be sent and summed in bfloat16 or wider, within the bound.
A program may use at most 64 MiB of HBM per device.

```python
import jax
import jax.numpy as jnp
from jax import lax

STATE_DEV = 1
NY = 64
NZ = 128
LEVELS = 4
COARSE_SWEEPS = 3
NSTATE = 8
NX = 512


def block_levels(own_key, shape, shards, low, top_value):
    def one(dim, blocks):
        heights = jax.random.uniform(jax.random.fold_in(jax.random.fold_in(own_key, 6), dim), (blocks,), jnp.float32, low / len(shards), top_value / len(shards))
        return jnp.repeat(jnp.exp(heights), shape[dim] // blocks).reshape((-1,) + (1,) * (len(shape) - dim - 1))

    gain = one(*shards[0])
    for cut in shards[1:]:
        gain = gain * one(*cut)
    return gain


def gaussian(rng, extent, deviation, most, split=(), held_as=jnp.bfloat16):
    array = deviation * jax.random.normal(rng, extent, jnp.float32)
    if split:
        array = array * block_levels(rng, extent, split, -0.22, 0.18)
    return jnp.clip(array, -most, most).astype(held_as)


def setup_inputs(seed: int = 0) -> dict:
    key_of = jax.random.split(jax.random.key(seed), 3)
    return {
        "orbitals": gaussian(key_of[0], (NSTATE, NX, NY, NZ), 1.0, 6.0, ((0, 8), (1, 64)), jnp.float32),
        "potential": jnp.clip(2.0 * jax.random.uniform(key_of[1], (NX, NY, NZ), jnp.float32) ** block_levels(key_of[1], (NX, NY, NZ), ((0, 64),), -0.2, 0.2), 0.0, 2.0),
    }


CENTER = -2.5
NEAR_COEF = 4.0 / 3.0
FAR_COEF = -1.0 / 12.0
SHIFT_TERM = 0.25
DAMPING = 2.0 / 3.0


def laplace_four(values, axis):
    near = jnp.roll(values, 1, axis) + jnp.roll(values, -1, axis)
    far = jnp.roll(values, 2, axis) + jnp.roll(values, -2, axis)
    return CENTER * values + NEAR_COEF * near + FAR_COEF * far


def level_apply(values, inverse):
    beside = jnp.roll(values, 1, 1) + jnp.roll(values, -1, 1)
    beside = beside + jnp.roll(values, 1, 2) + jnp.roll(values, -1, 2)
    beside = beside + jnp.roll(values, 1, 3) + jnp.roll(values, -1, 3)
    return (SHIFT_TERM + 3.0 * inverse) * values - 0.5 * inverse * beside


def restrict(values):
    count, sx, sy, sz = values.shape
    shaped = values.reshape(count, sx // 2, 2, sy // 2, 2, sz // 2, 2)
    return jnp.mean(shaped, axis=(2, 4, 6))


def prolong(values):
    return jnp.repeat(jnp.repeat(jnp.repeat(values, 2, 1), 2, 2), 2, 3)


def jacobi_sweep(iterate, source, inverse):
    diagonal = SHIFT_TERM + 3.0 * inverse
    return iterate + DAMPING * (source - level_apply(iterate, inverse)) / diagonal


def vcycle(source, depth_level):
    inverse = 0.25 ** depth_level
    diagonal = SHIFT_TERM + 3.0 * inverse
    iterate = DAMPING * source / diagonal
    if depth_level == LEVELS - 1:
        for repeat in range(COARSE_SWEEPS - 1):
            iterate = jacobi_sweep(iterate, source, inverse)
        return iterate
    remainder = source - level_apply(iterate, inverse)
    coarse_error = vcycle(restrict(remainder), depth_level + 1)
    iterate = iterate + prolong(coarse_error)
    return jacobi_sweep(iterate, source, inverse)


def reference(orbitals, potential):
    def one_block(block):
        lap = laplace_four(block, 1) + laplace_four(block, 2) + laplace_four(block, 3)
        hpsi = -0.5 * lap + potential[None] * block
        numer = jnp.sum(block * hpsi, axis=(1, 2, 3))
        denom = jnp.sum(block * block, axis=(1, 2, 3))
        energy = numer / denom
        residual = hpsi - energy[:, None, None, None] * block
        return vcycle(residual, 0)

    blocks = orbitals.reshape(NSTATE // STATE_DEV, STATE_DEV, NX, NY, NZ)
    corrections = lax.map(one_block, blocks).reshape(NSTATE, NX, NY, NZ)
    rounded = corrections.astype(jnp.bfloat16).reshape(NSTATE, NX * NY * NZ)
    summed = jnp.dot(rounded, rounded.T, preferred_element_type=jnp.float32)
    correlation_gram = summed / jnp.float32(NX * NY * NZ)
    return corrections, correlation_gram
```

```python
import functools

import jax
import jax.numpy as jnp
from jax import lax
from jax.experimental import pallas as pl
from jax.experimental.pallas import tpu as pltpu
from jax.sharding import PartitionSpec as P

MESH = pl.DeviceIdType.MESH
HIGH = lax.Precision.HIGHEST
F32 = jnp.float32

SHIFT_TERM = 0.25
DAMPING = 2.0 / 3.0
LANES = 128
ROWS = 64
PLANES = 8
STATES = 8
RING = 16
REACH = 3


def scales(level):
    inverse = 0.25**level
    diagonal = SHIFT_TERM + 3.0 * inverse
    scaled = DAMPING / diagonal
    return scaled, 0.5 * inverse * scaled


def iota(shape, dim):
    return lax.broadcasted_iota(jnp.int32, shape, dim)


def beside(plane, segment):
    rows = plane.shape[0]
    total = pltpu.roll(plane, 1, 0) + pltpu.roll(plane, rows - 1, 0)
    low, high = pltpu.roll(plane, 1, 1), pltpu.roll(plane, LANES - 1, 1)
    if segment != LANES:
        cell = iota(plane.shape, 1) & (segment - 1)
        low = jnp.where(cell == 0, pltpu.roll(plane, LANES - segment + 1, 1), low)
        high = jnp.where(cell == segment - 1, pltpu.roll(plane, segment - 1, 1), high)
    return total + (low + high)


def beside_two(plane):
    rows = plane.shape[0]
    total = pltpu.roll(plane, 2, 0) + pltpu.roll(plane, rows - 2, 0)
    return total + (pltpu.roll(plane, 2, 1) + pltpu.roll(plane, LANES - 2, 1))


def matrices():
    k, j = iota((LANES, LANES), 0), iota((LANES, LANES), 1)
    down_h = (j < 64) & ((k >> 1) == j)
    down_o = (j >= 64) & ((k >> 1) == j - 64)
    down_two = ((k >> 6) == ((j >> 5) & 1)) & (((k & 63) >> 1) == (j & 31))
    down_three = (k < 64) & ((k >> 5) == ((j >> 4) & 1)) & (((k & 31) >> 1) == (j & 15))
    up_two = (k < 32) & ((k >> 4) == ((j >> 5) & 1)) & ((k & 15) == ((j & 31) >> 1))
    up_one = (k < 64) & ((k >> 5) == (j >> 6)) & ((k & 31) == ((j & 63) >> 1))
    up_zero = k == (j >> 1)
    eighth, one = jnp.full((LANES, LANES), 0.125, F32), jnp.ones((LANES, LANES), F32)
    zero = jnp.zeros((LANES, LANES), F32)
    return [
        jnp.where(mask, eighth, zero) for mask in (down_h, down_o, down_two, down_three)
    ] + [jnp.where(mask, one, zero) for mask in (up_two, up_one, up_zero)]


def times(left, right):
    return jnp.dot(left, right, precision=HIGH, preferred_element_type=F32)


def kernel(
    slabs,
    o_hbm, p_hbm, out_ref, gram_ref,
    o_buf, p_buf, h_buf, pair_buf, mats, f1_buf, f2_buf, f3_buf, two_buf, three_buf,
    up2_buf, up1_buf, up0_buf, e_y, e_z, rounded, mixed, rows_buf, g_z, g_xy,
    load_sem, halo_send, halo_recv, f1_send, f1_recv, f23_send, f23_recv,
    ey_send, ey_recv, ez_send, ez_recv, x_send, x_recv, gz_send, gz_recv, gx_send, gx_recv,
):
    g, s = lax.axis_index("grid"), lax.axis_index("state")
    y, z = g // RING, g % RING
    columns = slabs // RING

    def slab(step):
        return (lax.rem(g + step + slabs, slabs), s)

    def on_ring(step):
        return (y * RING + lax.rem(z + step, RING), s)

    def on_column(step):
        return (lax.rem(y + step, columns) * RING + z, s)

    def on_face(step):
        up, side = step // STATES, step % STATES
        return (lax.rem(y + up, columns) * RING + z, lax.rem(s + side, STATES))

    def send(src, dst, send_sem, recv_sem, peer):
        return pltpu.make_async_remote_copy(
            src_ref=src, dst_ref=dst, send_sem=send_sem, recv_sem=recv_sem,
            device_id=peer, device_id_type=MESH,
        )

    loads = [
        pltpu.make_async_copy(o_hbm.at[0], o_buf.at[pl.ds(3, PLANES)], load_sem.at[0]),
        pltpu.make_async_copy(p_hbm, p_buf.at[pl.ds(1, PLANES)], load_sem.at[1]),
    ]
    for load in loads:
        load.start()

    peers = [slab(d) for step in range(1, REACH + 1) for d in (step, -step)]
    peers += [on_ring(d) for d in range(1, RING)]
    peers += [on_face(d) for d in range(1, STATES * columns)]
    barrier = pltpu.get_barrier_semaphore()
    for peer in peers:
        pl.semaphore_signal(barrier, inc=1, device_id=peer, device_id_type=MESH)
    pl.semaphore_wait(barrier, len(peers))

    halos = [
        send(o_hbm.at[0, pl.ds(5, 3)], o_buf.at[pl.ds(0, 3)], halo_send.at[0], halo_recv.at[0], slab(1)),
        send(o_hbm.at[0, pl.ds(0, 3)], o_buf.at[pl.ds(11, 3)], halo_send.at[1], halo_recv.at[1], slab(-1)),
        send(p_hbm.at[pl.ds(7, 1)], p_buf.at[pl.ds(0, 1)], halo_send.at[2], halo_recv.at[2], slab(1)),
        send(p_hbm.at[pl.ds(0, 1)], p_buf.at[pl.ds(9, 1)], halo_send.at[3], halo_recv.at[3], slab(-1)),
    ]
    for copy in halos:
        copy.start()
    for index, matrix in enumerate(matrices()):
        mats[index] = matrix
    rows_buf[...] = jnp.zeros_like(rows_buf)
    for load in loads:
        load.wait()

    c0, k0 = scales(0)
    near = {}

    def apply_h(p):
        centre = o_buf[p + 3]
        first = (o_buf[p + 2] + o_buf[p + 4]) + beside(centre, LANES)
        second = (o_buf[p + 1] + o_buf[p + 5]) + beside_two(centre)
        value = (3.75 + p_buf[p + 1]) * centre - (2.0 / 3.0) * first + (1.0 / 24.0) * second
        h_buf[p + 1] = value
        if 0 <= p < PLANES:
            up0_buf[p] = centre * (1.0 / 3.0) + k0 * first
        return value

    for p in range(2, PLANES - 2):
        apply_h(p)
    for copy in halos:
        copy.wait()
    for p in (-1, 0, 1, PLANES - 2, PLANES - 1, PLANES):
        apply_h(p)

    top = jnp.zeros((ROWS, LANES), F32)
    bottom = jnp.zeros((ROWS, LANES), F32)
    for p in range(PLANES):
        centre = o_buf[p + 3]
        top += centre * h_buf[p + 1]
        bottom += centre * centre
    top, bottom = jnp.sum(top, 0, keepdims=True), jnp.sum(bottom, 0, keepdims=True)
    lane_row = iota((1, LANES), 1)
    e_y[y] = jnp.where(
        lane_row < 64, top + pltpu.roll(top, 64, 1), bottom + pltpu.roll(bottom, 64, 1)
    )
    energy_y = [
        send(e_y.at[y], e_y.at[y], ey_send.at[d - 1], ey_recv.at[d - 1], on_column(d))
        for d in range(1, columns)
    ]
    for copy in energy_y:
        copy.start()

    for q in range(PLANES // 2):
        both_h = None
        for p in (2 * q, 2 * q + 1):
            value = h_buf[p + 1]
            around = (h_buf[p] + h_buf[p + 2]) + beside(value, LANES)
            rest = value * (1.0 / 3.0) + k0 * around
            both_h = rest if both_h is None else both_h + rest
        pair_buf[q] = both_h
        pair_buf[q + 4] = up0_buf[2 * q] + up0_buf[2 * q + 1]
    halved = pair_buf[:, pl.ds(0, 32, 2), :] + pair_buf[:, pl.ds(1, 32, 2), :]
    f1 = times(halved[:4].reshape(LANES, LANES), mats[0]) + times(
        halved[4:].reshape(LANES, LANES), mats[1]
    )
    f1_buf[3:7] = f1.reshape(4, 32, LANES)
    first = [
        send(f1_buf.at[pl.ds(4, 3)], f1_buf.at[pl.ds(0, 3)], f1_send.at[0], f1_recv.at[0], slab(1)),
        send(f1_buf.at[pl.ds(3, 3)], f1_buf.at[pl.ds(7, 3)], f1_send.at[1], f1_recv.at[1], slab(-1)),
    ]
    for copy in first:
        copy.start()

    for copy in energy_y:
        copy.wait()
    e_z[z] = jnp.sum(e_y[...], axis=0)
    energy_z = [
        send(e_z.at[z], e_z.at[z], ez_send.at[d - 1], ez_recv.at[d - 1], on_ring(d))
        for d in range(1, RING)
    ]
    for copy in energy_z:
        copy.start()
    for copy in first:
        copy.wait()

    c1, k1 = scales(1)
    c2, k2 = scales(2)
    c3, k3 = scales(3)

    def remainder(buf, index, factor, segment):
        plane = buf[index]
        around = (buf[index - 1] + buf[index + 1]) + beside(plane, segment)
        return plane * (1.0 / 3.0) + factor * around

    for q in range(4):
        two_buf[q] = remainder(f1_buf, 2 * q + 1, k1, 64) + remainder(f1_buf, 2 * q + 2, k1, 64)
    halved = two_buf[:, pl.ds(0, 16, 2), :] + two_buf[:, pl.ds(1, 16, 2), :]
    f2_buf[1:5] = times(halved.reshape(64, LANES), mats[2]).reshape(4, 16, LANES)
    second = [
        send(f2_buf.at[3], f2_buf.at[5], f23_send.at[0], f23_recv.at[0], slab(-1)),
        send(f2_buf.at[2], f2_buf.at[0], f23_send.at[1], f23_recv.at[1], slab(1)),
    ]
    three_buf[...] = remainder(f2_buf, 2, k2, 32) + remainder(f2_buf, 3, k2, 32)
    halved = three_buf[pl.ds(0, 8, 2), :] + three_buf[pl.ds(1, 8, 2), :]
    f3_buf[REACH] = times(halved, mats[3])
    third = []
    for d in range(1, REACH + 1):
        for step in (d, -d):
            at = len(third) + 2
            third.append(
                send(f3_buf.at[REACH], f3_buf.at[REACH - step], f23_send.at[at], f23_recv.at[at], slab(step))
            )
    for copy in third[::-1] + second:
        copy.start()
    for copy in second + third:
        copy.wait()

    source = {p: f3_buf[p + REACH] for p in range(-REACH, REACH + 1)}
    iterate = {p: c3 * source[p] for p in source}
    for reach in (REACH - 1, REACH - 2):
        iterate = {
            p: iterate[p] * (1.0 / 3.0) + c3 * source[p]
            + k3 * ((iterate[p - 1] + iterate[p + 1]) + beside(iterate[p], 16))
            for p in range(-reach, reach + 1)
        }
    for p in range(-1, 2):
        spread = times(iterate[p], mats[4])
        up2_buf[p + 1, pl.ds(0, 8, 2), :] = spread
        up2_buf[p + 1, pl.ds(1, 8, 2), :] = spread
    fixed = {p: c2 * f2_buf[p + 2] + up2_buf[(p >> 1) + 1] for p in range(-2, 4)}
    for p in range(-1, 3):
        value = (
            fixed[p] * (1.0 / 3.0) + c2 * f2_buf[p + 2]
            + k2 * ((fixed[p - 1] + fixed[p + 1]) + beside(fixed[p], 32))
        )
        spread = times(value, mats[5])
        up1_buf[p + 1, pl.ds(0, 16, 2), :] = spread
        up1_buf[p + 1, pl.ds(1, 16, 2), :] = spread
    fixed = {p: c1 * f1_buf[p + 3] + up1_buf[(p >> 1) + 1] for p in range(-2, 6)}
    error = {
        p: fixed[p] * (1.0 / 3.0) + c1 * f1_buf[p + 3]
        + k1 * ((fixed[p - 1] + fixed[p + 1]) + beside(fixed[p], 64))
        for p in range(-1, 5)
    }

    for copy in energy_z:
        copy.wait()
    sums = jnp.sum(e_z[...], axis=0)
    numer = jnp.sum(jnp.where(lane_row < 64, sums, 0.0), axis=1, keepdims=True)
    denom = jnp.sum(jnp.where(lane_row < 64, 0.0, sums), axis=1, keepdims=True)
    energy = numer / denom
    for p in range(-1, 5):
        spread = times(error[p] - energy * pltpu.roll(error[p], 64, 1), mats[6])
        up0_buf[p + 1, pl.ds(0, 32, 2), :] = spread
        up0_buf[p + 1, pl.ds(1, 32, 2), :] = spread
    for p in range(-1, PLANES + 1):
        residual = h_buf[p + 1] - energy * o_buf[p + 3]
        h_buf[p + 1] = residual
        p_buf[p + 1] = c0 * residual + up0_buf[(p >> 1) + 1]
    for p in range(PLANES):
        value = p_buf[p + 1]
        around = (p_buf[p] + p_buf[p + 2]) + beside(value, LANES)
        value = value * (1.0 / 3.0) + c0 * h_buf[p + 1] + k0 * around
        out_ref[0, p] = value
        rounded[p] = value.astype(jnp.bfloat16)
    mix = []
    for d in range(1, STATES):
        to = lax.rem(s + d, STATES)
        mix.append(send(rounded.at[to], mixed.at[s], x_send.at[d - 1], x_recv.at[d - 1], (g, to)))
    for copy in mix:
        copy.start()
    mixed[s] = rounded[s]
    for copy in mix:
        copy.wait()

    pairs = [(i, j) for i in range(STATES) for j in range(i, STATES)]
    held = {pair: None for pair in pairs}
    for block in range(ROWS // 16):
        values = [mixed[i, 16 * block : 16 * block + 16].astype(F32) for i in range(STATES)]
        for i, j in pairs:
            product = values[i] * values[j]
            product = product[:8] + product[8:]
            held[i, j] = product if held[i, j] is None else held[i, j] + product
    for i, j in pairs:
        row = jnp.sum(held[i, j], 0, keepdims=True)
        rows_buf[8 * i + j : 8 * i + j + 1] = row
        if i != j:
            rows_buf[8 * j + i : 8 * j + i + 1] = row
    flat = lax.dot_general(
        jnp.ones((8, LANES), F32), rows_buf[...], (((1,), (1,)), ((), ())),
        precision=HIGH, preferred_element_type=F32,
    )
    g_z[z] = flat[:1]
    gram_z = [
        send(g_z.at[z], g_z.at[z], gz_send.at[d - 1], gz_recv.at[d - 1], on_ring(d))
        for d in range(1, RING)
    ]
    for copy in gram_z:
        copy.start()
    for copy in gram_z:
        copy.wait()
    mine = y * STATES + s
    g_xy[mine] = jnp.sum(g_z[...], axis=0)
    gram_xy = [
        send(g_xy.at[mine], g_xy.at[mine], gx_send.at[d - 1], gx_recv.at[d - 1], on_face(d))
        for d in range(1, STATES * columns)
    ]
    for copy in gram_xy:
        copy.start()
    for copy in gram_xy:
        copy.wait()
    total = jnp.sum(g_xy[...], axis=0)
    picked = jnp.zeros((1, STATES), F32)
    for t in range(STATES):
        picked += jnp.where(s == t, total[:, STATES * t : STATES * t + STATES], 0.0)
    gram_ref[...] = picked / F32(PLANES * ROWS * LANES * slabs)


def solution(mesh):
    slabs = mesh.shape["grid"]
    columns = slabs // RING
    faces = STATES * columns
    dma = pltpu.SemaphoreType.DMA

    def on_device(orbitals, potential):
        return pl.pallas_call(
            functools.partial(kernel, slabs),
            out_shape=(
                jax.ShapeDtypeStruct((1, PLANES, ROWS, LANES), F32),
                jax.ShapeDtypeStruct((1, STATES), F32),
            ),
            in_specs=[pl.BlockSpec(memory_space=pl.ANY)] * 2,
            out_specs=(
                pl.BlockSpec(memory_space=pltpu.VMEM),
                pl.BlockSpec(memory_space=pltpu.VMEM),
            ),
            scratch_shapes=[
                pltpu.VMEM((PLANES + 6, ROWS, LANES), F32),
                pltpu.VMEM((PLANES + 2, ROWS, LANES), F32),
                pltpu.VMEM((PLANES + 2, ROWS, LANES), F32),
                pltpu.VMEM((8, ROWS, LANES), F32),
                pltpu.VMEM((7, LANES, LANES), F32),
                pltpu.VMEM((10, 32, LANES), F32),
                pltpu.VMEM((6, 16, LANES), F32),
                pltpu.VMEM((2 * REACH + 1, 8, LANES), F32),
                pltpu.VMEM((4, 32, LANES), F32),
                pltpu.VMEM((16, LANES), F32),
                pltpu.VMEM((3, 16, LANES), F32),
                pltpu.VMEM((4, 32, LANES), F32),
                pltpu.VMEM((8, ROWS, LANES), F32),
                pltpu.VMEM((columns, 1, LANES), F32),
                pltpu.VMEM((RING, 1, LANES), F32),
                pltpu.VMEM((PLANES, ROWS, LANES), jnp.bfloat16),
                pltpu.VMEM((STATES, ROWS, LANES), jnp.bfloat16),
                pltpu.VMEM((LANES, LANES), F32),
                pltpu.VMEM((RING, 1, LANES), F32),
                pltpu.VMEM((faces, 1, LANES), F32),
                dma((2,)), dma((4,)), dma((4,)), dma((2,)), dma((2,)), dma((8,)), dma((8,)),
                dma((columns - 1,)), dma((columns - 1,)), dma((RING - 1,)), dma((RING - 1,)),
                dma((STATES - 1,)), dma((STATES - 1,)), dma((RING - 1,)), dma((RING - 1,)),
                dma((faces - 1,)), dma((faces - 1,)),
            ],
            compiler_params=pltpu.CompilerParams(
                collective_id=0, has_side_effects=True, vmem_limit_bytes=32 * 1024 * 1024
            ),
        )(orbitals, potential)

    return jax.shard_map(
        on_device,
        mesh=mesh,
        in_specs=(P("state", "grid", None, None), P("grid", None, None)),
        out_specs=(P("state", "grid", None, None), P("state", None)),
        check_vma=False,
    )
```

```python
import functools

import jax
import jax.numpy as jnp
from jax import lax
from jax.experimental import pallas as pl
from jax.experimental.pallas import tpu as pltpu
from jax.sharding import PartitionSpec as P

MESH = pl.DeviceIdType.MESH
HIGH = lax.Precision.HIGHEST
F32 = jnp.float32

SHIFT_TERM = 0.25
DAMPING = 2.0 / 3.0
LANES = 128
ROWS = 64
HALF = ROWS // 2
PLANES = 8
STATES = 8
CHIPS = 4
RING = 16
REACH = 4
THIRD = 1.0 / 3.0
NEAR = -2.0 / 3.0
FAR = 1.0 / 24.0


def scales(level):
    inverse = 0.25**level
    diagonal = SHIFT_TERM + 3.0 * inverse
    scaled = DAMPING / diagonal
    return scaled, 0.5 * inverse * scaled


C0, K0 = scales(0)
C1, K1 = scales(1)
C2, K2 = scales(2)
C3, K3 = scales(3)


def iota(shape, dim):
    return lax.broadcasted_iota(jnp.int32, shape, dim)


def beside(plane, segment=LANES):
    rows = plane.shape[0]
    total = pltpu.roll(plane, 1, 0) + pltpu.roll(plane, rows - 1, 0)
    low, high = pltpu.roll(plane, 1, 1), pltpu.roll(plane, LANES - 1, 1)
    if segment != LANES:
        cell = iota(plane.shape, 1) & (segment - 1)
        low = jnp.where(cell == 0, pltpu.roll(plane, LANES - segment + 1, 1), low)
        high = jnp.where(cell == segment - 1, pltpu.roll(plane, segment - 1, 1), high)
    return total + (low + high)


def beside_two(plane):
    rows = plane.shape[0]
    total = pltpu.roll(plane, 2, 0) + pltpu.roll(plane, rows - 2, 0)
    return total + (pltpu.roll(plane, 2, 1) + pltpu.roll(plane, LANES - 2, 1))


def matrices():
    k, j = iota((LANES, LANES), 0), iota((LANES, LANES), 1)
    down_h = (j < 64) & ((k >> 1) == j)
    down_o = (j >= 64) & ((k >> 1) == j - 64)
    down_two = ((k >> 6) == ((j >> 5) & 1)) & (((k & 63) >> 1) == (j & 31))
    down_three = (k < 64) & ((k >> 5) == ((j >> 4) & 1)) & (((k & 31) >> 1) == (j & 15))
    up_two = (k < 32) & ((k >> 4) == ((j >> 5) & 1)) & ((k & 15) == ((j & 31) >> 1))
    up_one = (k < 64) & ((k >> 5) == (j >> 6)) & ((k & 31) == ((j & 63) >> 1))
    up_h = k == (j >> 1)
    up_o = k - 64 == (j >> 1)
    eighth, one = jnp.full((LANES, LANES), 0.125, F32), jnp.ones((LANES, LANES), F32)
    zero = jnp.zeros((LANES, LANES), F32)
    return [
        jnp.where(mask, eighth, zero) for mask in (down_h, down_o, down_two, down_three)
    ] + [jnp.where(mask, one, zero) for mask in (up_two, up_one, up_h, up_o)]


def times(left, right):
    return jnp.dot(left, right, precision=HIGH, preferred_element_type=F32)


def kernel(
    slabs,
    o_hbm, p_hbm, out_ref, gram_ref,
    o_buf, p_buf, h_buf, r_buf, g_out, g_in, pair_buf, mats,
    f1_buf, two_buf, f2_out, f2_in, three_buf, f3_in,
    up2_buf, up1_buf, uph_buf, upo_buf, a_buf, b_buf,
    e_y, e_z, rounded, mixed, rows_buf, g_z, g_xy,
    load_sem, halo_send, halo_recv, f1_sem, f2_sem, f3_sem, ey_sem, ez_sem, x_sem, gz_sem, gx_sem,
    token,
):
    g, s = lax.axis_index("grid"), lax.axis_index("state")
    y, z = g // RING, g % RING
    x, core = s // 2, s % 2
    columns = slabs // RING

    def slab(step):
        return (lax.rem(g + step + slabs, slabs), s)

    def on_ring(step):
        return (y * RING + lax.rem(z + step + RING, RING), s)

    def on_column(step):
        return (lax.rem(y + step + columns, columns) * RING + z, s)

    def state_at(step, other):
        return 2 * lax.rem(x + step + CHIPS, CHIPS) + (lax.rem(core + 1, 2) if other else core)

    def on_face(step):
        up, side = step // STATES, step % STATES
        return (lax.rem(y + up, columns) * RING + z, lax.rem(s + side, STATES))

    def send(src, dst, sems, peer):
        copy = pltpu.make_async_remote_copy(
            src_ref=src, dst_ref=dst, send_sem=sems[0], recv_sem=sems[1],
            device_id=peer, device_id_type=MESH,
        )
        copy.start()

    def take(sem, view):
        pltpu.make_async_copy(view, view, sem).wait()

    def signal(sem, peers):
        for peer in peers:
            pl.semaphore_signal(sem, inc=1, device_id=peer, device_id_type=MESH)

    partner = (g, state_at(0, True))
    close = [slab(1), slab(-1), on_ring(1), on_ring(-1), on_column(1), on_column(-1)]
    close += [(g, state_at(1, False)), (g, state_at(-1, False))]
    barrier = pltpu.get_barrier_semaphore()
    signal(barrier, close + [partner])
    loads = [
        pltpu.make_async_copy(o_hbm.at[0], o_buf.at[pl.ds(2, PLANES)], load_sem.at[0]),
        pltpu.make_async_copy(p_hbm, p_buf, load_sem.at[1]),
    ]
    for load in loads:
        load.start()
    with jax.named_scope("w_barrier"):
        pl.semaphore_wait(barrier, len(close) + 1)

    right, left = slab(1), slab(-1)

    def halo(part, mine, theirs):
        sems = (halo_send, halo_recv.at[part])
        send(o_hbm.at[0, pl.ds(6, 2), pl.ds(mine, HALF)], o_buf.at[pl.ds(0, 2), pl.ds(mine, HALF)], sems, right)
        send(o_hbm.at[0, pl.ds(0, 2), pl.ds(theirs, HALF)], o_buf.at[pl.ds(10, 2), pl.ds(theirs, HALF)], sems, left)

    signal(token.at[0], close)
    halo(0, 0, HALF)
    with jax.named_scope("w_load"):
        for load in loads:
            load.wait()
    g_out[0] = p_buf[0] * o_buf[2] + FAR * o_buf[4]
    g_out[1] = p_buf[7] * o_buf[9] + FAR * o_buf[7]
    with jax.named_scope("w_t1"):
        pl.semaphore_wait(token.at[0], len(close))
    signal(token.at[1], [slab(2), slab(-2), on_ring(2), on_ring(-2)])
    halo(1, HALF, 0)
    sems = (halo_send, halo_recv.at[2])
    send(g_out.at[1], g_in.at[0], sems, right)
    send(g_out.at[0], g_in.at[1], sems, left)

    top = jnp.zeros((ROWS, LANES), F32)
    bottom = jnp.zeros((ROWS, LANES), F32)
    for p in range(PLANES):
        centre = o_buf[p + 2]
        first, second = beside(centre), beside_two(centre)
        for q in (p - 1, p + 1):
            if 0 <= q < PLANES:
                first += o_buf[q + 2]
        for q in (p - 2, p + 2):
            if 0 <= q < PLANES:
                second += o_buf[q + 2]
        value = (3.75 + p_buf[p]) * centre + NEAR * first + FAR * second
        h_buf[p + 1] = value
        r_buf[p] = centre * THIRD + K0 * first
        top += centre * value
        bottom += centre * centre
    for index, matrix in enumerate(matrices()):
        mats[index] = matrix
    rows_buf[...] = jnp.zeros_like(rows_buf)
    top, bottom = jnp.sum(top, 0, keepdims=True), jnp.sum(bottom, 0, keepdims=True)
    lane_row = iota((1, LANES), 1)
    with jax.named_scope("w_t2"):
        pl.semaphore_wait(token.at[1], 4)
    signal(token.at[2], [on_ring(4), on_ring(-4), partner])

    with jax.named_scope("w_halo_a"):
        take(halo_recv.at[0], o_buf.at[pl.ds(0, 2)])
    cross = o_buf[2, :HALF] * (2.0 * NEAR * o_buf[1, :HALF] + 2.0 * FAR * o_buf[0, :HALF])
    cross += 2.0 * FAR * o_buf[1, :HALF] * o_buf[3, :HALF]
    cross += o_buf[9, HALF:] * (2.0 * NEAR * o_buf[10, HALF:] + 2.0 * FAR * o_buf[11, HALF:])
    cross += 2.0 * FAR * o_buf[10, HALF:] * o_buf[8, HALF:]
    top += jnp.sum(cross, 0, keepdims=True)
    e_y[y] = jnp.where(
        lane_row < 64, top + pltpu.roll(top, 64, 1), bottom + pltpu.roll(bottom, 64, 1)
    )
    for d in range(1, columns):
        send(e_y.at[y], e_y.at[y], (ey_sem.at[0], ey_sem.at[1]), on_column(d))

    with jax.named_scope("w_halo_b"):
        take(halo_recv.at[1], o_buf.at[pl.ds(0, 2)])
        take(halo_recv.at[2], g_in)
    h_buf[1] += NEAR * o_buf[1] + FAR * o_buf[0]
    h_buf[2] += FAR * o_buf[1]
    h_buf[8] += NEAR * o_buf[10] + FAR * o_buf[11]
    h_buf[7] += FAR * o_buf[10]
    r_buf[0] += K0 * o_buf[1]
    r_buf[7] += K0 * o_buf[10]
    for ghost, at, inner, outer, side in ((1, 0, 2, 0, 0), (10, 9, 9, 11, 1)):
        centre = o_buf[ghost]
        first = (o_buf[inner] + o_buf[outer]) + beside(centre)
        second = o_buf[2 * inner - ghost] + beside_two(centre)
        h_buf[at] = 3.75 * centre + g_in[side] + NEAR * first + FAR * second
    for q in range(PLANES // 2):
        both = None
        for p in (2 * q, 2 * q + 1):
            value = h_buf[p + 1]
            rest = value * THIRD + K0 * ((h_buf[p] + h_buf[p + 2]) + beside(value))
            both = rest if both is None else both + rest
        pair_buf[q] = both
        pair_buf[q + 4] = r_buf[2 * q] + r_buf[2 * q + 1]
    halved = pair_buf[:, pl.ds(0, 32, 2), :] + pair_buf[:, pl.ds(1, 32, 2), :]
    f1 = times(halved[:4].reshape(LANES, LANES), mats[0]) + times(
        halved[4:].reshape(LANES, LANES), mats[1]
    )
    f1 = f1.reshape(4, 32, LANES)
    f1_buf[2:6] = f1

    rest = []
    for p in range(4):
        total = beside(f1[p], 64)
        for q in (p - 1, p + 1):
            if 0 <= q < 4:
                total += f1[q]
        rest.append(f1[p] * THIRD + K1 * total)
    two_buf[0] = K1 * f1[0]
    two_buf[1] = rest[0] + rest[1]
    two_buf[2] = rest[2] + rest[3]
    two_buf[3] = K1 * f1[3]
    halved = two_buf[:, pl.ds(0, 16, 2), :] + two_buf[:, pl.ds(1, 16, 2), :]
    share = times(halved.reshape(64, LANES), mats[2]).reshape(4, 16, LANES)
    low = iota((16, LANES), 1) < 64
    f2_out[0] = jnp.where(low, share[0], share[1])
    f2_out[1] = jnp.where(low, share[2], share[3])
    a, b, c, d = share[0], share[1], share[2], share[3]
    three_buf[0] = a * (K2 + THIRD) + K2 * (b + beside(a, 32))
    three_buf[1] = (b + c) * (THIRD + K2) + K2 * ((a + d) + (beside(b, 32) + beside(c, 32)))
    three_buf[2] = d * (K2 + THIRD) + K2 * (c + beside(d, 32))
    halved = three_buf[:, pl.ds(0, 8, 2), :] + three_buf[:, pl.ds(1, 8, 2), :]
    parts = times(halved.reshape(24, LANES), mats[3]).reshape(3, 8, LANES)
    lane = iota((8, LANES), 1)
    f3_in[REACH] = jnp.where(
        lane < 32, parts[0],
        jnp.where(lane < 64, parts[1], jnp.where(lane < 96, parts[2], 0.0)),
    )
    sems = (f3_sem.at[0], f3_sem.at[1])
    for step in range(REACH, 0, -1):
        send(f3_in.at[REACH], f3_in.at[REACH - step], sems, slab(step))
        send(f3_in.at[REACH], f3_in.at[REACH + step], sems, slab(-step))

    with jax.named_scope("w_ey"):
        take(ey_sem.at[1], e_y.at[pl.ds(0, columns - 1)])
    e_z[z] = jnp.sum(e_y[...], axis=0)
    with jax.named_scope("w_t3"):
        pl.semaphore_wait(token.at[2], 3)
    for d in range(1, RING):
        send(e_z.at[z], e_z.at[z], (ez_sem.at[0], ez_sem.at[1]), on_ring(d))
    sems = (f2_sem.at[0], f2_sem.at[1])
    send(f2_out, f2_in.at[pl.ds(0, 2)], sems, right)
    send(f2_out, f2_in.at[pl.ds(2, 2)], sems, left)
    send(f2_out.at[1], f2_in.at[4], sems, slab(2))
    send(f2_out.at[0], f2_in.at[5], sems, slab(-2))
    sems = (f1_sem.at[0], f1_sem.at[1])
    send(f1_buf.at[pl.ds(4, 2)], f1_buf.at[pl.ds(0, 2)], sems, right)
    send(f1_buf.at[pl.ds(2, 2)], f1_buf.at[pl.ds(6, 2)], sems, left)

    with jax.named_scope("w_f"):
        take(f3_sem.at[1], f3_in.at[pl.ds(0, 2 * REACH)])
        take(f2_sem.at[1], f2_in)
        take(f1_sem.at[1], f1_buf.at[pl.ds(0, 4)])

    source = {}
    for p in range(1 - REACH, REACH):
        at = p + REACH
        total = jnp.where(lane < 32, f3_in[at + 1], jnp.where(lane < 64, f3_in[at], f3_in[at - 1]))
        total = total + pltpu.roll(total, 32, 1)
        source[p] = total + pltpu.roll(total, 64, 1)
    iterate = {p: C3 * source[p] for p in source}
    for reach in (2, 1):
        iterate = {
            p: iterate[p] * THIRD + C3 * source[p]
            + K3 * ((iterate[p - 1] + iterate[p + 1]) + beside(iterate[p], 16))
            for p in range(-reach, reach + 1)
        }
    spread = times(jnp.concatenate([iterate[p] for p in range(-1, 2)], 0), mats[4]).reshape(3, 8, LANES)
    up2_buf[:, pl.ds(0, 8, 2), :] = spread
    up2_buf[:, pl.ds(1, 8, 2), :] = spread

    def lower(tile):
        return jnp.where(low, tile, pltpu.roll(tile, 64, 1))

    def upper(tile):
        return jnp.where(low, pltpu.roll(tile, 64, 1), tile)

    f2 = {
        -2: upper(f2_in[0]) + upper(f2_in[4]),
        -1: share[0] + lower(f2_in[1]),
        0: share[1] + upper(f2_in[1]),
        1: share[2] + lower(f2_in[2]),
        2: share[3] + upper(f2_in[2]),
        3: lower(f2_in[3]) + lower(f2_in[5]),
    }
    fixed = {p: C2 * f2[p] + up2_buf[(p >> 1) + 1] for p in range(-2, 4)}
    value = [
        fixed[p] * THIRD + C2 * f2[p] + K2 * ((fixed[p - 1] + fixed[p + 1]) + beside(fixed[p], 32))
        for p in range(-1, 3)
    ]
    spread = times(jnp.concatenate(value, 0), mats[5]).reshape(4, 16, LANES)
    up1_buf[:, pl.ds(0, 16, 2), :] = spread
    up1_buf[:, pl.ds(1, 16, 2), :] = spread
    fixed = {p: C1 * f1_buf[p + 2] + up1_buf[(p >> 1) + 1] for p in range(-2, 6)}
    error = jnp.concatenate(
        [
            fixed[p] * THIRD + C1 * f1_buf[p + 2]
            + K1 * ((fixed[p - 1] + fixed[p + 1]) + beside(fixed[p], 64))
            for p in range(-1, 5)
        ],
        0,
    )

    for matrix, up_buf, field, shift, last in ((6, uph_buf, h_buf, 1, a_buf), (7, upo_buf, o_buf, 2, b_buf)):
        spread = times(error, mats[matrix]).reshape(6, 32, LANES)
        up_buf[:, pl.ds(0, 32, 2), :] = spread
        up_buf[:, pl.ds(1, 32, 2), :] = spread
        fixed = {}
        for p in range(-1, PLANES + 1):
            fixed[p] = C0 * field[p + shift] + up_buf[(p >> 1) + 1]
            if p >= 1:
                value = fixed[p - 1]
                around = (fixed[p - 2] + fixed[p]) + beside(value)
                last[p - 1] = value * THIRD + C0 * field[p - 1 + shift] + K0 * around
    with jax.named_scope("w_ez"):
        take(ez_sem.at[1], e_z.at[pl.ds(0, RING - 1)])
    sums = jnp.sum(e_z[...], axis=0)
    numer = jnp.sum(jnp.where(lane_row < 64, sums, 0.0), axis=1, keepdims=True)
    denom = jnp.sum(jnp.where(lane_row < 64, 0.0, sums), axis=1, keepdims=True)
    energy = numer / denom

    def finish(p):
        value = a_buf[p] - energy * b_buf[p]
        out_ref[0, p] = value
        return value.astype(jnp.bfloat16)

    for step, other in ((2, False), (2, True), (1, False), (-1, False), (1, True), (-1, True), (0, True)):
        to = state_at(step, other)
        rounded[to] = finish(to)
        send(rounded.at[to], mixed.at[s], (x_sem.at[0], x_sem.at[1]), (g, to))
    mixed[s] = finish(s)
    with jax.named_scope("w_mix"):
        take(x_sem.at[1], mixed.at[pl.ds(0, STATES - 1)])

    pairs = [(i, j) for i in range(STATES) for j in range(i, STATES)]
    held = {pair: None for pair in pairs}
    for block in range(ROWS // 16):
        values = [mixed[i, 16 * block : 16 * block + 16].astype(F32) for i in range(STATES)]
        for i, j in pairs:
            product = values[i] * values[j]
            product = product[:8] + product[8:]
            held[i, j] = product if held[i, j] is None else held[i, j] + product
    for i, j in pairs:
        row = jnp.sum(held[i, j], 0, keepdims=True)
        rows_buf[8 * i + j : 8 * i + j + 1] = row
        if i != j:
            rows_buf[8 * j + i : 8 * j + i + 1] = row
    flat = lax.dot_general(
        jnp.ones((8, LANES), F32), rows_buf[...], (((1,), (1,)), ((), ())),
        precision=HIGH, preferred_element_type=F32,
    )
    g_z[z] = flat[:1]
    for d in range(1, RING):
        send(g_z.at[z], g_z.at[z], (gz_sem.at[0], gz_sem.at[1]), on_ring(d))
    with jax.named_scope("w_gz"):
        take(gz_sem.at[1], g_z.at[pl.ds(0, RING - 1)])
    mine = y * STATES + s
    g_xy[mine] = jnp.sum(g_z[...], axis=0)
    for d in range(1, STATES * columns):
        send(g_xy.at[mine], g_xy.at[mine], (gx_sem.at[0], gx_sem.at[1]), on_face(d))
    with jax.named_scope("w_sends"):
        take(halo_send, o_buf.at[pl.ds(0, 6)])
        take(f1_sem.at[0], f1_buf.at[pl.ds(0, 4)])
        take(f2_sem.at[0], f2_in)
        take(f3_sem.at[0], f3_in.at[pl.ds(0, 2 * REACH)])
        take(ey_sem.at[0], e_y.at[pl.ds(0, columns - 1)])
        take(ez_sem.at[0], e_z.at[pl.ds(0, RING - 1)])
        take(x_sem.at[0], mixed.at[pl.ds(0, STATES - 1)])
        take(gz_sem.at[0], g_z.at[pl.ds(0, RING - 1)])
    with jax.named_scope("w_gxy"):
        take(gx_sem.at[1], g_xy.at[pl.ds(0, STATES * columns - 1)])
    total = jnp.sum(g_xy[...], axis=0)
    picked = jnp.zeros((1, STATES), F32)
    for t in range(STATES):
        picked += jnp.where(s == t, total[:, STATES * t : STATES * t + STATES], 0.0)
    gram_ref[...] = picked / F32(PLANES * ROWS * LANES * slabs)
    with jax.named_scope("w_last"):
        take(gx_sem.at[0], g_xy.at[pl.ds(0, STATES * columns - 1)])


def solution(mesh):
    slabs = mesh.shape["grid"]
    columns = slabs // RING
    faces = STATES * columns
    dma = pltpu.SemaphoreType.DMA

    def vmem(*shape, dtype=F32):
        return pltpu.VMEM(shape, dtype)

    def on_device(orbitals, potential):
        return pl.pallas_call(
            functools.partial(kernel, slabs),
            out_shape=(
                jax.ShapeDtypeStruct((1, PLANES, ROWS, LANES), F32),
                jax.ShapeDtypeStruct((1, STATES), F32),
            ),
            in_specs=[pl.BlockSpec(memory_space=pltpu.HBM)] * 2,
            out_specs=(
                pl.BlockSpec(memory_space=pltpu.VMEM),
                pl.BlockSpec(memory_space=pltpu.VMEM),
            ),
            scratch_shapes=[
                vmem(PLANES + 4, ROWS, LANES),
                vmem(PLANES, ROWS, LANES),
                vmem(PLANES + 2, ROWS, LANES),
                vmem(PLANES, ROWS, LANES),
                vmem(2, ROWS, LANES),
                vmem(2, ROWS, LANES),
                vmem(PLANES, ROWS, LANES),
                vmem(8, LANES, LANES),
                vmem(8, 32, LANES),
                vmem(4, 32, LANES),
                vmem(2, 16, LANES),
                vmem(6, 16, LANES),
                vmem(3, 16, LANES),
                vmem(2 * REACH + 1, 8, LANES),
                vmem(3, 16, LANES),
                vmem(4, 32, LANES),
                vmem(6, ROWS, LANES),
                vmem(6, ROWS, LANES),
                vmem(PLANES, ROWS, LANES),
                vmem(PLANES, ROWS, LANES),
                vmem(columns, 1, LANES),
                vmem(RING, 1, LANES),
                vmem(PLANES, ROWS, LANES, dtype=jnp.bfloat16),
                vmem(STATES, ROWS, LANES, dtype=jnp.bfloat16),
                vmem(LANES, LANES),
                vmem(RING, 1, LANES),
                vmem(faces, 1, LANES),
                dma((2,)), dma(()), dma((3,)), dma((2,)), dma((2,)), dma((2,)),
                dma((2,)), dma((2,)), dma((2,)), dma((2,)), dma((2,)),
                pltpu.SemaphoreType.REGULAR((3,)),
            ],
            compiler_params=pltpu.CompilerParams(
                collective_id=0, has_side_effects=True, vmem_limit_bytes=32 * 1024 * 1024
            ),
        )(*[pltpu.with_memory_space_constraint(v, pltpu.HBM) for v in (orbitals, potential)])

    return jax.shard_map(
        on_device,
        mesh=mesh,
        in_specs=(P("state", "grid", None, None), P("grid", None, None)),
        out_specs=(P("state", "grid", None, None), P("state", None)),
        check_vma=False,
    )
```

```python
import functools

import jax
import jax.numpy as jnp
from jax import lax
from jax.experimental import pallas as pl
from jax.experimental.pallas import tpu as pltpu
from jax.sharding import PartitionSpec as P

MESH = pl.DeviceIdType.MESH
HIGH = lax.Precision.HIGHEST
F32 = jnp.float32

SHIFT_TERM = 0.25
DAMPING = 2.0 / 3.0
LANES = 128
ROWS = 64
HALF = ROWS // 2
PLANES = 8
STATES = 8
CHIPS = 4
RING = 16
REACH = 4
THIRD = 1.0 / 3.0
NEAR = -2.0 / 3.0
FAR = 1.0 / 24.0


def scales(level):
    inverse = 0.25**level
    diagonal = SHIFT_TERM + 3.0 * inverse
    scaled = DAMPING / diagonal
    return scaled, 0.5 * inverse * scaled


C0, K0 = scales(0)
C1, K1 = scales(1)
C2, K2 = scales(2)
C3, K3 = scales(3)


def iota(shape, dim):
    return lax.broadcasted_iota(jnp.int32, shape, dim)


def beside(plane, segment=LANES):
    rows = plane.shape[0]
    total = pltpu.roll(plane, 1, 0) + pltpu.roll(plane, rows - 1, 0)
    low, high = pltpu.roll(plane, 1, 1), pltpu.roll(plane, LANES - 1, 1)
    if segment != LANES:
        cell = iota(plane.shape, 1) & (segment - 1)
        low = jnp.where(cell == 0, pltpu.roll(plane, LANES - segment + 1, 1), low)
        high = jnp.where(cell == segment - 1, pltpu.roll(plane, segment - 1, 1), high)
    return total + (low + high)


def beside_two(plane):
    rows = plane.shape[0]
    total = pltpu.roll(plane, 2, 0) + pltpu.roll(plane, rows - 2, 0)
    return total + (pltpu.roll(plane, 2, 1) + pltpu.roll(plane, LANES - 2, 1))


def matrices():
    k, j = iota((LANES, LANES), 0), iota((LANES, LANES), 1)
    down_h = (j < 64) & ((k >> 1) == j)
    down_o = (j >= 64) & ((k >> 1) == j - 64)
    down_two = ((k >> 6) == ((j >> 5) & 1)) & (((k & 63) >> 1) == (j & 31))
    down_three = (k < 64) & ((k >> 5) == ((j >> 4) & 1)) & (((k & 31) >> 1) == (j & 15))
    up_two = (k < 32) & ((k >> 4) == ((j >> 5) & 1)) & ((k & 15) == ((j & 31) >> 1))
    up_one = (k < 64) & ((k >> 5) == (j >> 6)) & ((k & 31) == ((j & 63) >> 1))
    up_h = k == (j >> 1)
    up_o = k - 64 == (j >> 1)
    eighth, one = jnp.full((LANES, LANES), 0.125, F32), jnp.ones((LANES, LANES), F32)
    zero = jnp.zeros((LANES, LANES), F32)
    return [
        jnp.where(mask, eighth, zero) for mask in (down_h, down_o, down_two, down_three)
    ] + [jnp.where(mask, one, zero) for mask in (up_two, up_one, up_h, up_o)]


def times(left, right):
    return jnp.dot(left, right, precision=HIGH, preferred_element_type=F32)


def kernel(
    slabs,
    o_hbm, p_hbm, out_ref, gram_ref,
    o_buf, p_buf, h_buf, r_buf, g_out, g_in, pair_buf, mats,
    f1_buf, two_buf, f2_out, f2_in, three_buf, f3_in,
    up2_buf, up1_buf, uph_buf, upo_buf, a_buf, b_buf,
    e_y, e_z, rounded, mixed, rows_buf, g_z, g_xy,
    load_sem, halo_send, halo_recv, f1_sem, f2_sem, f3_sem, ey_sem, ez_sem, x_sem, gz_sem, gx_sem,
    token,
):
    g, s = lax.axis_index("grid"), lax.axis_index("state")
    y, z = g >> 4, g & (RING - 1)
    x, core = s >> 1, s & 1
    columns = slabs // RING

    def slab(step):
        return ((g + step) & (slabs - 1), s)

    def on_ring(step):
        return (y * RING + ((z + step) & (RING - 1)), s)

    def on_column(step):
        return (((y + step) & (columns - 1)) * RING + z, s)

    def state_at(step, other):
        return 2 * ((x + step) & (CHIPS - 1)) + (1 - core if other else core)

    def on_face(step):
        up, side = step // STATES, step % STATES
        return (((y + up) & (columns - 1)) * RING + z, (s + side) & (STATES - 1))

    def send(src, dst, sems, peer):
        copy = pltpu.make_async_remote_copy(
            src_ref=src, dst_ref=dst, send_sem=sems[0], recv_sem=sems[1],
            device_id=peer, device_id_type=MESH,
        )
        copy.start()

    def take(sem, view):
        pltpu.make_async_copy(view, view, sem).wait()

    def signal(sem, peers):
        for peer in peers:
            pl.semaphore_signal(sem, inc=1, device_id=peer, device_id_type=MESH)

    others = [(step, other) for step in (2, 1, -1) for other in (False, True)] + [(0, True)]
    next_two = [slab(1), slab(-1), on_ring(2), on_ring(-2)]
    close = next_two + [on_column(2)] + [(g, state_at(*pair)) for pair in others]
    close += [on_ring(1), on_ring(-1), on_column(1), on_column(-1)]
    barrier = pltpu.get_barrier_semaphore()
    signal(barrier, close)
    loads = [
        pltpu.make_async_copy(o_hbm.at[0], o_buf.at[pl.ds(2, PLANES)], load_sem.at[0]),
        pltpu.make_async_copy(p_hbm, p_buf, load_sem.at[1]),
    ]
    for load in loads:
        load.start()
    with jax.named_scope("w_barrier"):
        pl.semaphore_wait(barrier, len(close))

    right, left = slab(1), slab(-1)

    def halo(part, mine, theirs):
        sems = (halo_send, halo_recv.at[part])
        send(o_hbm.at[0, pl.ds(6, 2), pl.ds(mine, HALF)], o_buf.at[pl.ds(0, 2), pl.ds(mine, HALF)], sems, right)
        send(o_hbm.at[0, pl.ds(0, 2), pl.ds(theirs, HALF)], o_buf.at[pl.ds(10, 2), pl.ds(theirs, HALF)], sems, left)

    signal(token.at[0], next_two)
    halo(0, 0, HALF)
    with jax.named_scope("w_load"):
        for load in loads:
            load.wait()
    g_out[0] = p_buf[0] * o_buf[2] + FAR * o_buf[4]
    g_out[1] = p_buf[7] * o_buf[9] + FAR * o_buf[7]

    top = jnp.zeros((ROWS, LANES), F32)
    bottom = jnp.zeros((ROWS, LANES), F32)
    for p in range(PLANES):
        centre = o_buf[p + 2]
        first, second = beside(centre), beside_two(centre)
        for q in (p - 1, p + 1):
            if 0 <= q < PLANES:
                first += o_buf[q + 2]
        for q in (p - 2, p + 2):
            if 0 <= q < PLANES:
                second += o_buf[q + 2]
        value = (3.75 + p_buf[p]) * centre + NEAR * first + FAR * second
        h_buf[p + 1] = value
        r_buf[p] = centre * THIRD + K0 * first
        top += centre * value
        bottom += centre * centre
    halo(1, HALF, 0)
    sems = (halo_send, halo_recv.at[2])
    send(g_out.at[1], g_in.at[0], sems, right)
    send(g_out.at[0], g_in.at[1], sems, left)
    for index, matrix in enumerate(matrices()):
        mats[index] = matrix
    rows_buf[...] = jnp.zeros_like(rows_buf)
    top, bottom = jnp.sum(top, 0, keepdims=True), jnp.sum(bottom, 0, keepdims=True)
    lane_row = iota((1, LANES), 1)

    with jax.named_scope("w_t1"):
        pl.semaphore_wait(token.at[0], len(next_two))
    signal(token.at[1], [on_ring(4), on_ring(-4)])
    signal(token.at[2], [slab(2), slab(-2)])
    with jax.named_scope("w_halo_a"):
        take(halo_recv.at[0], o_buf.at[pl.ds(0, 2)])
    cross = o_buf[2, :HALF] * (2.0 * NEAR * o_buf[1, :HALF] + 2.0 * FAR * o_buf[0, :HALF])
    cross += 2.0 * FAR * o_buf[1, :HALF] * o_buf[3, :HALF]
    cross += o_buf[9, HALF:] * (2.0 * NEAR * o_buf[10, HALF:] + 2.0 * FAR * o_buf[11, HALF:])
    cross += 2.0 * FAR * o_buf[10, HALF:] * o_buf[8, HALF:]
    top += jnp.sum(cross, 0, keepdims=True)
    e_y[y] = jnp.where(
        lane_row < 64, top + pltpu.roll(top, 64, 1), bottom + pltpu.roll(bottom, 64, 1)
    )
    for d in range(1, columns):
        send(e_y.at[y], e_y.at[y], (ey_sem.at[0], ey_sem.at[1]), on_column(d))

    with jax.named_scope("w_halo_b"):
        take(halo_recv.at[1], o_buf.at[pl.ds(0, 2)])
        take(halo_recv.at[2], g_in)
    h_buf[1] += NEAR * o_buf[1] + FAR * o_buf[0]
    h_buf[2] += FAR * o_buf[1]
    h_buf[8] += NEAR * o_buf[10] + FAR * o_buf[11]
    h_buf[7] += FAR * o_buf[10]
    r_buf[0] += K0 * o_buf[1]
    r_buf[7] += K0 * o_buf[10]
    for ghost, at, inner, outer, side in ((1, 0, 2, 0, 0), (10, 9, 9, 11, 1)):
        centre = o_buf[ghost]
        first = (o_buf[inner] + o_buf[outer]) + beside(centre)
        second = o_buf[2 * inner - ghost] + beside_two(centre)
        h_buf[at] = 3.75 * centre + g_in[side] + NEAR * first + FAR * second
    for q in range(PLANES // 2):
        both = None
        for p in (2 * q, 2 * q + 1):
            value = h_buf[p + 1]
            rest = value * THIRD + K0 * ((h_buf[p] + h_buf[p + 2]) + beside(value))
            both = rest if both is None else both + rest
        pair_buf[q] = both
        pair_buf[q + 4] = r_buf[2 * q] + r_buf[2 * q + 1]
    halved = pair_buf[:, pl.ds(0, 32, 2), :] + pair_buf[:, pl.ds(1, 32, 2), :]
    f1 = times(halved[:4].reshape(LANES, LANES), mats[0]) + times(
        halved[4:].reshape(LANES, LANES), mats[1]
    )
    f1 = f1.reshape(4, 32, LANES)
    f1_buf[2:6] = f1
    sems = (f1_sem.at[0], f1_sem.at[1])
    send(f1_buf.at[pl.ds(4, 2)], f1_buf.at[pl.ds(0, 2)], sems, right)
    send(f1_buf.at[pl.ds(2, 2)], f1_buf.at[pl.ds(6, 2)], sems, left)

    rest = []
    for p in range(4):
        total = beside(f1[p], 64)
        for q in (p - 1, p + 1):
            if 0 <= q < 4:
                total += f1[q]
        rest.append(f1[p] * THIRD + K1 * total)
    two_buf[0] = K1 * f1[0]
    two_buf[1] = rest[0] + rest[1]
    two_buf[2] = rest[2] + rest[3]
    two_buf[3] = K1 * f1[3]
    halved = two_buf[:, pl.ds(0, 16, 2), :] + two_buf[:, pl.ds(1, 16, 2), :]
    share = times(halved.reshape(64, LANES), mats[2]).reshape(4, 16, LANES)
    low = iota((8, LANES), 1) < 64
    for k in range(4):
        f2_out[k] = jnp.where(low, share[k][:8], share[k][8:])
    a, b, c, d = share[0], share[1], share[2], share[3]
    three_buf[0] = a * (K2 + THIRD) + K2 * (b + beside(a, 32))
    three_buf[1] = (b + c) * (THIRD + K2) + K2 * ((a + d) + (beside(b, 32) + beside(c, 32)))
    three_buf[2] = d * (K2 + THIRD) + K2 * (c + beside(d, 32))
    halved = three_buf[:, pl.ds(0, 8, 2), :] + three_buf[:, pl.ds(1, 8, 2), :]
    parts = times(halved.reshape(24, LANES), mats[3]).reshape(3, 8, LANES)
    lane = iota((8, LANES), 1)
    f3_in[REACH] = jnp.where(
        lane < 32, parts[0],
        jnp.where(lane < 64, parts[1], jnp.where(lane < 96, parts[2], 0.0)),
    )
    with jax.named_scope("w_t2"):
        pl.semaphore_wait(token.at[2], 2)
    sems = (f3_sem.at[0], f3_sem.at[1])
    for step in range(REACH, 0, -1):
        send(f3_in.at[REACH], f3_in.at[REACH - step], sems, slab(step))
        send(f3_in.at[REACH], f3_in.at[REACH + step], sems, slab(-step))
    sems = (f2_sem.at[0], f2_sem.at[1])
    send(f2_out.at[pl.ds(1, 3)], f2_in.at[pl.ds(0, 3)], sems, right)
    send(f2_out.at[pl.ds(0, 3)], f2_in.at[pl.ds(3, 3)], sems, left)
    send(f2_out.at[3], f2_in.at[6], sems, slab(2))
    send(f2_out.at[0], f2_in.at[7], sems, slab(-2))

    with jax.named_scope("w_ey"):
        take(ey_sem.at[1], e_y.at[pl.ds(0, columns - 1)])
    e_z[z] = jnp.sum(e_y[...], axis=0)
    with jax.named_scope("w_t3"):
        pl.semaphore_wait(token.at[1], 2)
    for d in range(1, RING):
        send(e_z.at[z], e_z.at[z], (ez_sem.at[0], ez_sem.at[1]), on_ring(d))

    with jax.named_scope("w_f"):
        take(f3_sem.at[1], f3_in.at[pl.ds(0, 2 * REACH)])
        take(f2_sem.at[1], f2_in)
        take(f1_sem.at[1], f1_buf.at[pl.ds(0, 4)])

    source = {}
    for p in range(1 - REACH, REACH):
        at = p + REACH
        total = jnp.where(lane < 32, f3_in[at + 1], jnp.where(lane < 64, f3_in[at], f3_in[at - 1]))
        total = total + pltpu.roll(total, 32, 1)
        source[p] = total + pltpu.roll(total, 64, 1)
    iterate = {p: C3 * source[p] for p in source}
    for reach in (2, 1):
        iterate = {
            p: iterate[p] * THIRD + C3 * source[p]
            + K3 * ((iterate[p - 1] + iterate[p + 1]) + beside(iterate[p], 16))
            for p in range(-reach, reach + 1)
        }
    spread = times(jnp.concatenate([iterate[p] for p in range(-1, 2)], 0), mats[4]).reshape(3, 8, LANES)
    up2_buf[:, pl.ds(0, 8, 2), :] = spread
    up2_buf[:, pl.ds(1, 8, 2), :] = spread

    def unfold(tile):
        turned = pltpu.roll(tile, 64, 1)
        return jnp.concatenate([jnp.where(low, tile, turned), jnp.where(low, turned, tile)], 0)

    f2 = {
        -2: unfold(f2_in[0] + f2_in[6]),
        -1: share[0] + unfold(f2_in[1]),
        0: share[1] + unfold(f2_in[2]),
        1: share[2] + unfold(f2_in[3]),
        2: share[3] + unfold(f2_in[4]),
        3: unfold(f2_in[5] + f2_in[7]),
    }
    fixed = {p: C2 * f2[p] + up2_buf[(p >> 1) + 1] for p in range(-2, 4)}
    value = [
        fixed[p] * THIRD + C2 * f2[p] + K2 * ((fixed[p - 1] + fixed[p + 1]) + beside(fixed[p], 32))
        for p in range(-1, 3)
    ]
    spread = times(jnp.concatenate(value, 0), mats[5]).reshape(4, 16, LANES)
    up1_buf[:, pl.ds(0, 16, 2), :] = spread
    up1_buf[:, pl.ds(1, 16, 2), :] = spread
    fixed = {p: C1 * f1_buf[p + 2] + up1_buf[(p >> 1) + 1] for p in range(-2, 6)}
    error = jnp.concatenate(
        [
            fixed[p] * THIRD + C1 * f1_buf[p + 2]
            + K1 * ((fixed[p - 1] + fixed[p + 1]) + beside(fixed[p], 64))
            for p in range(-1, 5)
        ],
        0,
    )

    for matrix, up_buf, field, shift, last in ((6, uph_buf, h_buf, 1, a_buf), (7, upo_buf, o_buf, 2, b_buf)):
        spread = times(error, mats[matrix]).reshape(6, 32, LANES)
        up_buf[:, pl.ds(0, 32, 2), :] = spread
        up_buf[:, pl.ds(1, 32, 2), :] = spread
        fixed = {}
        for p in range(-1, PLANES + 1):
            fixed[p] = C0 * field[p + shift] + up_buf[(p >> 1) + 1]
            if p >= 1:
                value = fixed[p - 1]
                around = (fixed[p - 2] + fixed[p]) + beside(value)
                last[p - 1] = value * THIRD + C0 * field[p - 1 + shift] + K0 * around
    with jax.named_scope("w_ez"):
        take(ez_sem.at[1], e_z.at[pl.ds(0, RING - 1)])
    sums = jnp.sum(e_z[...], axis=0)
    numer = jnp.sum(jnp.where(lane_row < 64, sums, 0.0), axis=1, keepdims=True)
    denom = jnp.sum(jnp.where(lane_row < 64, 0.0, sums), axis=1, keepdims=True)
    energy = numer / denom

    def finish(p):
        value = a_buf[p] - energy * b_buf[p]
        out_ref[0, p] = value
        return value.astype(jnp.bfloat16)

    for step, other in others:
        to = state_at(step, other)
        rounded[to] = finish(to)
        send(rounded.at[to], mixed.at[s], (x_sem.at[0], x_sem.at[1]), (g, to))
    mixed[s] = finish(s)
    with jax.named_scope("w_mix"):
        take(x_sem.at[1], mixed.at[pl.ds(0, STATES - 1)])

    pairs = [(i, j) for i in range(STATES) for j in range(i, STATES)]
    held = {pair: None for pair in pairs}
    for block in range(ROWS // 16):
        values = [mixed[i, 16 * block : 16 * block + 16].astype(F32) for i in range(STATES)]
        for i, j in pairs:
            product = values[i] * values[j]
            product = product[:8] + product[8:]
            held[i, j] = product if held[i, j] is None else held[i, j] + product
    for i, j in pairs:
        row = jnp.sum(held[i, j], 0, keepdims=True)
        rows_buf[8 * i + j : 8 * i + j + 1] = row
        if i != j:
            rows_buf[8 * j + i : 8 * j + i + 1] = row
    flat = lax.dot_general(
        jnp.ones((8, LANES), F32), rows_buf[...], (((1,), (1,)), ((), ())),
        precision=HIGH, preferred_element_type=F32,
    )
    g_z[z] = flat[:1]
    for d in range(1, RING):
        send(g_z.at[z], g_z.at[z], (gz_sem.at[0], gz_sem.at[1]), on_ring(d))
    with jax.named_scope("w_gz"):
        take(gz_sem.at[1], g_z.at[pl.ds(0, RING - 1)])
    mine = y * STATES + s
    g_xy[mine] = jnp.sum(g_z[...], axis=0)
    for d in range(1, STATES * columns):
        send(g_xy.at[mine], g_xy.at[mine], (gx_sem.at[0], gx_sem.at[1]), on_face(d))
    with jax.named_scope("w_sends"):
        take(halo_send, o_buf.at[pl.ds(0, 6)])
        take(f1_sem.at[0], f1_buf.at[pl.ds(0, 4)])
        take(f2_sem.at[0], f2_in)
        take(f3_sem.at[0], f3_in.at[pl.ds(0, 2 * REACH)])
        take(ey_sem.at[0], e_y.at[pl.ds(0, columns - 1)])
        take(ez_sem.at[0], e_z.at[pl.ds(0, RING - 1)])
        take(x_sem.at[0], mixed.at[pl.ds(0, STATES - 1)])
        take(gz_sem.at[0], g_z.at[pl.ds(0, RING - 1)])
    with jax.named_scope("w_gxy"):
        take(gx_sem.at[1], g_xy.at[pl.ds(0, STATES * columns - 1)])
    total = jnp.sum(g_xy[...], axis=0)
    picked = jnp.zeros((1, STATES), F32)
    for t in range(STATES):
        picked += jnp.where(s == t, total[:, STATES * t : STATES * t + STATES], 0.0)
    gram_ref[...] = picked / F32(PLANES * ROWS * LANES * slabs)
    with jax.named_scope("w_last"):
        take(gx_sem.at[0], g_xy.at[pl.ds(0, STATES * columns - 1)])


def solution(mesh):
    slabs = mesh.shape["grid"]
    columns = slabs // RING
    faces = STATES * columns
    dma = pltpu.SemaphoreType.DMA

    def vmem(*shape, dtype=F32):
        return pltpu.VMEM(shape, dtype)

    def write_out(values, gram, values_hbm, gram_hbm, sem):
        copies = [
            pltpu.make_async_copy(values, values_hbm, sem.at[0]),
            pltpu.make_async_copy(gram, gram_hbm, sem.at[1]),
        ]
        for copy in copies:
            copy.start()
        for copy in copies:
            copy.wait()

    def on_device(orbitals, potential):
        shapes = (
            jax.ShapeDtypeStruct((1, PLANES, ROWS, LANES), F32),
            jax.ShapeDtypeStruct((1, STATES), F32),
        )
        results = pl.pallas_call(
            functools.partial(kernel, slabs),
            out_shape=(
                jax.ShapeDtypeStruct((1, PLANES, ROWS, LANES), F32),
                jax.ShapeDtypeStruct((1, STATES), F32),
            ),
            in_specs=[pl.BlockSpec(memory_space=pltpu.HBM)] * 2,
            out_specs=(
                pl.BlockSpec(memory_space=pltpu.VMEM),
                pl.BlockSpec(memory_space=pltpu.VMEM),
            ),
            scratch_shapes=[
                vmem(PLANES + 4, ROWS, LANES),
                vmem(PLANES, ROWS, LANES),
                vmem(PLANES + 2, ROWS, LANES),
                vmem(PLANES, ROWS, LANES),
                vmem(2, ROWS, LANES),
                vmem(2, ROWS, LANES),
                vmem(PLANES, ROWS, LANES),
                vmem(8, LANES, LANES),
                vmem(8, 32, LANES),
                vmem(4, 32, LANES),
                vmem(4, 8, LANES),
                vmem(8, 8, LANES),
                vmem(3, 16, LANES),
                vmem(2 * REACH + 1, 8, LANES),
                vmem(3, 16, LANES),
                vmem(4, 32, LANES),
                vmem(6, ROWS, LANES),
                vmem(6, ROWS, LANES),
                vmem(PLANES, ROWS, LANES),
                vmem(PLANES, ROWS, LANES),
                vmem(columns, 1, LANES),
                vmem(RING, 1, LANES),
                vmem(PLANES, ROWS, LANES, dtype=jnp.bfloat16),
                vmem(STATES, ROWS, LANES, dtype=jnp.bfloat16),
                vmem(LANES, LANES),
                vmem(RING, 1, LANES),
                vmem(faces, 1, LANES),
                dma((2,)), dma(()), dma((3,)), dma((2,)), dma((2,)), dma((2,)),
                dma((2,)), dma((2,)), dma((2,)), dma((2,)), dma((2,)),
                pltpu.SemaphoreType.REGULAR((3,)),
            ],
            compiler_params=pltpu.CompilerParams(
                collective_id=0, has_side_effects=True, vmem_limit_bytes=32 * 1024 * 1024
            ),
        )(*[pltpu.with_memory_space_constraint(v, pltpu.HBM) for v in (orbitals, potential)])

        return pl.pallas_call(
            write_out,
            out_shape=shapes,
            in_specs=[pl.BlockSpec(memory_space=pltpu.VMEM)] * 2,
            out_specs=(pl.BlockSpec(memory_space=pltpu.HBM), pl.BlockSpec(memory_space=pltpu.HBM)),
            scratch_shapes=[dma((2,))],
            compiler_params=pltpu.CompilerParams(vmem_limit_bytes=1024 * 1024),
        )(*results)

    return jax.shard_map(
        on_device,
        mesh=mesh,
        in_specs=(P("state", "grid", None, None), P("grid", None, None)),
        out_specs=(P("state", "grid", None, None), P("state", None)),
        check_vma=False,
    )
```

```python
import functools

import jax
import jax.numpy as jnp
from jax import lax
from jax.experimental import pallas as pl
from jax.experimental.pallas import tpu as pltpu
from jax.sharding import PartitionSpec as P

MESH = pl.DeviceIdType.MESH
HIGH = lax.Precision.HIGHEST
F32 = jnp.float32

SHIFT_TERM = 0.25
DAMPING = 2.0 / 3.0
LANES = 128
ROWS = 64
HALF = ROWS // 2
PLANES = 8
STATES = 8
CHIPS = 4
RING = 16
REACH = 4
THIRD = 1.0 / 3.0
NEAR = -2.0 / 3.0
FAR = 1.0 / 24.0


def scales(level):
    inverse = 0.25**level
    diagonal = SHIFT_TERM + 3.0 * inverse
    scaled = DAMPING / diagonal
    return scaled, 0.5 * inverse * scaled


C0, K0 = scales(0)
C1, K1 = scales(1)
C2, K2 = scales(2)
C3, K3 = scales(3)


def iota(shape, dim):
    return lax.broadcasted_iota(jnp.int32, shape, dim)


def beside(plane, segment=LANES):
    rows = plane.shape[0]
    total = pltpu.roll(plane, 1, 0) + pltpu.roll(plane, rows - 1, 0)
    low, high = pltpu.roll(plane, 1, 1), pltpu.roll(plane, LANES - 1, 1)
    if segment != LANES:
        cell = iota(plane.shape, 1) & (segment - 1)
        low = jnp.where(cell == 0, pltpu.roll(plane, LANES - segment + 1, 1), low)
        high = jnp.where(cell == segment - 1, pltpu.roll(plane, segment - 1, 1), high)
    return total + (low + high)


def beside_two(plane):
    rows = plane.shape[0]
    total = pltpu.roll(plane, 2, 0) + pltpu.roll(plane, rows - 2, 0)
    return total + (pltpu.roll(plane, 2, 1) + pltpu.roll(plane, LANES - 2, 1))


def matrices():
    k, j = iota((LANES, LANES), 0), iota((LANES, LANES), 1)
    down_h = (j < 64) & ((k >> 1) == j)
    down_o = (j >= 64) & ((k >> 1) == j - 64)
    down_two = ((k >> 6) == ((j >> 5) & 1)) & (((k & 63) >> 1) == (j & 31))
    down_three = (k < 64) & ((k >> 5) == ((j >> 4) & 1)) & (((k & 31) >> 1) == (j & 15))
    up_two = (k < 32) & ((k >> 4) == ((j >> 5) & 1)) & ((k & 15) == ((j & 31) >> 1))
    up_one = (k < 64) & ((k >> 5) == (j >> 6)) & ((k & 31) == ((j & 63) >> 1))
    up_h = k == (j >> 1)
    up_o = k - 64 == (j >> 1)
    eighth, one = jnp.full((LANES, LANES), 0.125, F32), jnp.ones((LANES, LANES), F32)
    zero = jnp.zeros((LANES, LANES), F32)
    return [
        jnp.where(mask, eighth, zero) for mask in (down_h, down_o, down_two, down_three)
    ] + [jnp.where(mask, one, zero) for mask in (up_two, up_one, up_h, up_o)]


def times(left, right):
    return jnp.dot(left, right, precision=HIGH, preferred_element_type=F32)


def kernel(
    slabs,
    o_hbm, p_hbm, out_ref, gram_ref,
    o_buf, p_buf, h_buf, r_buf, g_out, g_in, pair_buf, mats,
    f1_buf, two_buf, f2_out, f2_in, three_buf, f3_in,
    up2_buf, up1_buf, uph_buf, upo_buf, a_buf, b_buf,
    e_y, e_z, rounded, mixed, rows_buf, g_z, g_xy, wide,
    load_sem, halo_send, halo_recv, f1_sem, f2_sem, f3_sem, ey_sem, ez_sem, x_sem, gz_sem, gx_sem,
    token,
):
    g, s = lax.axis_index("grid"), lax.axis_index("state")
    y, z = g >> 4, g & (RING - 1)
    x, core = s >> 1, s & 1
    columns = slabs // RING

    def slab(step):
        return ((g + step) & (slabs - 1), s)

    def on_ring(step):
        return (y * RING + ((z + step) & (RING - 1)), s)

    def on_column(step):
        return (((y + step) & (columns - 1)) * RING + z, s)

    def state_at(step, other):
        return 2 * ((x + step) & (CHIPS - 1)) + (1 - core if other else core)

    def on_face(step):
        up, side = step // STATES, step % STATES
        return (((y + up) & (columns - 1)) * RING + z, (s + side) & (STATES - 1))

    def send(src, dst, sems, peer):
        copy = pltpu.make_async_remote_copy(
            src_ref=src, dst_ref=dst, send_sem=sems[0], recv_sem=sems[1],
            device_id=peer, device_id_type=MESH,
        )
        copy.start()

    def take(sem, view):
        pltpu.make_async_copy(view, view, sem).wait()

    def signal(sem, peers):
        for peer in peers:
            pl.semaphore_signal(sem, inc=1, device_id=peer, device_id_type=MESH)

    others = [(step, other) for step in (2, 1, -1) for other in (False, True)] + [(0, True)]
    next_two = [slab(1), slab(-1), on_ring(2), on_ring(-2)]
    partner = (g, state_at(0, True))
    next_two += [on_column(1), on_column(-1), (g, state_at(1, False)), (g, state_at(-1, False))]
    close = next_two + [on_ring(1), on_ring(-1), partner]
    barrier = pltpu.get_barrier_semaphore()
    signal(barrier, close)
    loads = [
        pltpu.make_async_copy(o_hbm.at[0], o_buf.at[pl.ds(2, PLANES)], load_sem.at[0]),
        pltpu.make_async_copy(p_hbm, p_buf, load_sem.at[1]),
    ]
    for load in loads:
        load.start()
    with jax.named_scope("w_load"):
        for load in loads:
            load.wait()
    with jax.named_scope("w_barrier"):
        pl.semaphore_wait(barrier, len(close))

    right, left = slab(1), slab(-1)

    def halo(part, mine, theirs):
        sems = (halo_send, halo_recv.at[part])
        send(o_buf.at[pl.ds(8, 2), pl.ds(mine, HALF)], o_buf.at[pl.ds(0, 2), pl.ds(mine, HALF)], sems, right)
        send(o_buf.at[pl.ds(2, 2), pl.ds(theirs, HALF)], o_buf.at[pl.ds(10, 2), pl.ds(theirs, HALF)], sems, left)

    signal(token.at[0], next_two)
    halo(0, 0, HALF)
    g_out[0] = p_buf[0] * o_buf[2] + FAR * o_buf[4]
    g_out[1] = p_buf[7] * o_buf[9] + FAR * o_buf[7]

    top = jnp.zeros((ROWS, LANES), F32)
    bottom = jnp.zeros((ROWS, LANES), F32)
    for p in range(PLANES):
        centre = o_buf[p + 2]
        first, second = beside(centre), beside_two(centre)
        for q in (p - 1, p + 1):
            if 0 <= q < PLANES:
                first += o_buf[q + 2]
        for q in (p - 2, p + 2):
            if 0 <= q < PLANES:
                second += o_buf[q + 2]
        value = (3.75 + p_buf[p]) * centre + NEAR * first + FAR * second
        h_buf[p + 1] = value
        r_buf[p] = centre * THIRD + K0 * first
        top += centre * value
        bottom += centre * centre
    halo(1, HALF, 0)
    sems = (halo_send, halo_recv.at[2])
    send(g_out.at[1], g_in.at[0], sems, right)
    send(g_out.at[0], g_in.at[1], sems, left)
    made = matrices()
    for index in range(6):
        mats[index] = made[index]
    wide[:, :LANES] = made[6]
    wide[:, LANES:] = made[7]
    rows_buf[...] = jnp.zeros_like(rows_buf)
    top, bottom = jnp.sum(top, 0, keepdims=True), jnp.sum(bottom, 0, keepdims=True)
    lane_row = iota((1, LANES), 1)

    with jax.named_scope("w_t1"):
        pl.semaphore_wait(token.at[0], len(next_two))
    signal(token.at[1], [on_ring(4), on_ring(-4), partner])
    signal(token.at[2], [slab(2), slab(-2)])
    with jax.named_scope("w_halo_a"):
        take(halo_recv.at[0], o_buf.at[pl.ds(0, 2)])
    cross = o_buf[2, :HALF] * (2.0 * NEAR * o_buf[1, :HALF] + 2.0 * FAR * o_buf[0, :HALF])
    cross += 2.0 * FAR * o_buf[1, :HALF] * o_buf[3, :HALF]
    cross += o_buf[9, HALF:] * (2.0 * NEAR * o_buf[10, HALF:] + 2.0 * FAR * o_buf[11, HALF:])
    cross += 2.0 * FAR * o_buf[10, HALF:] * o_buf[8, HALF:]
    top += jnp.sum(cross, 0, keepdims=True)
    e_y[y] = jnp.where(
        lane_row < 64, top + pltpu.roll(top, 64, 1), bottom + pltpu.roll(bottom, 64, 1)
    )
    for d in (2, 1, 3):
        send(e_y.at[y], e_y.at[y], (ey_sem.at[0], ey_sem.at[1]), on_column(d))

    with jax.named_scope("w_halo_b"):
        take(halo_recv.at[1], o_buf.at[pl.ds(0, 2)])
        take(halo_recv.at[2], g_in)
    h_buf[1] += NEAR * o_buf[1] + FAR * o_buf[0]
    h_buf[2] += FAR * o_buf[1]
    h_buf[8] += NEAR * o_buf[10] + FAR * o_buf[11]
    h_buf[7] += FAR * o_buf[10]
    r_buf[0] += K0 * o_buf[1]
    r_buf[7] += K0 * o_buf[10]
    for ghost, at, inner, outer, side in ((1, 0, 2, 0, 0), (10, 9, 9, 11, 1)):
        centre = o_buf[ghost]
        first = (o_buf[inner] + o_buf[outer]) + beside(centre)
        second = o_buf[2 * inner - ghost] + beside_two(centre)
        h_buf[at] = 3.75 * centre + g_in[side] + NEAR * first + FAR * second
    for q in range(PLANES // 2):
        both = None
        for p in (2 * q, 2 * q + 1):
            value = h_buf[p + 1]
            rest = value * THIRD + K0 * ((h_buf[p] + h_buf[p + 2]) + beside(value))
            a_buf[p] = C0 * (value + rest)
            b_buf[p] = C0 * (o_buf[p + 2] + r_buf[p])
            both = rest if both is None else both + rest
        pair_buf[q] = both
        pair_buf[q + 4] = r_buf[2 * q] + r_buf[2 * q + 1]
    halved = pair_buf[:, pl.ds(0, 32, 2), :] + pair_buf[:, pl.ds(1, 32, 2), :]
    halved = [halved[:4].reshape(LANES, LANES), halved[4:].reshape(LANES, LANES)]
    f1 = times(jnp.concatenate(halved, 1), mats[0:2].reshape(2 * LANES, LANES))
    f1 = f1.reshape(4, 32, LANES)
    f1_buf[2:6] = f1
    sems = (f1_sem.at[0], f1_sem.at[1])
    send(f1_buf.at[pl.ds(4, 2)], f1_buf.at[pl.ds(0, 2)], sems, right)
    send(f1_buf.at[pl.ds(2, 2)], f1_buf.at[pl.ds(6, 2)], sems, left)

    rest = []
    for p in range(4):
        total = beside(f1[p], 64)
        for q in (p - 1, p + 1):
            if 0 <= q < 4:
                total += f1[q]
        rest.append(f1[p] * THIRD + K1 * total)
    two_buf[0] = K1 * f1[0]
    two_buf[1] = rest[0] + rest[1]
    two_buf[2] = rest[2] + rest[3]
    two_buf[3] = K1 * f1[3]
    halved = two_buf[:, pl.ds(0, 16, 2), :] + two_buf[:, pl.ds(1, 16, 2), :]
    share = times(halved.reshape(64, LANES), mats[2]).reshape(4, 16, LANES)
    low = iota((8, LANES), 1) < 64
    for k in range(4):
        f2_out[k] = jnp.where(low, share[k][:8], share[k][8:])
    a, b, c, d = share[0], share[1], share[2], share[3]
    three_buf[0] = a * (K2 + THIRD) + K2 * (b + beside(a, 32))
    three_buf[1] = (b + c) * (THIRD + K2) + K2 * ((a + d) + (beside(b, 32) + beside(c, 32)))
    three_buf[2] = d * (K2 + THIRD) + K2 * (c + beside(d, 32))
    halved = three_buf[:, pl.ds(0, 8, 2), :] + three_buf[:, pl.ds(1, 8, 2), :]
    parts = times(halved.reshape(24, LANES), mats[3]).reshape(3, 8, LANES)
    lane = iota((8, LANES), 1)
    f3_in[REACH] = jnp.where(
        lane < 32, parts[0],
        jnp.where(lane < 64, parts[1], jnp.where(lane < 96, parts[2], 0.0)),
    )
    with jax.named_scope("w_t2"):
        pl.semaphore_wait(token.at[2], 2)
    sems = (f3_sem.at[0], f3_sem.at[1])
    for step in range(REACH, 0, -1):
        send(f3_in.at[REACH], f3_in.at[REACH - step], sems, slab(step))
        send(f3_in.at[REACH], f3_in.at[REACH + step], sems, slab(-step))
    sems = (f2_sem.at[0], f2_sem.at[1])
    send(f2_out.at[pl.ds(1, 3)], f2_in.at[pl.ds(0, 3)], sems, right)
    send(f2_out.at[pl.ds(0, 3)], f2_in.at[pl.ds(3, 3)], sems, left)
    send(f2_out.at[3], f2_in.at[6], sems, slab(2))
    send(f2_out.at[0], f2_in.at[7], sems, slab(-2))

    with jax.named_scope("w_ey"):
        take(ey_sem.at[1], e_y.at[pl.ds(0, columns - 1)])
    e_z[z] = jnp.sum(e_y[...], axis=0)
    with jax.named_scope("w_t3"):
        pl.semaphore_wait(token.at[1], 3)
    for d in sorted(range(1, RING), key=lambda d: abs(d - RING // 2)):
        send(e_z.at[z], e_z.at[z], (ez_sem.at[0], ez_sem.at[1]), on_ring(d))

    with jax.named_scope("w_f"):
        take(f3_sem.at[1], f3_in.at[pl.ds(0, 2 * REACH)])
        take(f2_sem.at[1], f2_in)
        take(f1_sem.at[1], f1_buf.at[pl.ds(0, 4)])

    source = {}
    for p in range(1 - REACH, REACH):
        at = p + REACH
        total = jnp.where(lane < 32, f3_in[at + 1], jnp.where(lane < 64, f3_in[at], f3_in[at - 1]))
        total = total + pltpu.roll(total, 32, 1)
        source[p] = total + pltpu.roll(total, 64, 1)
    iterate = {p: C3 * source[p] for p in source}
    for reach in (2, 1):
        iterate = {
            p: iterate[p] * THIRD + C3 * source[p]
            + K3 * ((iterate[p - 1] + iterate[p + 1]) + beside(iterate[p], 16))
            for p in range(-reach, reach + 1)
        }
    spread = times(jnp.concatenate([iterate[p] for p in range(-1, 2)], 0), mats[4]).reshape(3, 8, LANES)
    up2_buf[:, pl.ds(0, 8, 2), :] = spread
    up2_buf[:, pl.ds(1, 8, 2), :] = spread

    def unfold(tile):
        turned = pltpu.roll(tile, 64, 1)
        return jnp.concatenate([jnp.where(low, tile, turned), jnp.where(low, turned, tile)], 0)

    f2 = {
        -2: unfold(f2_in[0] + f2_in[6]),
        -1: share[0] + unfold(f2_in[1]),
        0: share[1] + unfold(f2_in[2]),
        1: share[2] + unfold(f2_in[3]),
        2: share[3] + unfold(f2_in[4]),
        3: unfold(f2_in[5] + f2_in[7]),
    }
    fixed = {p: C2 * f2[p] + up2_buf[(p >> 1) + 1] for p in range(-2, 4)}
    value = [
        fixed[p] * THIRD + C2 * f2[p] + K2 * ((fixed[p - 1] + fixed[p + 1]) + beside(fixed[p], 32))
        for p in range(-1, 3)
    ]
    spread = times(jnp.concatenate(value, 0), mats[5]).reshape(4, 16, LANES)
    up1_buf[:, pl.ds(0, 16, 2), :] = spread
    up1_buf[:, pl.ds(1, 16, 2), :] = spread
    fixed = {p: C1 * f1_buf[p + 2] + up1_buf[(p >> 1) + 1] for p in range(-2, 6)}
    error = jnp.concatenate(
        [
            fixed[p] * THIRD + C1 * f1_buf[p + 2]
            + K1 * ((fixed[p - 1] + fixed[p + 1]) + beside(fixed[p], 64))
            for p in range(-1, 5)
        ],
        0,
    )

    spread = times(error, wide[...])
    for at, up_buf, last in ((0, uph_buf, a_buf), (LANES, upo_buf, b_buf)):
        part = spread[:, at : at + LANES].reshape(6, 32, LANES)
        up_buf[:, pl.ds(0, 32, 2), :] = part
        up_buf[:, pl.ds(1, 32, 2), :] = part
        for q in range(1, 5):
            value = up_buf[q]
            same = value * (THIRD + K0) + K0 * beside(value)
            last[2 * q - 2] += same + K0 * up_buf[q - 1]
            last[2 * q - 1] += same + K0 * up_buf[q + 1]
    with jax.named_scope("w_ez"):
        take(ez_sem.at[1], e_z.at[pl.ds(0, RING - 1)])
    sums = jnp.sum(e_z[...], axis=0)
    numer = jnp.sum(jnp.where(lane_row < 64, sums, 0.0), axis=1, keepdims=True)
    denom = jnp.sum(jnp.where(lane_row < 64, 0.0, sums), axis=1, keepdims=True)
    energy = numer / denom

    def finish(p):
        value = a_buf[p] - energy * b_buf[p]
        out_ref[0, p] = value
        return value.astype(jnp.bfloat16)

    for step, other in others:
        to = state_at(step, other)
        rounded[to] = finish(to)
        send(rounded.at[to], mixed.at[s], (x_sem.at[0], x_sem.at[1]), (g, to))
    mixed[s] = finish(s)
    with jax.named_scope("w_mix"):
        take(x_sem.at[1], mixed.at[pl.ds(0, STATES - 1)])

    pairs = [(i, j) for i in range(STATES) for j in range(i, STATES)]
    held = {pair: None for pair in pairs}
    for block in range(ROWS // 16):
        values = [mixed[i, 16 * block : 16 * block + 16].astype(F32) for i in range(STATES)]
        for i, j in pairs:
            product = values[i] * values[j]
            product = product[:8] + product[8:]
            held[i, j] = product if held[i, j] is None else held[i, j] + product
    for i, j in pairs:
        row = jnp.sum(held[i, j], 0, keepdims=True)
        rows_buf[8 * i + j : 8 * i + j + 1] = row
        if i != j:
            rows_buf[8 * j + i : 8 * j + i + 1] = row
    flat = lax.dot_general(
        jnp.ones((8, LANES), F32), rows_buf[...], (((1,), (1,)), ((), ())),
        precision=HIGH, preferred_element_type=F32,
    )
    g_z[z] = flat[:1]
    for d in sorted(range(1, RING), key=lambda d: abs(d - RING // 2)):
        send(g_z.at[z], g_z.at[z], (gz_sem.at[0], gz_sem.at[1]), on_ring(d))
    with jax.named_scope("w_gz"):
        take(gz_sem.at[1], g_z.at[pl.ds(0, RING - 1)])
    mine = y * STATES + s
    g_xy[mine] = jnp.sum(g_z[...], axis=0)
    for d in sorted(range(1, STATES * columns), key=lambda d: abs(d // STATES - 2) + abs(d % STATES - 4) / 2):
        send(g_xy.at[mine], g_xy.at[mine], (gx_sem.at[0], gx_sem.at[1]), on_face(d))
    with jax.named_scope("w_sends"):
        take(halo_send, o_buf.at[pl.ds(0, 6)])
        take(f1_sem.at[0], f1_buf.at[pl.ds(0, 4)])
        take(f2_sem.at[0], f2_in)
        take(f3_sem.at[0], f3_in.at[pl.ds(0, 2 * REACH)])
        take(ey_sem.at[0], e_y.at[pl.ds(0, columns - 1)])
        take(ez_sem.at[0], e_z.at[pl.ds(0, RING - 1)])
        take(x_sem.at[0], mixed.at[pl.ds(0, STATES - 1)])
        take(gz_sem.at[0], g_z.at[pl.ds(0, RING - 1)])
    with jax.named_scope("w_gxy"):
        take(gx_sem.at[1], g_xy.at[pl.ds(0, STATES * columns - 1)])
    total = jnp.sum(g_xy[...], axis=0)
    picked = jnp.zeros((1, STATES), F32)
    for t in range(STATES):
        picked += jnp.where(s == t, total[:, STATES * t : STATES * t + STATES], 0.0)
    gram_ref[...] = picked / F32(PLANES * ROWS * LANES * slabs)
    with jax.named_scope("w_last"):
        take(gx_sem.at[0], g_xy.at[pl.ds(0, STATES * columns - 1)])


def solution(mesh):
    slabs = mesh.shape["grid"]
    columns = slabs // RING
    faces = STATES * columns
    dma = pltpu.SemaphoreType.DMA

    def vmem(*shape, dtype=F32):
        return pltpu.VMEM(shape, dtype)

    def write_out(values, gram, values_hbm, gram_hbm, sem):
        copies = [
            pltpu.make_async_copy(values, values_hbm, sem.at[0]),
            pltpu.make_async_copy(gram, gram_hbm, sem.at[1]),
        ]
        for copy in copies:
            copy.start()
        for copy in copies:
            copy.wait()

    def on_device(orbitals, potential):
        shapes = (
            jax.ShapeDtypeStruct((1, PLANES, ROWS, LANES), F32),
            jax.ShapeDtypeStruct((1, STATES), F32),
        )
        results = pl.pallas_call(
            functools.partial(kernel, slabs),
            out_shape=(
                jax.ShapeDtypeStruct((1, PLANES, ROWS, LANES), F32),
                jax.ShapeDtypeStruct((1, STATES), F32),
            ),
            in_specs=[pl.BlockSpec(memory_space=pltpu.HBM)] * 2,
            out_specs=(
                pl.BlockSpec(memory_space=pltpu.VMEM),
                pl.BlockSpec(memory_space=pltpu.VMEM),
            ),
            scratch_shapes=[
                vmem(PLANES + 4, ROWS, LANES),
                vmem(PLANES, ROWS, LANES),
                vmem(PLANES + 2, ROWS, LANES),
                vmem(PLANES, ROWS, LANES),
                vmem(2, ROWS, LANES),
                vmem(2, ROWS, LANES),
                vmem(PLANES, ROWS, LANES),
                vmem(6, LANES, LANES),
                vmem(8, 32, LANES),
                vmem(4, 32, LANES),
                vmem(4, 8, LANES),
                vmem(8, 8, LANES),
                vmem(3, 16, LANES),
                vmem(2 * REACH + 1, 8, LANES),
                vmem(3, 16, LANES),
                vmem(4, 32, LANES),
                vmem(6, ROWS, LANES),
                vmem(6, ROWS, LANES),
                vmem(PLANES, ROWS, LANES),
                vmem(PLANES, ROWS, LANES),
                vmem(columns, 1, LANES),
                vmem(RING, 1, LANES),
                vmem(PLANES, ROWS, LANES, dtype=jnp.bfloat16),
                vmem(STATES, ROWS, LANES, dtype=jnp.bfloat16),
                vmem(LANES, LANES),
                vmem(RING, 1, LANES),
                vmem(faces, 1, LANES),
                vmem(LANES, 2 * LANES),
                dma((2,)), dma(()), dma((3,)), dma((2,)), dma((2,)), dma((2,)),
                dma((2,)), dma((2,)), dma((2,)), dma((2,)), dma((2,)),
                pltpu.SemaphoreType.REGULAR((3,)),
            ],
            compiler_params=pltpu.CompilerParams(
                collective_id=0, has_side_effects=True, vmem_limit_bytes=32 * 1024 * 1024
            ),
        )(*[pltpu.with_memory_space_constraint(v, pltpu.HBM) for v in (orbitals, potential)])

        return pl.pallas_call(
            write_out,
            out_shape=shapes,
            in_specs=[pl.BlockSpec(memory_space=pltpu.VMEM)] * 2,
            out_specs=(pl.BlockSpec(memory_space=pltpu.HBM), pl.BlockSpec(memory_space=pltpu.HBM)),
            scratch_shapes=[dma((2,))],
            compiler_params=pltpu.CompilerParams(vmem_limit_bytes=1024 * 1024),
        )(*results)

    return jax.shard_map(
        on_device,
        mesh=mesh,
        in_specs=(P("state", "grid", None, None), P("grid", None, None)),
        out_specs=(P("state", "grid", None, None), P("state", None)),
        check_vma=False,
    )
```

```python
import functools

import jax
import jax.numpy as jnp
from jax import lax
from jax.experimental import pallas as pl
from jax.experimental.pallas import tpu as pltpu
from jax.sharding import PartitionSpec as P

MESH = pl.DeviceIdType.MESH
HIGH = lax.Precision.HIGHEST
F32 = jnp.float32

SHIFT_TERM = 0.25
DAMPING = 2.0 / 3.0
LANES = 128
ROWS = 64
HALF = ROWS // 2
PLANES = 8
STATES = 8
CHIPS = 4
RING = 16
REACH = 4
THIRD = 1.0 / 3.0
NEAR = -2.0 / 3.0
FAR = 1.0 / 24.0


def scales(level):
    inverse = 0.25**level
    diagonal = SHIFT_TERM + 3.0 * inverse
    scaled = DAMPING / diagonal
    return scaled, 0.5 * inverse * scaled


C0, K0 = scales(0)
C1, K1 = scales(1)
C2, K2 = scales(2)
C3, K3 = scales(3)


def iota(shape, dim):
    return lax.broadcasted_iota(jnp.int32, shape, dim)


def beside(plane, segment=LANES):
    rows = plane.shape[0]
    total = pltpu.roll(plane, 1, 0) + pltpu.roll(plane, rows - 1, 0)
    low, high = pltpu.roll(plane, 1, 1), pltpu.roll(plane, LANES - 1, 1)
    if segment != LANES:
        cell = iota(plane.shape, 1) & (segment - 1)
        low = jnp.where(cell == 0, pltpu.roll(plane, LANES - segment + 1, 1), low)
        high = jnp.where(cell == segment - 1, pltpu.roll(plane, segment - 1, 1), high)
    return total + (low + high)


def beside_two(plane):
    rows = plane.shape[0]
    total = pltpu.roll(plane, 2, 0) + pltpu.roll(plane, rows - 2, 0)
    return total + (pltpu.roll(plane, 2, 1) + pltpu.roll(plane, LANES - 2, 1))


def matrices():
    k, j = iota((LANES, LANES), 0), iota((LANES, LANES), 1)
    down_h = (j < 64) & ((k >> 1) == j)
    down_o = (j >= 64) & ((k >> 1) == j - 64)
    down_two = ((k >> 6) == ((j >> 5) & 1)) & (((k & 63) >> 1) == (j & 31))
    down_three = (k < 64) & ((k >> 5) == ((j >> 4) & 1)) & (((k & 31) >> 1) == (j & 15))
    up_two = (k < 32) & ((k >> 4) == ((j >> 5) & 1)) & ((k & 15) == ((j & 31) >> 1))
    up_one = (k < 64) & ((k >> 5) == (j >> 6)) & ((k & 31) == ((j & 63) >> 1))
    up_h = k == (j >> 1)
    up_o = k - 64 == (j >> 1)
    eighth, one = jnp.full((LANES, LANES), 0.125, F32), jnp.ones((LANES, LANES), F32)
    zero = jnp.zeros((LANES, LANES), F32)
    return [
        jnp.where(mask, eighth, zero) for mask in (down_h, down_o, down_two, down_three)
    ] + [jnp.where(mask, one, zero) for mask in (up_two, up_one, up_h, up_o)]


def times(left, right):
    return jnp.dot(left, right, precision=HIGH, preferred_element_type=F32)


def kernel(
    slabs,
    o_hbm, p_hbm, out_ref, gram_ref,
    o_buf, p_buf, h_buf, r_buf, g_out, g_in, pair_buf, mats,
    f1_buf, two_buf, f2_out, f2_in, three_buf, f3_in,
    up2_buf, up1_buf, uph_buf, upo_buf, a_buf, b_buf,
    e_y, e_z, rounded, mixed, rows_buf, g_z, g_xy, wide,
    load_sem, halo_send, halo_recv, f1_sem, f2_sem, f3_sem, ey_sem, ez_sem, x_sem, gz_sem, gx_sem,
    token,
):
    g, s = lax.axis_index("grid"), lax.axis_index("state")
    y, z = g >> 4, g & (RING - 1)
    x, core = s >> 1, s & 1
    columns = slabs // RING

    def slab(step):
        return ((g + step) & (slabs - 1), s)

    def on_ring(step):
        return (y * RING + ((z + step) & (RING - 1)), s)

    def on_column(step):
        return (((y + step) & (columns - 1)) * RING + z, s)

    hub = core == 1
    chip_states = (s - core, s - core + 1)

    def state_at(step, other):
        return 2 * ((x + step) & (CHIPS - 1)) + (1 - core if other else core)

    def on_face(step):
        up, side = step // STATES, step % STATES
        return (((y + up) & (columns - 1)) * RING + z, (s + side) & (STATES - 1))

    def each_core(zero, one):
        pl.when(core == 0)(zero)
        pl.when(core == 1)(one)

    def send(src, dst, sems, peer):
        copy = pltpu.make_async_remote_copy(
            src_ref=src, dst_ref=dst, send_sem=sems[0], recv_sem=sems[1],
            device_id=peer, device_id_type=MESH,
        )
        copy.start()

    def take(sem, view):
        pltpu.make_async_copy(view, view, sem).wait()

    def signal(sem, peers):
        for peer in peers:
            pl.semaphore_signal(sem, inc=1, device_id=peer, device_id_type=MESH)

    others = [(step, other) for step in (2, 1, -1) for other in (False, True)] + [(0, True)]
    next_two = [slab(1), slab(-1), on_ring(2), on_ring(-2)]
    partner = (g, state_at(0, True))
    next_two += [on_column(1), on_column(-1), (g, state_at(1, False)), (g, state_at(-1, False))]
    close = next_two + [on_ring(1), on_ring(-1), partner]
    barrier = pltpu.get_barrier_semaphore()
    signal(barrier, close)
    loads = [
        pltpu.make_async_copy(o_hbm.at[0], o_buf.at[pl.ds(2, PLANES)], load_sem.at[0]),
        pltpu.make_async_copy(p_hbm, p_buf, load_sem.at[1]),
    ]
    for load in loads:
        load.start()
    with jax.named_scope("w_load"):
        for load in loads:
            load.wait()
    with jax.named_scope("w_barrier"):
        pl.semaphore_wait(barrier, len(close))

    right, left = slab(1), slab(-1)

    def halo(part, mine, theirs):
        sems = (halo_send, halo_recv.at[part])
        send(o_buf.at[pl.ds(8, 2), pl.ds(mine, HALF)], o_buf.at[pl.ds(0, 2), pl.ds(mine, HALF)], sems, right)
        send(o_buf.at[pl.ds(2, 2), pl.ds(theirs, HALF)], o_buf.at[pl.ds(10, 2), pl.ds(theirs, HALF)], sems, left)

    signal(token.at[0], next_two)
    halo(0, 0, HALF)
    g_out[0] = p_buf[0] * o_buf[2] + FAR * o_buf[4]
    g_out[1] = p_buf[7] * o_buf[9] + FAR * o_buf[7]

    top = jnp.zeros((ROWS, LANES), F32)
    bottom = jnp.zeros((ROWS, LANES), F32)
    for p in range(PLANES):
        centre = o_buf[p + 2]
        first, second = beside(centre), beside_two(centre)
        for q in (p - 1, p + 1):
            if 0 <= q < PLANES:
                first += o_buf[q + 2]
        for q in (p - 2, p + 2):
            if 0 <= q < PLANES:
                second += o_buf[q + 2]
        value = (3.75 + p_buf[p]) * centre + NEAR * first + FAR * second
        h_buf[p + 1] = value
        r_buf[p] = centre * THIRD + K0 * first
        top += centre * value
        bottom += centre * centre
    halo(1, HALF, 0)
    sems = (halo_send, halo_recv.at[2])
    send(g_out.at[1], g_in.at[0], sems, right)
    send(g_out.at[0], g_in.at[1], sems, left)
    made = matrices()
    for index in range(6):
        mats[index] = made[index]
    wide[:, :LANES] = made[6]
    wide[:, LANES:] = made[7]
    rows_buf[...] = jnp.zeros_like(rows_buf)
    top, bottom = jnp.sum(top, 0, keepdims=True), jnp.sum(bottom, 0, keepdims=True)
    lane_row = iota((1, LANES), 1)

    with jax.named_scope("w_t1"):
        pl.semaphore_wait(token.at[0], len(next_two))
    signal(token.at[1], [on_ring(4), on_ring(-4)])
    signal(token.at[3], [partner])
    signal(token.at[2], [slab(2), slab(-2)])
    with jax.named_scope("w_halo_a"):
        take(halo_recv.at[0], o_buf.at[pl.ds(0, 2)])
    cross = o_buf[2, :HALF] * (2.0 * NEAR * o_buf[1, :HALF] + 2.0 * FAR * o_buf[0, :HALF])
    cross += 2.0 * FAR * o_buf[1, :HALF] * o_buf[3, :HALF]
    cross += o_buf[9, HALF:] * (2.0 * NEAR * o_buf[10, HALF:] + 2.0 * FAR * o_buf[11, HALF:])
    cross += 2.0 * FAR * o_buf[10, HALF:] * o_buf[8, HALF:]
    top += jnp.sum(cross, 0, keepdims=True)
    e_y[core * columns + y] = jnp.where(
        lane_row < 64, top + pltpu.roll(top, 64, 1), bottom + pltpu.roll(bottom, 64, 1)
    )
    pl.semaphore_wait(token.at[3], 1)

    def to_hubs(steps):
        mine = e_y.at[core * columns + y]
        for d in steps:
            send(mine, mine, (ey_sem.at[0], ey_sem.at[1]), (on_column(d)[0], chip_states[1]))

    each_core(lambda: to_hubs((2, 1, 3, 0)), lambda: to_hubs((2, 1, 3)))

    with jax.named_scope("w_halo_b"):
        take(halo_recv.at[1], o_buf.at[pl.ds(0, 2)])
        take(halo_recv.at[2], g_in)
    h_buf[1] += NEAR * o_buf[1] + FAR * o_buf[0]
    h_buf[2] += FAR * o_buf[1]
    h_buf[8] += NEAR * o_buf[10] + FAR * o_buf[11]
    h_buf[7] += FAR * o_buf[10]
    r_buf[0] += K0 * o_buf[1]
    r_buf[7] += K0 * o_buf[10]
    for ghost, at, inner, outer, side in ((1, 0, 2, 0, 0), (10, 9, 9, 11, 1)):
        centre = o_buf[ghost]
        first = (o_buf[inner] + o_buf[outer]) + beside(centre)
        second = o_buf[2 * inner - ghost] + beside_two(centre)
        h_buf[at] = 3.75 * centre + g_in[side] + NEAR * first + FAR * second
    for q in range(PLANES // 2):
        both = None
        for p in (2 * q, 2 * q + 1):
            value = h_buf[p + 1]
            rest = value * THIRD + K0 * ((h_buf[p] + h_buf[p + 2]) + beside(value))
            a_buf[p] = C0 * (value + rest)
            b_buf[p] = C0 * (o_buf[p + 2] + r_buf[p])
            both = rest if both is None else both + rest
        pair_buf[q] = both
        pair_buf[q + 4] = r_buf[2 * q] + r_buf[2 * q + 1]
    halved = pair_buf[:, pl.ds(0, 32, 2), :] + pair_buf[:, pl.ds(1, 32, 2), :]
    halved = [halved[:4].reshape(LANES, LANES), halved[4:].reshape(LANES, LANES)]
    f1 = times(jnp.concatenate(halved, 1), mats[0:2].reshape(2 * LANES, LANES))
    f1 = f1.reshape(4, 32, LANES)
    f1_buf[2:6] = f1
    sems = (f1_sem.at[0], f1_sem.at[1])
    send(f1_buf.at[pl.ds(4, 2)], f1_buf.at[pl.ds(0, 2)], sems, right)
    send(f1_buf.at[pl.ds(2, 2)], f1_buf.at[pl.ds(6, 2)], sems, left)

    rest = []
    for p in range(4):
        total = beside(f1[p], 64)
        for q in (p - 1, p + 1):
            if 0 <= q < 4:
                total += f1[q]
        rest.append(f1[p] * THIRD + K1 * total)
    two_buf[0] = K1 * f1[0]
    two_buf[1] = rest[0] + rest[1]
    two_buf[2] = rest[2] + rest[3]
    two_buf[3] = K1 * f1[3]
    halved = two_buf[:, pl.ds(0, 16, 2), :] + two_buf[:, pl.ds(1, 16, 2), :]
    share = times(halved.reshape(64, LANES), mats[2]).reshape(4, 16, LANES)
    low = iota((8, LANES), 1) < 64
    for k in range(4):
        f2_out[k] = jnp.where(low, share[k][:8], share[k][8:])
    a, b, c, d = share[0], share[1], share[2], share[3]
    three_buf[0] = a * (K2 + THIRD) + K2 * (b + beside(a, 32))
    three_buf[1] = (b + c) * (THIRD + K2) + K2 * ((a + d) + (beside(b, 32) + beside(c, 32)))
    three_buf[2] = d * (K2 + THIRD) + K2 * (c + beside(d, 32))
    halved = three_buf[:, pl.ds(0, 8, 2), :] + three_buf[:, pl.ds(1, 8, 2), :]
    parts = times(halved.reshape(24, LANES), mats[3]).reshape(3, 8, LANES)
    lane = iota((8, LANES), 1)
    f3_in[REACH] = jnp.where(
        lane < 32, parts[0],
        jnp.where(lane < 64, parts[1], jnp.where(lane < 96, parts[2], 0.0)),
    )
    with jax.named_scope("w_t2"):
        pl.semaphore_wait(token.at[2], 2)
    sems = (f3_sem.at[0], f3_sem.at[1])
    for step in range(REACH, 0, -1):
        send(f3_in.at[REACH], f3_in.at[REACH - step], sems, slab(step))
        send(f3_in.at[REACH], f3_in.at[REACH + step], sems, slab(-step))
    sems = (f2_sem.at[0], f2_sem.at[1])
    send(f2_out.at[pl.ds(1, 3)], f2_in.at[pl.ds(0, 3)], sems, right)
    send(f2_out.at[pl.ds(0, 3)], f2_in.at[pl.ds(3, 3)], sems, left)
    send(f2_out.at[3], f2_in.at[6], sems, slab(2))
    send(f2_out.at[0], f2_in.at[7], sems, slab(-2))

    with jax.named_scope("w_t3"):
        pl.semaphore_wait(token.at[1], 2)
    far_first = sorted(range(1, RING), key=lambda d: abs(d - RING // 2))

    @pl.when(core == 0)
    def _():
        signal(token.at[4], [partner])

    @pl.when(hub)
    def _():
        pl.semaphore_wait(token.at[4], 1)
        take(ey_sem.at[1], e_y.at[pl.ds(0, 2 * columns - 1)])
        first = jnp.sum(e_y[:columns], axis=0)
        second = jnp.sum(e_y[columns:], axis=0)
        first, second = first + pltpu.roll(first, 96, 1), second + pltpu.roll(second, 96, 1)
        e_z[z] = jnp.where(
            lane_row < 64,
            jnp.where(lane_row < 32, first, pltpu.roll(first, 96, 1)),
            jnp.where(lane_row < 96, pltpu.roll(second, 64, 1), pltpu.roll(second, 32, 1)),
        )
        for d in far_first:
            for state in chip_states:
                send(e_z.at[z], e_z.at[z], (ez_sem.at[0], ez_sem.at[1]), (on_ring(d)[0], state))
        send(e_z.at[z], e_z.at[z], (ez_sem.at[0], ez_sem.at[1]), partner)

    with jax.named_scope("w_f"):
        take(f3_sem.at[1], f3_in.at[pl.ds(0, 2 * REACH)])
        take(f2_sem.at[1], f2_in)
        take(f1_sem.at[1], f1_buf.at[pl.ds(0, 4)])

    source = {}
    for p in range(1 - REACH, REACH):
        at = p + REACH
        total = jnp.where(lane < 32, f3_in[at + 1], jnp.where(lane < 64, f3_in[at], f3_in[at - 1]))
        total = total + pltpu.roll(total, 32, 1)
        source[p] = total + pltpu.roll(total, 64, 1)
    iterate = {p: C3 * source[p] for p in source}
    for reach in (2, 1):
        iterate = {
            p: iterate[p] * THIRD + C3 * source[p]
            + K3 * ((iterate[p - 1] + iterate[p + 1]) + beside(iterate[p], 16))
            for p in range(-reach, reach + 1)
        }
    spread = times(jnp.concatenate([iterate[p] for p in range(-1, 2)], 0), mats[4]).reshape(3, 8, LANES)
    up2_buf[:, pl.ds(0, 8, 2), :] = spread
    up2_buf[:, pl.ds(1, 8, 2), :] = spread

    def unfold(tile):
        turned = pltpu.roll(tile, 64, 1)
        return jnp.concatenate([jnp.where(low, tile, turned), jnp.where(low, turned, tile)], 0)

    f2 = {
        -2: unfold(f2_in[0] + f2_in[6]),
        -1: share[0] + unfold(f2_in[1]),
        0: share[1] + unfold(f2_in[2]),
        1: share[2] + unfold(f2_in[3]),
        2: share[3] + unfold(f2_in[4]),
        3: unfold(f2_in[5] + f2_in[7]),
    }
    fixed = {p: C2 * f2[p] + up2_buf[(p >> 1) + 1] for p in range(-2, 4)}
    value = [
        fixed[p] * THIRD + C2 * f2[p] + K2 * ((fixed[p - 1] + fixed[p + 1]) + beside(fixed[p], 32))
        for p in range(-1, 3)
    ]
    spread = times(jnp.concatenate(value, 0), mats[5]).reshape(4, 16, LANES)
    up1_buf[:, pl.ds(0, 16, 2), :] = spread
    up1_buf[:, pl.ds(1, 16, 2), :] = spread
    fixed = {p: C1 * f1_buf[p + 2] + up1_buf[(p >> 1) + 1] for p in range(-2, 6)}
    error = jnp.concatenate(
        [
            fixed[p] * THIRD + C1 * f1_buf[p + 2]
            + K1 * ((fixed[p - 1] + fixed[p + 1]) + beside(fixed[p], 64))
            for p in range(-1, 5)
        ],
        0,
    )

    spread = times(error, wide[...])
    for at, up_buf, last in ((0, uph_buf, a_buf), (LANES, upo_buf, b_buf)):
        part = spread[:, at : at + LANES].reshape(6, 32, LANES)
        up_buf[:, pl.ds(0, 32, 2), :] = part
        up_buf[:, pl.ds(1, 32, 2), :] = part
        for q in range(1, 5):
            value = up_buf[q]
            same = value * (THIRD + K0) + K0 * beside(value)
            last[2 * q - 2] += same + K0 * up_buf[q - 1]
            last[2 * q - 1] += same + K0 * up_buf[q + 1]
    each_core(
        lambda: take(ez_sem.at[1], e_z.at[pl.ds(0, RING)]),
        lambda: take(ez_sem.at[1], e_z.at[pl.ds(0, RING - 1)]),
    )
    with jax.named_scope("w_ez"):
        sums = jnp.sum(e_z[...], axis=0)
    part = lane_row >> 5
    numer = jnp.sum(jnp.where(part == 2 * core, sums, 0.0), axis=1, keepdims=True)
    denom = jnp.sum(jnp.where(part == 2 * core + 1, sums, 0.0), axis=1, keepdims=True)
    energy = numer / denom

    def finish(p):
        value = a_buf[p] - energy * b_buf[p]
        out_ref[0, p] = value
        return value.astype(jnp.bfloat16)

    for step, other in others:
        to = state_at(step, other)
        rounded[to] = finish(to)
        send(rounded.at[to], mixed.at[s], (x_sem.at[0], x_sem.at[1]), (g, to))
    mixed[s] = finish(s)
    with jax.named_scope("w_mix"):
        take(x_sem.at[1], mixed.at[pl.ds(0, STATES - 1)])

    pairs = [(i, j) for i in range(STATES) for j in range(i, STATES)]
    held = {pair: None for pair in pairs}
    for block in range(ROWS // 16):
        values = [mixed[i, 16 * block : 16 * block + 16].astype(F32) for i in range(STATES)]
        for i, j in pairs:
            product = values[i] * values[j]
            product = product[:8] + product[8:]
            held[i, j] = product if held[i, j] is None else held[i, j] + product
    for i, j in pairs:
        row = jnp.sum(held[i, j], 0, keepdims=True)
        rows_buf[8 * i + j : 8 * i + j + 1] = row
        if i != j:
            rows_buf[8 * j + i : 8 * j + i + 1] = row
    flat = lax.dot_general(
        jnp.ones((8, LANES), F32), rows_buf[...], (((1,), (1,)), ((), ())),
        precision=HIGH, preferred_element_type=F32,
    )
    mine = core * RING + z
    g_z[mine] = flat[:1]
    rows_out = (gz_sem.at[0], gz_sem.at[1])
    for d in far_first:
        send(g_z.at[mine], g_z.at[mine], rows_out, (on_ring(d)[0], chip_states[1]))
    pl.when(core == 0)(lambda: send(g_z.at[mine], g_z.at[mine], rows_out, partner))

    @pl.when(hub)
    def _():
        take(gz_sem.at[1], g_z.at[pl.ds(0, 2 * RING - 1)])
        place = y * CHIPS + x
        g_xy[place] = jnp.sum(g_z[...], axis=0)
        for d in sorted(range(1, STATES * columns), key=lambda d: abs(d // STATES - 2) + abs(d % STATES - 4) / 2):
            send(g_xy.at[place], g_xy.at[place], (gx_sem.at[0], gx_sem.at[1]), on_face(d))

    with jax.named_scope("w_sends"):
        take(halo_send, o_buf.at[pl.ds(0, 6)])
        take(f1_sem.at[0], f1_buf.at[pl.ds(0, 4)])
        take(f2_sem.at[0], f2_in)
        take(f3_sem.at[0], f3_in.at[pl.ds(0, 2 * REACH)])
        take(x_sem.at[0], mixed.at[pl.ds(0, STATES - 1)])

    @pl.when(core == 0)
    def _():
        take(ey_sem.at[0], g_z.at[pl.ds(0, columns)])
        take(gz_sem.at[0], g_z.at[pl.ds(0, RING)])
        take(gx_sem.at[1], g_xy)

    @pl.when(hub)
    def _():
        take(ey_sem.at[0], g_z.at[pl.ds(0, columns - 1)])
        take(ez_sem.at[0], g_z.at[pl.ds(0, 2 * RING - 1)])
        take(gz_sem.at[0], g_z.at[pl.ds(0, RING - 1)])
        take(gx_sem.at[1], g_xy.at[pl.ds(0, CHIPS * columns - 1)])

    total = jnp.sum(g_xy[...], axis=0)
    picked = jnp.zeros((1, STATES), F32)
    for t in range(STATES):
        picked += jnp.where(s == t, total[:, STATES * t : STATES * t + STATES], 0.0)
    gram_ref[...] = picked / F32(PLANES * ROWS * LANES * slabs)
    pl.when(hub)(lambda: take(gx_sem.at[0], g_z.at[pl.ds(0, STATES * columns - 1)]))


def solution(mesh):
    slabs = mesh.shape["grid"]
    columns = slabs // RING
    dma = pltpu.SemaphoreType.DMA

    def vmem(*shape, dtype=F32):
        return pltpu.VMEM(shape, dtype)

    def write_out(values, gram, values_hbm, gram_hbm, sem):
        copies = [
            pltpu.make_async_copy(values, values_hbm, sem.at[0]),
            pltpu.make_async_copy(gram, gram_hbm, sem.at[1]),
        ]
        for copy in copies:
            copy.start()
        for copy in copies:
            copy.wait()

    def on_device(orbitals, potential):
        shapes = (
            jax.ShapeDtypeStruct((1, PLANES, ROWS, LANES), F32),
            jax.ShapeDtypeStruct((1, STATES), F32),
        )
        results = pl.pallas_call(
            functools.partial(kernel, slabs),
            out_shape=(
                jax.ShapeDtypeStruct((1, PLANES, ROWS, LANES), F32),
                jax.ShapeDtypeStruct((1, STATES), F32),
            ),
            in_specs=[pl.BlockSpec(memory_space=pltpu.HBM)] * 2,
            out_specs=(
                pl.BlockSpec(memory_space=pltpu.VMEM),
                pl.BlockSpec(memory_space=pltpu.VMEM),
            ),
            scratch_shapes=[
                vmem(PLANES + 4, ROWS, LANES),
                vmem(PLANES, ROWS, LANES),
                vmem(PLANES + 2, ROWS, LANES),
                vmem(PLANES, ROWS, LANES),
                vmem(2, ROWS, LANES),
                vmem(2, ROWS, LANES),
                vmem(PLANES, ROWS, LANES),
                vmem(6, LANES, LANES),
                vmem(8, 32, LANES),
                vmem(4, 32, LANES),
                vmem(4, 8, LANES),
                vmem(8, 8, LANES),
                vmem(3, 16, LANES),
                vmem(2 * REACH + 1, 8, LANES),
                vmem(3, 16, LANES),
                vmem(4, 32, LANES),
                vmem(6, ROWS, LANES),
                vmem(6, ROWS, LANES),
                vmem(PLANES, ROWS, LANES),
                vmem(PLANES, ROWS, LANES),
                vmem(2 * columns, 1, LANES),
                vmem(RING, 1, LANES),
                vmem(PLANES, ROWS, LANES, dtype=jnp.bfloat16),
                vmem(STATES, ROWS, LANES, dtype=jnp.bfloat16),
                vmem(LANES, LANES),
                vmem(2 * RING, 1, LANES),
                vmem(CHIPS * columns, 1, LANES),
                vmem(LANES, 2 * LANES),
                dma((2,)), dma(()), dma((3,)), dma((2,)), dma((2,)), dma((2,)),
                dma((2,)), dma((2,)), dma((2,)), dma((2,)), dma((2,)),
                pltpu.SemaphoreType.REGULAR((5,)),
            ],
            compiler_params=pltpu.CompilerParams(
                collective_id=0, has_side_effects=True, vmem_limit_bytes=32 * 1024 * 1024
            ),
        )(*[pltpu.with_memory_space_constraint(v, pltpu.HBM) for v in (orbitals, potential)])

        return pl.pallas_call(
            write_out,
            out_shape=shapes,
            in_specs=[pl.BlockSpec(memory_space=pltpu.VMEM)] * 2,
            out_specs=(pl.BlockSpec(memory_space=pltpu.HBM), pl.BlockSpec(memory_space=pltpu.HBM)),
            scratch_shapes=[dma((2,))],
            compiler_params=pltpu.CompilerParams(vmem_limit_bytes=1024 * 1024),
        )(*results)

    return jax.shard_map(
        on_device,
        mesh=mesh,
        in_specs=(P("state", "grid", None, None), P("grid", None, None)),
        out_specs=(P("state", "grid", None, None), P("state", None)),
        check_vma=False,
    )
```

```python
import functools

import jax
import jax.numpy as jnp
from jax import lax
from jax.experimental import pallas as pl
from jax.experimental.pallas import tpu as pltpu
from jax.sharding import PartitionSpec as P

MESH = pl.DeviceIdType.MESH
HIGH = lax.Precision.HIGHEST
F32 = jnp.float32

SHIFT_TERM = 0.25
DAMPING = 2.0 / 3.0
LANES = 128
ROWS = 64
HALF = ROWS // 2
PLANES = 8
STATES = 8
CHIPS = 4
RING = 16
REACH = 4
THIRD = 1.0 / 3.0
NEAR = -2.0 / 3.0
FAR = 1.0 / 24.0


def scales(level):
    inverse = 0.25**level
    diagonal = SHIFT_TERM + 3.0 * inverse
    scaled = DAMPING / diagonal
    return scaled, 0.5 * inverse * scaled


C0, K0 = scales(0)
C1, K1 = scales(1)
C2, K2 = scales(2)
C3, K3 = scales(3)


def iota(shape, dim):
    return lax.broadcasted_iota(jnp.int32, shape, dim)


def beside(plane, segment=LANES):
    rows = plane.shape[0]
    total = pltpu.roll(plane, 1, 0) + pltpu.roll(plane, rows - 1, 0)
    low, high = pltpu.roll(plane, 1, 1), pltpu.roll(plane, LANES - 1, 1)
    if segment != LANES:
        cell = iota(plane.shape, 1) & (segment - 1)
        low = jnp.where(cell == 0, pltpu.roll(plane, LANES - segment + 1, 1), low)
        high = jnp.where(cell == segment - 1, pltpu.roll(plane, segment - 1, 1), high)
    return total + (low + high)


def beside_two(plane):
    rows = plane.shape[0]
    total = pltpu.roll(plane, 2, 0) + pltpu.roll(plane, rows - 2, 0)
    return total + (pltpu.roll(plane, 2, 1) + pltpu.roll(plane, LANES - 2, 1))


def matrices():
    k, j = iota((LANES, LANES), 0), iota((LANES, LANES), 1)
    down_h = (j < 64) & ((k >> 1) == j)
    down_o = (j >= 64) & ((k >> 1) == j - 64)
    down_two = ((k >> 6) == ((j >> 5) & 1)) & (((k & 63) >> 1) == (j & 31))
    down_three = (k < 64) & ((k >> 5) == ((j >> 4) & 1)) & (((k & 31) >> 1) == (j & 15))
    up_two = (k < 32) & ((k >> 4) == ((j >> 5) & 1)) & ((k & 15) == ((j & 31) >> 1))
    up_one = (k < 64) & ((k >> 5) == (j >> 6)) & ((k & 31) == ((j & 63) >> 1))
    up_h = k == (j >> 1)
    up_o = k - 64 == (j >> 1)
    eighth, one = jnp.full((LANES, LANES), 0.125, F32), jnp.ones((LANES, LANES), F32)
    zero = jnp.zeros((LANES, LANES), F32)
    return [
        jnp.where(mask, eighth, zero) for mask in (down_h, down_o, down_two, down_three)
    ] + [jnp.where(mask, one, zero) for mask in (up_two, up_one, up_h, up_o)]


def times(left, right):
    return jnp.dot(left, right, precision=HIGH, preferred_element_type=F32)


def kernel(
    slabs,
    o_hbm, p_hbm, out_ref, gram_ref,
    o_buf, p_buf, h_buf, r_buf, g_out, g_in, pair_buf, mats,
    f1_buf, two_buf, f2_out, f2_in, three_buf, f3_in,
    up2_buf, up1_buf, uph_buf, upo_buf, a_buf, b_buf,
    e_y, e_z, rounded, mixed, rows_buf, g_z, g_xy, wide,
    load_sem, halo_send, halo_recv, f1_sem, f2_sem, f3_sem, ey_sem, ez_sem, x_sem, gz_sem, gx_sem,
    token,
):
    g, s = lax.axis_index("grid"), lax.axis_index("state")
    y, z = g >> 4, g & (RING - 1)
    x, core = s >> 1, s & 1
    columns = slabs // RING

    def slab(step):
        return ((g + step) & (slabs - 1), s)

    def on_ring(step):
        return (y * RING + ((z + step) & (RING - 1)), s)

    def on_column(step):
        return (((y + step) & (columns - 1)) * RING + z, s)

    hub = core == 1
    chip_states = (s - core, s - core + 1)

    def state_at(step, other):
        return 2 * ((x + step) & (CHIPS - 1)) + (1 - core if other else core)

    def on_face(step):
        up, side = step // STATES, step % STATES
        return (((y + up) & (columns - 1)) * RING + z, (s + side) & (STATES - 1))

    def each_core(zero, one):
        pl.when(core == 0)(zero)
        pl.when(core == 1)(one)

    def send(src, dst, sems, peer):
        copy = pltpu.make_async_remote_copy(
            src_ref=src, dst_ref=dst, send_sem=sems[0], recv_sem=sems[1],
            device_id=peer, device_id_type=MESH,
        )
        copy.start()

    def take(sem, view):
        pltpu.make_async_copy(view, view, sem).wait()

    def signal(sem, peers):
        for peer in peers:
            pl.semaphore_signal(sem, inc=1, device_id=peer, device_id_type=MESH)

    others = [(step, other) for step in (2, 1, -1) for other in (False, True)] + [(0, True)]
    next_two = [slab(1), slab(-1), on_ring(2), on_ring(-2)]
    partner = (g, state_at(0, True))
    next_two += [on_column(1), on_column(-1), (g, state_at(1, False)), (g, state_at(-1, False))]
    close = next_two + [on_ring(1), on_ring(-1), partner]
    barrier = pltpu.get_barrier_semaphore()
    signal(barrier, close)
    loads = [
        pltpu.make_async_copy(o_hbm.at[0], o_buf.at[pl.ds(2, PLANES)], load_sem.at[0]),
        pltpu.make_async_copy(p_hbm, p_buf, load_sem.at[1]),
    ]
    for load in loads:
        load.start()
    with jax.named_scope("w_load"):
        for load in loads:
            load.wait()
    with jax.named_scope("w_barrier"):
        pl.semaphore_wait(barrier, len(close))

    right, left = slab(1), slab(-1)

    def halo(part, mine, theirs):
        sems = (halo_send, halo_recv.at[part])
        send(o_buf.at[pl.ds(8, 2), pl.ds(mine, HALF)], o_buf.at[pl.ds(0, 2), pl.ds(mine, HALF)], sems, right)
        send(o_buf.at[pl.ds(2, 2), pl.ds(theirs, HALF)], o_buf.at[pl.ds(10, 2), pl.ds(theirs, HALF)], sems, left)

    signal(token.at[0], next_two)
    halo(0, 0, HALF)
    g_out[0] = p_buf[0] * o_buf[2] + FAR * o_buf[4]
    g_out[1] = p_buf[7] * o_buf[9] + FAR * o_buf[7]

    top = jnp.zeros((ROWS, LANES), F32)
    bottom = jnp.zeros((ROWS, LANES), F32)
    for p in range(PLANES):
        centre = o_buf[p + 2]
        first, second = beside(centre), beside_two(centre)
        for q in (p - 1, p + 1):
            if 0 <= q < PLANES:
                first += o_buf[q + 2]
        for q in (p - 2, p + 2):
            if 0 <= q < PLANES:
                second += o_buf[q + 2]
        value = (3.75 + p_buf[p]) * centre + NEAR * first + FAR * second
        h_buf[p + 1] = value
        r_buf[p] = centre * THIRD + K0 * first
        top += centre * value
        bottom += centre * centre
    halo(1, HALF, 0)
    sems = (halo_send, halo_recv.at[2])
    send(g_out.at[1], g_in.at[0], sems, right)
    send(g_out.at[0], g_in.at[1], sems, left)
    made = matrices()
    for index in range(6):
        mats[index] = made[index]
    wide[:, :LANES] = made[6]
    wide[:, LANES:] = made[7]
    rows_buf[...] = jnp.zeros_like(rows_buf)
    top, bottom = jnp.sum(top, 0, keepdims=True), jnp.sum(bottom, 0, keepdims=True)
    lane_row = iota((1, LANES), 1)

    with jax.named_scope("w_t1"):
        pl.semaphore_wait(token.at[0], len(next_two))
    signal(token.at[1], [on_ring(4), on_ring(-4)])
    signal(token.at[3], [partner])
    signal(token.at[2], [slab(2), slab(-2)])
    with jax.named_scope("w_halo_a"):
        take(halo_recv.at[0], o_buf.at[pl.ds(0, 2)])
    cross = o_buf[2, :HALF] * (2.0 * NEAR * o_buf[1, :HALF] + 2.0 * FAR * o_buf[0, :HALF])
    cross += 2.0 * FAR * o_buf[1, :HALF] * o_buf[3, :HALF]
    cross += o_buf[9, HALF:] * (2.0 * NEAR * o_buf[10, HALF:] + 2.0 * FAR * o_buf[11, HALF:])
    cross += 2.0 * FAR * o_buf[10, HALF:] * o_buf[8, HALF:]
    top += jnp.sum(cross, 0, keepdims=True)
    e_y[core * columns + y] = jnp.where(
        lane_row < 64, top + pltpu.roll(top, 64, 1), bottom + pltpu.roll(bottom, 64, 1)
    )
    pl.semaphore_wait(token.at[3], 1)

    def to_hubs(steps):
        mine = e_y.at[core * columns + y]
        for d in steps:
            send(mine, mine, (ey_sem.at[0], ey_sem.at[1]), (on_column(d)[0], chip_states[1]))

    each_core(lambda: to_hubs((2, 1, 3, 0)), lambda: to_hubs((2, 1, 3)))

    with jax.named_scope("w_halo_b"):
        take(halo_recv.at[1], o_buf.at[pl.ds(0, 2)])
        take(halo_recv.at[2], g_in)
    h_buf[1] += NEAR * o_buf[1] + FAR * o_buf[0]
    h_buf[2] += FAR * o_buf[1]
    h_buf[8] += NEAR * o_buf[10] + FAR * o_buf[11]
    h_buf[7] += FAR * o_buf[10]
    r_buf[0] += K0 * o_buf[1]
    r_buf[7] += K0 * o_buf[10]
    for ghost, at, inner, outer, side in ((1, 0, 2, 0, 0), (10, 9, 9, 11, 1)):
        centre = o_buf[ghost]
        first = (o_buf[inner] + o_buf[outer]) + beside(centre)
        second = o_buf[2 * inner - ghost] + beside_two(centre)
        h_buf[at] = 3.75 * centre + g_in[side] + NEAR * first + FAR * second
    for q in range(PLANES // 2):
        both = None
        for p in (2 * q, 2 * q + 1):
            value = h_buf[p + 1]
            rest = value * THIRD + K0 * ((h_buf[p] + h_buf[p + 2]) + beside(value))
            a_buf[p] = C0 * (value + rest)
            b_buf[p] = C0 * (o_buf[p + 2] + r_buf[p])
            both = rest if both is None else both + rest
        pair_buf[q] = both
        pair_buf[q + 4] = r_buf[2 * q] + r_buf[2 * q + 1]
    halved = pair_buf[:, pl.ds(0, 32, 2), :] + pair_buf[:, pl.ds(1, 32, 2), :]
    halved = [halved[:4].reshape(LANES, LANES), halved[4:].reshape(LANES, LANES)]
    f1 = times(jnp.concatenate(halved, 1), mats[0:2].reshape(2 * LANES, LANES))
    f1 = f1.reshape(4, 32, LANES)
    f1_buf[2:6] = f1
    sems = (f1_sem.at[0], f1_sem.at[1])
    send(f1_buf.at[pl.ds(4, 2)], f1_buf.at[pl.ds(0, 2)], sems, right)
    send(f1_buf.at[pl.ds(2, 2)], f1_buf.at[pl.ds(6, 2)], sems, left)

    rest = []
    for p in range(4):
        total = beside(f1[p], 64)
        for q in (p - 1, p + 1):
            if 0 <= q < 4:
                total += f1[q]
        rest.append(f1[p] * THIRD + K1 * total)
    two_buf[0] = K1 * f1[0]
    two_buf[1] = rest[0] + rest[1]
    two_buf[2] = rest[2] + rest[3]
    two_buf[3] = K1 * f1[3]
    halved = two_buf[:, pl.ds(0, 16, 2), :] + two_buf[:, pl.ds(1, 16, 2), :]
    share = times(halved.reshape(64, LANES), mats[2]).reshape(4, 16, LANES)
    low = iota((8, LANES), 1) < 64
    for k in range(4):
        f2_out[k] = jnp.where(low, share[k][:8], share[k][8:])
    a, b, c, d = share[0], share[1], share[2], share[3]
    three_buf[0] = a * (K2 + THIRD) + K2 * (b + beside(a, 32))
    three_buf[1] = (b + c) * (THIRD + K2) + K2 * ((a + d) + (beside(b, 32) + beside(c, 32)))
    three_buf[2] = d * (K2 + THIRD) + K2 * (c + beside(d, 32))
    halved = three_buf[:, pl.ds(0, 8, 2), :] + three_buf[:, pl.ds(1, 8, 2), :]
    parts = times(halved.reshape(24, LANES), mats[3]).reshape(3, 8, LANES)
    lane = iota((8, LANES), 1)
    f3_in[REACH] = jnp.where(
        lane < 32, parts[0],
        jnp.where(lane < 64, parts[1], jnp.where(lane < 96, parts[2], 0.0)),
    )
    with jax.named_scope("w_t2"):
        pl.semaphore_wait(token.at[2], 2)
    sems = (f3_sem.at[0], f3_sem.at[1])
    for step in range(REACH, 0, -1):
        send(f3_in.at[REACH], f3_in.at[REACH - step], sems, slab(step))
        send(f3_in.at[REACH], f3_in.at[REACH + step], sems, slab(-step))
    sems = (f2_sem.at[0], f2_sem.at[1])
    send(f2_out.at[pl.ds(1, 3)], f2_in.at[pl.ds(0, 3)], sems, right)
    send(f2_out.at[pl.ds(0, 3)], f2_in.at[pl.ds(3, 3)], sems, left)
    send(f2_out.at[3], f2_in.at[6], sems, slab(2))
    send(f2_out.at[0], f2_in.at[7], sems, slab(-2))

    with jax.named_scope("w_t3"):
        pl.semaphore_wait(token.at[1], 2)
    far_first = sorted(range(1, RING), key=lambda d: abs(d - RING // 2))

    @pl.when(core == 0)
    def _():
        signal(token.at[4], [partner])

    @pl.when(hub)
    def _():
        pl.semaphore_wait(token.at[4], 1)
        take(ey_sem.at[1], e_y.at[pl.ds(0, 2 * columns - 1)])
        first = jnp.sum(e_y[:columns], axis=0)
        second = jnp.sum(e_y[columns:], axis=0)
        first, second = first + pltpu.roll(first, 96, 1), second + pltpu.roll(second, 96, 1)
        e_z[z] = jnp.where(
            lane_row < 64,
            jnp.where(lane_row < 32, first, pltpu.roll(first, 96, 1)),
            jnp.where(lane_row < 96, pltpu.roll(second, 64, 1), pltpu.roll(second, 32, 1)),
        )
        for d in far_first:
            for state in chip_states:
                send(e_z.at[z], e_z.at[z], (ez_sem.at[0], ez_sem.at[1]), (on_ring(d)[0], state))
        send(e_z.at[z], e_z.at[z], (ez_sem.at[0], ez_sem.at[1]), partner)

    with jax.named_scope("w_f"):
        take(f3_sem.at[1], f3_in.at[pl.ds(0, 2 * REACH)])
        take(f2_sem.at[1], f2_in)
        take(f1_sem.at[1], f1_buf.at[pl.ds(0, 4)])

    source = {}
    for p in range(1 - REACH, REACH):
        at = p + REACH
        total = jnp.where(lane < 32, f3_in[at + 1], jnp.where(lane < 64, f3_in[at], f3_in[at - 1]))
        total = total + pltpu.roll(total, 32, 1)
        source[p] = total + pltpu.roll(total, 64, 1)
    iterate = {p: C3 * source[p] for p in source}
    for reach in (2, 1):
        iterate = {
            p: iterate[p] * THIRD + C3 * source[p]
            + K3 * ((iterate[p - 1] + iterate[p + 1]) + beside(iterate[p], 16))
            for p in range(-reach, reach + 1)
        }
    spread = times(jnp.concatenate([iterate[p] for p in range(-1, 2)], 0), mats[4]).reshape(3, 8, LANES)
    up2_buf[:, pl.ds(0, 8, 2), :] = spread
    up2_buf[:, pl.ds(1, 8, 2), :] = spread

    def unfold(tile):
        turned = pltpu.roll(tile, 64, 1)
        return jnp.concatenate([jnp.where(low, tile, turned), jnp.where(low, turned, tile)], 0)

    f2 = {
        -2: unfold(f2_in[0] + f2_in[6]),
        -1: share[0] + unfold(f2_in[1]),
        0: share[1] + unfold(f2_in[2]),
        1: share[2] + unfold(f2_in[3]),
        2: share[3] + unfold(f2_in[4]),
        3: unfold(f2_in[5] + f2_in[7]),
    }
    fixed = {p: C2 * f2[p] + up2_buf[(p >> 1) + 1] for p in range(-2, 4)}
    value = [
        fixed[p] * THIRD + C2 * f2[p] + K2 * ((fixed[p - 1] + fixed[p + 1]) + beside(fixed[p], 32))
        for p in range(-1, 3)
    ]
    spread = times(jnp.concatenate(value, 0), mats[5]).reshape(4, 16, LANES)
    up1_buf[:, pl.ds(0, 16, 2), :] = spread
    up1_buf[:, pl.ds(1, 16, 2), :] = spread
    fixed = {p: C1 * f1_buf[p + 2] + up1_buf[(p >> 1) + 1] for p in range(-2, 6)}
    error = jnp.concatenate(
        [
            fixed[p] * THIRD + C1 * f1_buf[p + 2]
            + K1 * ((fixed[p - 1] + fixed[p + 1]) + beside(fixed[p], 64))
            for p in range(-1, 5)
        ],
        0,
    )

    spread = times(error, wide[...])
    for at, up_buf, last in ((0, uph_buf, a_buf), (LANES, upo_buf, b_buf)):
        part = spread[:, at : at + LANES].reshape(6, 32, LANES)
        up_buf[:, pl.ds(0, 32, 2), :] = part
        up_buf[:, pl.ds(1, 32, 2), :] = part
        for q in range(1, 5):
            value = up_buf[q]
            same = value * (THIRD + K0) + K0 * beside(value)
            last[2 * q - 2] += same + K0 * up_buf[q - 1]
            last[2 * q - 1] += same + K0 * up_buf[q + 1]
    each_core(
        lambda: take(ez_sem.at[1], e_z.at[pl.ds(0, RING)]),
        lambda: take(ez_sem.at[1], e_z.at[pl.ds(0, RING - 1)]),
    )
    with jax.named_scope("w_ez"):
        sums = jnp.sum(e_z[...], axis=0)
    part = lane_row >> 5
    numer = jnp.sum(jnp.where(part == 2 * core, sums, 0.0), axis=1, keepdims=True)
    denom = jnp.sum(jnp.where(part == 2 * core + 1, sums, 0.0), axis=1, keepdims=True)
    energy = numer / denom

    def finish(p):
        value = a_buf[p] - energy * b_buf[p]
        out_ref[0, p] = value
        return value.astype(jnp.bfloat16)

    def to_hub(step):
        chip = (x + step) & (CHIPS - 1)
        for plane in (0, 1):
            rounded[2 * chip + plane] = finish(2 * chip + plane)
        send(
            rounded.at[pl.ds(2 * chip, 2)], mixed.at[s], (x_sem.at[0], x_sem.at[1]), (g, 2 * chip + 1)
        )

    for step in (2, 1, -1):
        to_hub(step)

    @pl.when(core == 0)
    def _():
        to_hub(0)

    @pl.when(hub)
    def _():
        for plane in (0, 1):
            mixed[s, plane] = finish(2 * x + plane)
        take(x_sem.at[1], mixed.at[pl.ds(0, STATES - 1)])
        pairs = [(i, j) for i in range(STATES) for j in range(i, STATES)]
        held = {pair: None for pair in pairs}
        for at in range(2 * ROWS // 16):
            rows = slice(16 * at % ROWS, 16 * at % ROWS + 16)
            values = [mixed[i, 16 * at // ROWS, rows].astype(F32) for i in range(STATES)]
            for i, j in pairs:
                product = values[i] * values[j]
                product = product[:8] + product[8:]
                held[i, j] = product if held[i, j] is None else held[i, j] + product
        for i, j in pairs:
            row = jnp.sum(held[i, j], 0, keepdims=True)
            rows_buf[8 * i + j : 8 * i + j + 1] = row
            if i != j:
                rows_buf[8 * j + i : 8 * j + i + 1] = row
        flat = lax.dot_general(
            jnp.ones((8, LANES), F32), rows_buf[...], (((1,), (1,)), ((), ())),
            precision=HIGH, preferred_element_type=F32,
        )
        g_z[z] = flat[:1]
        for d in far_first:
            send(g_z.at[z], g_z.at[z], (gz_sem.at[0], gz_sem.at[1]), on_ring(d))
        take(gz_sem.at[1], g_z.at[pl.ds(0, RING - 1)])
        place = y * CHIPS + x
        g_xy[place] = jnp.sum(g_z[:RING], axis=0)
        order = {d: abs(d // STATES - 2) + abs(d % STATES - 4) / 2 - d % 2 for d in range(1, STATES * columns)}
        for d in sorted(order, key=order.get):
            send(g_xy.at[place], g_xy.at[place], (gx_sem.at[0], gx_sem.at[1]), on_face(d))

    with jax.named_scope("w_sends"):
        take(halo_send, o_buf.at[pl.ds(0, 6)])
        take(f1_sem.at[0], f1_buf.at[pl.ds(0, 4)])
        take(f2_sem.at[0], f2_in)
        take(f3_sem.at[0], f3_in.at[pl.ds(0, 2 * REACH)])

    @pl.when(core == 0)
    def _():
        take(ey_sem.at[0], g_z.at[pl.ds(0, columns)])
        take(x_sem.at[0], mixed.at[pl.ds(0, CHIPS)])
        take(gx_sem.at[1], g_xy)

    @pl.when(hub)
    def _():
        take(ey_sem.at[0], g_z.at[pl.ds(0, columns - 1)])
        take(ez_sem.at[0], g_z.at[pl.ds(0, 2 * RING - 1)])
        take(x_sem.at[0], mixed.at[pl.ds(0, CHIPS - 1)])
        take(gz_sem.at[0], g_z.at[pl.ds(0, RING - 1)])
        take(gx_sem.at[1], g_xy.at[pl.ds(0, CHIPS * columns - 1)])

    total = jnp.sum(g_xy[...], axis=0)
    picked = jnp.zeros((1, STATES), F32)
    for t in range(STATES):
        picked += jnp.where(s == t, total[:, STATES * t : STATES * t + STATES], 0.0)
    gram_ref[...] = picked / F32(PLANES * ROWS * LANES * slabs)
    pl.when(hub)(lambda: take(gx_sem.at[0], g_z.at[pl.ds(0, STATES * columns - 1)]))


def solution(mesh):
    slabs = mesh.shape["grid"]
    columns = slabs // RING
    dma = pltpu.SemaphoreType.DMA

    def vmem(*shape, dtype=F32):
        return pltpu.VMEM(shape, dtype)

    def write_out(values, gram, values_hbm, gram_hbm, sem):
        copies = [
            pltpu.make_async_copy(values, values_hbm, sem.at[0]),
            pltpu.make_async_copy(gram, gram_hbm, sem.at[1]),
        ]
        for copy in copies:
            copy.start()
        for copy in copies:
            copy.wait()

    def on_device(orbitals, potential):
        shapes = (
            jax.ShapeDtypeStruct((1, PLANES, ROWS, LANES), F32),
            jax.ShapeDtypeStruct((1, STATES), F32),
        )
        results = pl.pallas_call(
            functools.partial(kernel, slabs),
            out_shape=(
                jax.ShapeDtypeStruct((1, PLANES, ROWS, LANES), F32),
                jax.ShapeDtypeStruct((1, STATES), F32),
            ),
            in_specs=[pl.BlockSpec(memory_space=pltpu.HBM)] * 2,
            out_specs=(
                pl.BlockSpec(memory_space=pltpu.VMEM),
                pl.BlockSpec(memory_space=pltpu.VMEM),
            ),
            scratch_shapes=[
                vmem(PLANES + 4, ROWS, LANES),
                vmem(PLANES, ROWS, LANES),
                vmem(PLANES + 2, ROWS, LANES),
                vmem(PLANES, ROWS, LANES),
                vmem(2, ROWS, LANES),
                vmem(2, ROWS, LANES),
                vmem(PLANES, ROWS, LANES),
                vmem(6, LANES, LANES),
                vmem(8, 32, LANES),
                vmem(4, 32, LANES),
                vmem(4, 8, LANES),
                vmem(8, 8, LANES),
                vmem(3, 16, LANES),
                vmem(2 * REACH + 1, 8, LANES),
                vmem(3, 16, LANES),
                vmem(4, 32, LANES),
                vmem(6, ROWS, LANES),
                vmem(6, ROWS, LANES),
                vmem(PLANES, ROWS, LANES),
                vmem(PLANES, ROWS, LANES),
                vmem(2 * columns, 1, LANES),
                vmem(RING, 1, LANES),
                vmem(PLANES, ROWS, LANES, dtype=jnp.bfloat16),
                vmem(STATES, 2, ROWS, LANES, dtype=jnp.bfloat16),
                vmem(LANES, LANES),
                vmem(2 * RING, 1, LANES),
                vmem(CHIPS * columns, 1, LANES),
                vmem(LANES, 2 * LANES),
                dma((2,)), dma(()), dma((3,)), dma((2,)), dma((2,)), dma((2,)),
                dma((2,)), dma((2,)), dma((2,)), dma((2,)), dma((2,)),
                pltpu.SemaphoreType.REGULAR((5,)),
            ],
            compiler_params=pltpu.CompilerParams(
                collective_id=0, has_side_effects=True, vmem_limit_bytes=32 * 1024 * 1024
            ),
        )(*[pltpu.with_memory_space_constraint(v, pltpu.HBM) for v in (orbitals, potential)])

        return pl.pallas_call(
            write_out,
            out_shape=shapes,
            in_specs=[pl.BlockSpec(memory_space=pltpu.VMEM)] * 2,
            out_specs=(pl.BlockSpec(memory_space=pltpu.HBM), pl.BlockSpec(memory_space=pltpu.HBM)),
            scratch_shapes=[dma((2,))],
            compiler_params=pltpu.CompilerParams(vmem_limit_bytes=1024 * 1024),
        )(*results)

    return jax.shard_map(
        on_device,
        mesh=mesh,
        in_specs=(P("state", "grid", None, None), P("grid", None, None)),
        out_specs=(P("state", "grid", None, None), P("state", None)),
        check_vma=False,
    )
```

```python
import functools

import jax
import jax.numpy as jnp
from jax import lax
from jax.experimental import pallas as pl
from jax.experimental.pallas import tpu as pltpu
from jax.sharding import PartitionSpec as P

MESH = pl.DeviceIdType.MESH
HIGH = lax.Precision.HIGHEST
F32 = jnp.float32

SHIFT_TERM = 0.25
DAMPING = 2.0 / 3.0
LANES = 128
ROWS = 64
HALF = ROWS // 2
PLANES = 8
STATES = 8
CHIPS = 4
RING = 16
REACH = 4
THIRD = 1.0 / 3.0
NEAR = -2.0 / 3.0
FAR = 1.0 / 24.0


def scales(level):
    inverse = 0.25**level
    diagonal = SHIFT_TERM + 3.0 * inverse
    scaled = DAMPING / diagonal
    return scaled, 0.5 * inverse * scaled


C0, K0 = scales(0)
C1, K1 = scales(1)
C2, K2 = scales(2)
C3, K3 = scales(3)


def iota(shape, dim):
    return lax.broadcasted_iota(jnp.int32, shape, dim)


def beside(plane, segment=LANES):
    rows = plane.shape[0]
    total = pltpu.roll(plane, 1, 0) + pltpu.roll(plane, rows - 1, 0)
    low, high = pltpu.roll(plane, 1, 1), pltpu.roll(plane, LANES - 1, 1)
    if segment != LANES:
        cell = iota(plane.shape, 1) & (segment - 1)
        low = jnp.where(cell == 0, pltpu.roll(plane, LANES - segment + 1, 1), low)
        high = jnp.where(cell == segment - 1, pltpu.roll(plane, segment - 1, 1), high)
    return total + (low + high)


def beside_two(plane):
    rows = plane.shape[0]
    total = pltpu.roll(plane, 2, 0) + pltpu.roll(plane, rows - 2, 0)
    return total + (pltpu.roll(plane, 2, 1) + pltpu.roll(plane, LANES - 2, 1))


def matrices():
    k, j = iota((LANES, LANES), 0), iota((LANES, LANES), 1)
    down_h = (j < 64) & ((k >> 1) == j)
    down_o = (j >= 64) & ((k >> 1) == j - 64)
    down_two = ((k >> 6) == ((j >> 5) & 1)) & (((k & 63) >> 1) == (j & 31))
    down_three = (k < 64) & ((k >> 5) == ((j >> 4) & 1)) & (((k & 31) >> 1) == (j & 15))
    up_two = (k < 32) & ((k >> 4) == ((j >> 5) & 1)) & ((k & 15) == ((j & 31) >> 1))
    up_one = (k < 64) & ((k >> 5) == (j >> 6)) & ((k & 31) == ((j & 63) >> 1))
    up_h = k == (j >> 1)
    up_o = k - 64 == (j >> 1)
    eighth, one = jnp.full((LANES, LANES), 0.125, F32), jnp.ones((LANES, LANES), F32)
    zero = jnp.zeros((LANES, LANES), F32)
    return [
        jnp.where(mask, eighth, zero) for mask in (down_h, down_o, down_two, down_three)
    ] + [jnp.where(mask, one, zero) for mask in (up_two, up_one, up_h, up_o)]


def times(left, right):
    return jnp.dot(left, right, precision=HIGH, preferred_element_type=F32)


def kernel(
    slabs,
    o_hbm, p_hbm, out_ref, gram_ref,
    o_buf, p_buf, h_buf, r_buf, g_out, g_in, pair_buf, mats,
    f1_buf, two_buf, f2_out, f2_in, three_buf, f3_in,
    up2_buf, up1_buf, uph_buf, upo_buf, a_buf, b_buf,
    e_y, e_z, rounded, mixed, rows_buf, g_z, g_xy, wide,
    load_sem, halo_send, halo_recv, f1_sem, f2_sem, f3_sem, ey_sem, ez_sem, x_sem, gz_sem, gx_sem,
    token,
):
    g, s = lax.axis_index("grid"), lax.axis_index("state")
    y, z = g >> 4, g & (RING - 1)
    x, core = s >> 1, s & 1
    columns = slabs // RING

    def slab(step):
        return ((g + step) & (slabs - 1), s)

    def on_ring(step):
        return (y * RING + ((z + step) & (RING - 1)), s)

    def on_column(step):
        return (((y + step) & (columns - 1)) * RING + z, s)

    hub = core == 1
    chip_states = (s - core, s - core + 1)

    def state_at(step, other):
        return 2 * ((x + step) & (CHIPS - 1)) + (1 - core if other else core)

    def on_face(step):
        up, side = step // STATES, step % STATES
        return (((y + up) & (columns - 1)) * RING + z, (s + side) & (STATES - 1))

    def each_core(zero, one):
        pl.when(core == 0)(zero)
        pl.when(core == 1)(one)

    def send(src, dst, sems, peer):
        copy = pltpu.make_async_remote_copy(
            src_ref=src, dst_ref=dst, send_sem=sems[0], recv_sem=sems[1],
            device_id=peer, device_id_type=MESH,
        )
        copy.start()

    def take(sem, view):
        pltpu.make_async_copy(view, view, sem).wait()

    def signal(sem, peers):
        for peer in peers:
            pl.semaphore_signal(sem, inc=1, device_id=peer, device_id_type=MESH)

    others = [(step, other) for step in (2, 1, -1) for other in (False, True)] + [(0, True)]
    next_two = [slab(1), slab(-1), on_ring(2), on_ring(-2)]
    partner = (g, state_at(0, True))
    next_two += [on_column(1), on_column(-1), (g, state_at(1, False)), (g, state_at(-1, False))]
    close = next_two + [on_ring(1), on_ring(-1), partner]
    barrier = pltpu.get_barrier_semaphore()
    signal(barrier, close)
    loads = [
        pltpu.make_async_copy(o_hbm.at[0], o_buf.at[pl.ds(2, PLANES)], load_sem.at[0]),
        pltpu.make_async_copy(p_hbm, p_buf, load_sem.at[1]),
    ]
    for load in loads:
        load.start()
    made = matrices()
    for index in range(6):
        mats[index] = made[index]
    wide[:, :LANES] = made[6]
    wide[:, LANES:] = made[7]
    rows_buf[...] = jnp.zeros_like(rows_buf)
    with jax.named_scope("w_load"):
        for load in loads:
            load.wait()
    with jax.named_scope("w_barrier"):
        pl.semaphore_wait(barrier, len(close))

    right, left = slab(1), slab(-1)

    def halo(part, mine, theirs):
        sems = (halo_send, halo_recv.at[part])
        send(o_buf.at[pl.ds(8, 2), pl.ds(mine, HALF)], o_buf.at[pl.ds(0, 2), pl.ds(mine, HALF)], sems, right)
        send(o_buf.at[pl.ds(2, 2), pl.ds(theirs, HALF)], o_buf.at[pl.ds(10, 2), pl.ds(theirs, HALF)], sems, left)

    signal(token.at[0], next_two)
    halo(0, 0, HALF)
    g_out[0] = p_buf[0] * o_buf[2] + FAR * o_buf[4]
    g_out[1] = p_buf[7] * o_buf[9] + FAR * o_buf[7]

    top = jnp.zeros((ROWS, LANES), F32)
    bottom = jnp.zeros((ROWS, LANES), F32)
    for p in range(PLANES):
        centre = o_buf[p + 2]
        first, second = beside(centre), beside_two(centre)
        for q in (p - 1, p + 1):
            if 0 <= q < PLANES:
                first += o_buf[q + 2]
        for q in (p - 2, p + 2):
            if 0 <= q < PLANES:
                second += o_buf[q + 2]
        value = (3.75 + p_buf[p]) * centre + NEAR * first + FAR * second
        h_buf[p + 1] = value
        r_buf[p] = centre * THIRD + K0 * first
        top += centre * value
        bottom += centre * centre
    halo(1, HALF, 0)
    sems = (halo_send, halo_recv.at[2])
    send(g_out.at[1], g_in.at[0], sems, right)
    send(g_out.at[0], g_in.at[1], sems, left)
    top, bottom = jnp.sum(top, 0, keepdims=True), jnp.sum(bottom, 0, keepdims=True)
    lane_row = iota((1, LANES), 1)

    with jax.named_scope("w_t1"):
        pl.semaphore_wait(token.at[0], len(next_two))
    signal(token.at[1], [on_ring(4), on_ring(-4)])
    signal(token.at[3], [partner])
    signal(token.at[2], [slab(2), slab(-2)])
    with jax.named_scope("w_halo_a"):
        take(halo_recv.at[0], o_buf.at[pl.ds(0, 2)])
    cross = o_buf[2, :HALF] * (2.0 * NEAR * o_buf[1, :HALF] + 2.0 * FAR * o_buf[0, :HALF])
    cross += 2.0 * FAR * o_buf[1, :HALF] * o_buf[3, :HALF]
    cross += o_buf[9, HALF:] * (2.0 * NEAR * o_buf[10, HALF:] + 2.0 * FAR * o_buf[11, HALF:])
    cross += 2.0 * FAR * o_buf[10, HALF:] * o_buf[8, HALF:]
    top += jnp.sum(cross, 0, keepdims=True)
    e_y[core * columns + y] = jnp.where(
        lane_row < 64, top + pltpu.roll(top, 64, 1), bottom + pltpu.roll(bottom, 64, 1)
    )
    pl.semaphore_wait(token.at[3], 1)

    def to_hubs(steps):
        mine = e_y.at[core * columns + y]
        for d in steps:
            send(mine, mine, (ey_sem.at[0], ey_sem.at[1]), (on_column(d)[0], chip_states[1]))

    each_core(lambda: to_hubs((2, 1, 3, 0)), lambda: to_hubs((2, 1, 3)))

    with jax.named_scope("w_halo_b"):
        take(halo_recv.at[1], o_buf.at[pl.ds(0, 2)])
        take(halo_recv.at[2], g_in)
    h_buf[1] += NEAR * o_buf[1] + FAR * o_buf[0]
    h_buf[2] += FAR * o_buf[1]
    h_buf[8] += NEAR * o_buf[10] + FAR * o_buf[11]
    h_buf[7] += FAR * o_buf[10]
    r_buf[0] += K0 * o_buf[1]
    r_buf[7] += K0 * o_buf[10]
    for ghost, at, inner, outer, side in ((1, 0, 2, 0, 0), (10, 9, 9, 11, 1)):
        centre = o_buf[ghost]
        first = (o_buf[inner] + o_buf[outer]) + beside(centre)
        second = o_buf[2 * inner - ghost] + beside_two(centre)
        h_buf[at] = 3.75 * centre + g_in[side] + NEAR * first + FAR * second
    for q in range(PLANES // 2):
        both = None
        for p in (2 * q, 2 * q + 1):
            value = h_buf[p + 1]
            rest = value * THIRD + K0 * ((h_buf[p] + h_buf[p + 2]) + beside(value))
            a_buf[p] = C0 * (value + rest)
            b_buf[p] = C0 * (o_buf[p + 2] + r_buf[p])
            both = rest if both is None else both + rest
        pair_buf[q] = both
        pair_buf[q + 4] = r_buf[2 * q] + r_buf[2 * q + 1]
    halved = pair_buf[:, pl.ds(0, 32, 2), :] + pair_buf[:, pl.ds(1, 32, 2), :]
    halved = [halved[:4].reshape(LANES, LANES), halved[4:].reshape(LANES, LANES)]
    f1 = times(jnp.concatenate(halved, 1), mats[0:2].reshape(2 * LANES, LANES))
    f1 = f1.reshape(4, 32, LANES)
    f1_buf[2:6] = f1
    sems = (f1_sem.at[0], f1_sem.at[1])
    send(f1_buf.at[pl.ds(4, 2)], f1_buf.at[pl.ds(0, 2)], sems, right)
    send(f1_buf.at[pl.ds(2, 2)], f1_buf.at[pl.ds(6, 2)], sems, left)

    rest = []
    for p in range(4):
        total = beside(f1[p], 64)
        for q in (p - 1, p + 1):
            if 0 <= q < 4:
                total += f1[q]
        rest.append(f1[p] * THIRD + K1 * total)
    two_buf[0] = K1 * f1[0]
    two_buf[1] = rest[0] + rest[1]
    two_buf[2] = rest[2] + rest[3]
    two_buf[3] = K1 * f1[3]
    halved = two_buf[:, pl.ds(0, 16, 2), :] + two_buf[:, pl.ds(1, 16, 2), :]
    share = times(halved.reshape(64, LANES), mats[2]).reshape(4, 16, LANES)
    low = iota((8, LANES), 1) < 64
    for k in range(4):
        f2_out[k] = jnp.where(low, share[k][:8], share[k][8:])
    a, b, c, d = share[0], share[1], share[2], share[3]
    three_buf[0] = a * (K2 + THIRD) + K2 * (b + beside(a, 32))
    three_buf[1] = (b + c) * (THIRD + K2) + K2 * ((a + d) + (beside(b, 32) + beside(c, 32)))
    three_buf[2] = d * (K2 + THIRD) + K2 * (c + beside(d, 32))
    halved = three_buf[:, pl.ds(0, 8, 2), :] + three_buf[:, pl.ds(1, 8, 2), :]
    parts = times(halved.reshape(24, LANES), mats[3]).reshape(3, 8, LANES)
    lane = iota((8, LANES), 1)
    f3_in[REACH] = jnp.where(
        lane < 32, parts[0],
        jnp.where(lane < 64, parts[1], jnp.where(lane < 96, parts[2], 0.0)),
    )
    with jax.named_scope("w_t2"):
        pl.semaphore_wait(token.at[2], 2)
    sems = (f3_sem.at[0], f3_sem.at[1])
    for step in range(REACH, 0, -1):
        send(f3_in.at[REACH], f3_in.at[REACH - step], sems, slab(step))
        send(f3_in.at[REACH], f3_in.at[REACH + step], sems, slab(-step))
    sems = (f2_sem.at[0], f2_sem.at[1])
    send(f2_out.at[pl.ds(1, 3)], f2_in.at[pl.ds(0, 3)], sems, right)
    send(f2_out.at[pl.ds(0, 3)], f2_in.at[pl.ds(3, 3)], sems, left)
    send(f2_out.at[3], f2_in.at[6], sems, slab(2))
    send(f2_out.at[0], f2_in.at[7], sems, slab(-2))

    with jax.named_scope("w_t3"):
        pl.semaphore_wait(token.at[1], 2)
    far_first = sorted(range(1, RING), key=lambda d: abs(d - RING // 2))

    @pl.when(core == 0)
    def _():
        signal(token.at[4], [partner])

    @pl.when(hub)
    def _():
        pl.semaphore_wait(token.at[4], 1)
        take(ey_sem.at[1], e_y.at[pl.ds(0, 2 * columns - 1)])
        first = jnp.sum(e_y[:columns], axis=0)
        second = jnp.sum(e_y[columns:], axis=0)
        first, second = first + pltpu.roll(first, 96, 1), second + pltpu.roll(second, 96, 1)
        e_z[z] = jnp.where(
            lane_row < 64,
            jnp.where(lane_row < 32, first, pltpu.roll(first, 96, 1)),
            jnp.where(lane_row < 96, pltpu.roll(second, 64, 1), pltpu.roll(second, 32, 1)),
        )
        for d in far_first:
            for state in chip_states:
                send(e_z.at[z], e_z.at[z], (ez_sem.at[0], ez_sem.at[1]), (on_ring(d)[0], state))
        send(e_z.at[z], e_z.at[z], (ez_sem.at[0], ez_sem.at[1]), partner)

    with jax.named_scope("w_f"):
        take(f3_sem.at[1], f3_in.at[pl.ds(0, 2 * REACH)])
        take(f2_sem.at[1], f2_in)
        take(f1_sem.at[1], f1_buf.at[pl.ds(0, 4)])

    source = {}
    for p in range(1 - REACH, REACH):
        at = p + REACH
        total = jnp.where(lane < 32, f3_in[at + 1], jnp.where(lane < 64, f3_in[at], f3_in[at - 1]))
        total = total + pltpu.roll(total, 32, 1)
        source[p] = total + pltpu.roll(total, 64, 1)
    iterate = {p: C3 * source[p] for p in source}
    for reach in (2, 1):
        iterate = {
            p: iterate[p] * THIRD + C3 * source[p]
            + K3 * ((iterate[p - 1] + iterate[p + 1]) + beside(iterate[p], 16))
            for p in range(-reach, reach + 1)
        }
    spread = times(jnp.concatenate([iterate[p] for p in range(-1, 2)], 0), mats[4]).reshape(3, 8, LANES)
    up2_buf[:, pl.ds(0, 8, 2), :] = spread
    up2_buf[:, pl.ds(1, 8, 2), :] = spread

    def unfold(tile):
        turned = pltpu.roll(tile, 64, 1)
        return jnp.concatenate([jnp.where(low, tile, turned), jnp.where(low, turned, tile)], 0)

    f2 = {
        -2: unfold(f2_in[0] + f2_in[6]),
        -1: share[0] + unfold(f2_in[1]),
        0: share[1] + unfold(f2_in[2]),
        1: share[2] + unfold(f2_in[3]),
        2: share[3] + unfold(f2_in[4]),
        3: unfold(f2_in[5] + f2_in[7]),
    }
    fixed = {p: C2 * f2[p] + up2_buf[(p >> 1) + 1] for p in range(-2, 4)}
    value = [
        fixed[p] * THIRD + C2 * f2[p] + K2 * ((fixed[p - 1] + fixed[p + 1]) + beside(fixed[p], 32))
        for p in range(-1, 3)
    ]
    spread = times(jnp.concatenate(value, 0), mats[5]).reshape(4, 16, LANES)
    up1_buf[:, pl.ds(0, 16, 2), :] = spread
    up1_buf[:, pl.ds(1, 16, 2), :] = spread
    fixed = {p: C1 * f1_buf[p + 2] + up1_buf[(p >> 1) + 1] for p in range(-2, 6)}
    error = jnp.concatenate(
        [
            fixed[p] * THIRD + C1 * f1_buf[p + 2]
            + K1 * ((fixed[p - 1] + fixed[p + 1]) + beside(fixed[p], 64))
            for p in range(-1, 5)
        ],
        0,
    )

    spread = times(error, wide[...])
    for at, up_buf, last in ((0, uph_buf, a_buf), (LANES, upo_buf, b_buf)):
        part = spread[:, at : at + LANES].reshape(6, 32, LANES)
        up_buf[:, pl.ds(0, 32, 2), :] = part
        up_buf[:, pl.ds(1, 32, 2), :] = part
        for q in range(1, 5):
            value = up_buf[q]
            same = value * (THIRD + K0) + K0 * beside(value)
            last[2 * q - 2] += same + K0 * up_buf[q - 1]
            last[2 * q - 1] += same + K0 * up_buf[q + 1]
    each_core(
        lambda: take(ez_sem.at[1], e_z.at[pl.ds(0, RING)]),
        lambda: take(ez_sem.at[1], e_z.at[pl.ds(0, RING - 1)]),
    )
    with jax.named_scope("w_ez"):
        sums = jnp.sum(e_z[...], axis=0)
    part = lane_row >> 5
    numer = jnp.sum(jnp.where(part == 2 * core, sums, 0.0), axis=1, keepdims=True)
    denom = jnp.sum(jnp.where(part == 2 * core + 1, sums, 0.0), axis=1, keepdims=True)
    energy = numer / denom

    def finish(p):
        value = a_buf[p] - energy * b_buf[p]
        out_ref[0, p] = value
        return value.astype(jnp.bfloat16)

    def to_hub(step):
        chip = (x + step) & (CHIPS - 1)
        for plane in (0, 1):
            rounded[2 * chip + plane] = finish(2 * chip + plane)
        send(
            rounded.at[pl.ds(2 * chip, 2)], mixed.at[s], (x_sem.at[0], x_sem.at[1]), (g, 2 * chip + 1)
        )

    for step in (2, 1, -1):
        to_hub(step)

    @pl.when(core == 0)
    def _():
        to_hub(0)

    @pl.when(hub)
    def _():
        for plane in (0, 1):
            mixed[s, plane] = finish(2 * x + plane)
        take(x_sem.at[1], mixed.at[pl.ds(0, STATES - 1)])
        pairs = [(i, j) for i in range(STATES) for j in range(i, STATES)]
        held = {pair: None for pair in pairs}
        for at in range(2 * ROWS // 16):
            rows = slice(16 * at % ROWS, 16 * at % ROWS + 16)
            values = [mixed[i, 16 * at // ROWS, rows].astype(F32) for i in range(STATES)]
            for i, j in pairs:
                product = values[i] * values[j]
                product = product[:8] + product[8:]
                held[i, j] = product if held[i, j] is None else held[i, j] + product
        for i, j in pairs:
            row = jnp.sum(held[i, j], 0, keepdims=True)
            rows_buf[8 * i + j : 8 * i + j + 1] = row
            if i != j:
                rows_buf[8 * j + i : 8 * j + i + 1] = row
        flat = lax.dot_general(
            jnp.ones((8, LANES), F32), rows_buf[...], (((1,), (1,)), ((), ())),
            precision=HIGH, preferred_element_type=F32,
        )
        g_z[z] = flat[:1]
        for d in far_first:
            send(g_z.at[z], g_z.at[z], (gz_sem.at[0], gz_sem.at[1]), on_ring(d))
        take(gz_sem.at[1], g_z.at[pl.ds(0, RING - 1)])
        place = y * CHIPS + x
        g_xy[place] = jnp.sum(g_z[:RING], axis=0)
        order = {d: abs(d // STATES - 2) + abs(d % STATES - 4) / 2 - d % 2 for d in range(1, STATES * columns)}
        for d in sorted(order, key=order.get):
            send(g_xy.at[place], g_xy.at[place], (gx_sem.at[0], gx_sem.at[1]), on_face(d))

    with jax.named_scope("w_sends"):
        take(halo_send, o_buf.at[pl.ds(0, 6)])
        take(f1_sem.at[0], f1_buf.at[pl.ds(0, 4)])
        take(f2_sem.at[0], f2_in)
        take(f3_sem.at[0], f3_in.at[pl.ds(0, 2 * REACH)])

    @pl.when(core == 0)
    def _():
        take(ey_sem.at[0], g_z.at[pl.ds(0, columns)])
        take(x_sem.at[0], mixed.at[pl.ds(0, CHIPS)])
        take(gx_sem.at[1], g_xy)

    @pl.when(hub)
    def _():
        take(ey_sem.at[0], g_z.at[pl.ds(0, columns - 1)])
        take(ez_sem.at[0], g_z.at[pl.ds(0, 2 * RING - 1)])
        take(x_sem.at[0], mixed.at[pl.ds(0, CHIPS - 1)])
        take(gz_sem.at[0], g_z.at[pl.ds(0, RING - 1)])
        take(gx_sem.at[1], g_xy.at[pl.ds(0, CHIPS * columns - 1)])

    total = jnp.sum(g_xy[...], axis=0)
    picked = jnp.zeros((1, STATES), F32)
    for t in range(STATES):
        picked += jnp.where(s == t, total[:, STATES * t : STATES * t + STATES], 0.0)
    gram_ref[...] = picked / F32(PLANES * ROWS * LANES * slabs)
    pl.when(hub)(lambda: take(gx_sem.at[0], g_z.at[pl.ds(0, STATES * columns - 1)]))


def solution(mesh):
    slabs = mesh.shape["grid"]
    columns = slabs // RING
    dma = pltpu.SemaphoreType.DMA

    def vmem(*shape, dtype=F32):
        return pltpu.VMEM(shape, dtype)

    def write_out(values, gram, values_hbm, gram_hbm, sem):
        copies = [
            pltpu.make_async_copy(values, values_hbm, sem.at[0]),
            pltpu.make_async_copy(gram, gram_hbm, sem.at[1]),
        ]
        for copy in copies:
            copy.start()
        for copy in copies:
            copy.wait()

    def on_device(orbitals, potential):
        shapes = (
            jax.ShapeDtypeStruct((1, PLANES, ROWS, LANES), F32),
            jax.ShapeDtypeStruct((1, STATES), F32),
        )
        results = pl.pallas_call(
            functools.partial(kernel, slabs),
            out_shape=(
                jax.ShapeDtypeStruct((1, PLANES, ROWS, LANES), F32),
                jax.ShapeDtypeStruct((1, STATES), F32),
            ),
            in_specs=[pl.BlockSpec(memory_space=pltpu.HBM)] * 2,
            out_specs=(
                pl.BlockSpec(memory_space=pltpu.VMEM),
                pl.BlockSpec(memory_space=pltpu.VMEM),
            ),
            scratch_shapes=[
                vmem(PLANES + 4, ROWS, LANES),
                vmem(PLANES, ROWS, LANES),
                vmem(PLANES + 2, ROWS, LANES),
                vmem(PLANES, ROWS, LANES),
                vmem(2, ROWS, LANES),
                vmem(2, ROWS, LANES),
                vmem(PLANES, ROWS, LANES),
                vmem(6, LANES, LANES),
                vmem(8, 32, LANES),
                vmem(4, 32, LANES),
                vmem(4, 8, LANES),
                vmem(8, 8, LANES),
                vmem(3, 16, LANES),
                vmem(2 * REACH + 1, 8, LANES),
                vmem(3, 16, LANES),
                vmem(4, 32, LANES),
                vmem(6, ROWS, LANES),
                vmem(6, ROWS, LANES),
                vmem(PLANES, ROWS, LANES),
                vmem(PLANES, ROWS, LANES),
                vmem(2 * columns, 1, LANES),
                vmem(RING, 1, LANES),
                vmem(PLANES, ROWS, LANES, dtype=jnp.bfloat16),
                vmem(STATES, 2, ROWS, LANES, dtype=jnp.bfloat16),
                vmem(LANES, LANES),
                vmem(2 * RING, 1, LANES),
                vmem(CHIPS * columns, 1, LANES),
                vmem(LANES, 2 * LANES),
                dma((2,)), dma(()), dma((3,)), dma((2,)), dma((2,)), dma((2,)),
                dma((2,)), dma((2,)), dma((2,)), dma((2,)), dma((2,)),
                pltpu.SemaphoreType.REGULAR((5,)),
            ],
            compiler_params=pltpu.CompilerParams(
                collective_id=0, has_side_effects=True, vmem_limit_bytes=32 * 1024 * 1024
            ),
        )(*[pltpu.with_memory_space_constraint(v, pltpu.HBM) for v in (orbitals, potential)])

        return pl.pallas_call(
            write_out,
            out_shape=shapes,
            in_specs=[pl.BlockSpec(memory_space=pltpu.VMEM)] * 2,
            out_specs=(pl.BlockSpec(memory_space=pltpu.HBM), pl.BlockSpec(memory_space=pltpu.HBM)),
            scratch_shapes=[dma((2,))],
            compiler_params=pltpu.CompilerParams(vmem_limit_bytes=1024 * 1024),
        )(*results)

    return jax.shard_map(
        on_device,
        mesh=mesh,
        in_specs=(P("state", "grid", None, None), P("grid", None, None)),
        out_specs=(P("state", "grid", None, None), P("state", None)),
        check_vma=False,
    )
```

```python
import functools

import jax
import jax.numpy as jnp
from jax import lax
from jax.experimental import pallas as pl
from jax.experimental.pallas import tpu as pltpu
from jax.sharding import PartitionSpec as P

MESH = pl.DeviceIdType.MESH
HIGH = lax.Precision.HIGHEST
F32 = jnp.float32

SHIFT_TERM = 0.25
DAMPING = 2.0 / 3.0
LANES = 128
ROWS = 64
HALF = ROWS // 2
PLANES = 8
STATES = 8
CHIPS = 4
RING = 16
REACH = 4
THIRD = 1.0 / 3.0
NEAR = -2.0 / 3.0
FAR = 1.0 / 24.0


def scales(level):
    inverse = 0.25**level
    diagonal = SHIFT_TERM + 3.0 * inverse
    scaled = DAMPING / diagonal
    return scaled, 0.5 * inverse * scaled


C0, K0 = scales(0)
C1, K1 = scales(1)
C2, K2 = scales(2)
C3, K3 = scales(3)


def iota(shape, dim):
    return lax.broadcasted_iota(jnp.int32, shape, dim)


def beside(plane, segment=LANES):
    rows = plane.shape[0]
    total = pltpu.roll(plane, 1, 0) + pltpu.roll(plane, rows - 1, 0)
    low, high = pltpu.roll(plane, 1, 1), pltpu.roll(plane, LANES - 1, 1)
    if segment != LANES:
        cell = iota(plane.shape, 1) & (segment - 1)
        low = jnp.where(cell == 0, pltpu.roll(plane, LANES - segment + 1, 1), low)
        high = jnp.where(cell == segment - 1, pltpu.roll(plane, segment - 1, 1), high)
    return total + (low + high)


def beside_two(plane):
    rows = plane.shape[0]
    total = pltpu.roll(plane, 2, 0) + pltpu.roll(plane, rows - 2, 0)
    return total + (pltpu.roll(plane, 2, 1) + pltpu.roll(plane, LANES - 2, 1))


def matrices():
    k, j = iota((LANES, LANES), 0), iota((LANES, LANES), 1)
    down_h = (j < 64) & ((k >> 1) == j)
    down_o = (j >= 64) & ((k >> 1) == j - 64)
    down_two = ((k >> 6) == ((j >> 5) & 1)) & (((k & 63) >> 1) == (j & 31))
    down_three = (k < 64) & ((k >> 5) == ((j >> 4) & 1)) & (((k & 31) >> 1) == (j & 15))
    up_two = (k < 32) & ((k >> 4) == ((j >> 5) & 1)) & ((k & 15) == ((j & 31) >> 1))
    up_one = (k < 64) & ((k >> 5) == (j >> 6)) & ((k & 31) == ((j & 63) >> 1))
    up_h = k == (j >> 1)
    up_o = k - 64 == (j >> 1)
    eighth, one = jnp.full((LANES, LANES), 0.125, F32), jnp.ones((LANES, LANES), F32)
    zero = jnp.zeros((LANES, LANES), F32)
    return [
        jnp.where(mask, eighth, zero) for mask in (down_h, down_o, down_two, down_three)
    ] + [jnp.where(mask, one, zero) for mask in (up_two, up_one, up_h, up_o)]


def times(left, right):
    return jnp.dot(left, right, precision=HIGH, preferred_element_type=F32)


def kernel(
    slabs,
    o_hbm, p_hbm, out_ref, gram_ref,
    o_buf, p_buf, h_buf, r_buf, g_out, g_in, pair_buf, mats,
    f1_buf, two_buf, f2_out, f2_in, three_buf, f3_in,
    up2_buf, up1_buf, uph_buf, upo_buf, a_buf, b_buf,
    e_y, e_z, rounded, mixed, rows_buf, g_z, g_xy, wide,
    load_sem, halo_send, halo_recv, f1_sem, f2_sem, f3_sem, ey_sem, ez_sem, x_sem, gz_sem, gx_sem,
    token,
):
    g, s = lax.axis_index("grid"), lax.axis_index("state")
    y, z = g >> 4, g & (RING - 1)
    x, core = s >> 1, s & 1
    columns = slabs // RING

    def slab(step):
        return ((g + step) & (slabs - 1), s)

    def on_ring(step):
        return (y * RING + ((z + step) & (RING - 1)), s)

    def on_column(step):
        return (((y + step) & (columns - 1)) * RING + z, s)

    hub = core == 1
    chip_states = (s - core, s - core + 1)

    def state_at(step, other):
        return 2 * ((x + step) & (CHIPS - 1)) + (1 - core if other else core)

    def on_face(step):
        up, side = step // STATES, step % STATES
        return (((y + up) & (columns - 1)) * RING + z, (s + side) & (STATES - 1))

    def each_core(zero, one):
        pl.when(core == 0)(zero)
        pl.when(core == 1)(one)

    def send(src, dst, sems, peer):
        copy = pltpu.make_async_remote_copy(
            src_ref=src, dst_ref=dst, send_sem=sems[0], recv_sem=sems[1],
            device_id=peer, device_id_type=MESH,
        )
        copy.start()

    def take(sem, view):
        pltpu.make_async_copy(view, view, sem).wait()

    def signal(sem, peers):
        for peer in peers:
            pl.semaphore_signal(sem, inc=1, device_id=peer, device_id_type=MESH)

    others = [(step, other) for step in (2, 1, -1) for other in (False, True)] + [(0, True)]
    next_two = [slab(1), slab(-1), on_ring(2), on_ring(-2)]
    partner = (g, state_at(0, True))
    next_two += [on_column(1), on_column(-1), (g, state_at(1, False)), (g, state_at(-1, False))]
    close = next_two + [on_ring(1), on_ring(-1), partner]
    barrier = pltpu.get_barrier_semaphore()
    signal(barrier, close)
    loads = [
        pltpu.make_async_copy(o_hbm.at[0], o_buf.at[pl.ds(2, PLANES)], load_sem.at[0]),
        pltpu.make_async_copy(p_hbm, p_buf, load_sem.at[1]),
    ]
    for load in loads:
        load.start()
    with jax.named_scope("w_load"):
        for load in loads:
            load.wait()
    with jax.named_scope("w_barrier"):
        pl.semaphore_wait(barrier, len(close))

    right, left = slab(1), slab(-1)

    def halo(part, mine, theirs):
        sems = (halo_send, halo_recv.at[part])
        send(o_buf.at[pl.ds(8, 2), pl.ds(mine, HALF)], o_buf.at[pl.ds(0, 2), pl.ds(mine, HALF)], sems, right)
        send(o_buf.at[pl.ds(2, 2), pl.ds(theirs, HALF)], o_buf.at[pl.ds(10, 2), pl.ds(theirs, HALF)], sems, left)

    signal(token.at[0], next_two)
    halo(0, 0, HALF)
    g_out[0] = p_buf[0] * o_buf[2] + FAR * o_buf[4]
    g_out[1] = p_buf[7] * o_buf[9] + FAR * o_buf[7]

    top = jnp.zeros((ROWS, LANES), F32)
    bottom = jnp.zeros((ROWS, LANES), F32)
    for p in range(PLANES):
        centre = o_buf[p + 2]
        first, second = beside(centre), beside_two(centre)
        for q in (p - 1, p + 1):
            if 0 <= q < PLANES:
                first += o_buf[q + 2]
        for q in (p - 2, p + 2):
            if 0 <= q < PLANES:
                second += o_buf[q + 2]
        value = (3.75 + p_buf[p]) * centre + NEAR * first + FAR * second
        h_buf[p + 1] = value
        r_buf[p] = centre * THIRD + K0 * first
        top += centre * value
        bottom += centre * centre
    halo(1, HALF, 0)
    sems = (halo_send, halo_recv.at[2])
    send(g_out.at[1], g_in.at[0], sems, right)
    send(g_out.at[0], g_in.at[1], sems, left)
    made = matrices()
    for index in range(6):
        mats[index] = made[index]
    wide[:, :LANES] = made[6]
    wide[:, LANES:] = made[7]
    rows_buf[...] = jnp.zeros_like(rows_buf)
    top, bottom = jnp.sum(top, 0, keepdims=True), jnp.sum(bottom, 0, keepdims=True)
    lane_row = iota((1, LANES), 1)

    with jax.named_scope("w_t1"):
        pl.semaphore_wait(token.at[0], len(next_two))
    signal(token.at[1], [on_ring(4), on_ring(-4)])
    signal(token.at[3], [partner])
    signal(token.at[2], [slab(2), slab(-2)])
    with jax.named_scope("w_halo_a"):
        take(halo_recv.at[0], o_buf.at[pl.ds(0, 2)])
    cross = o_buf[2, :HALF] * (2.0 * NEAR * o_buf[1, :HALF] + 2.0 * FAR * o_buf[0, :HALF])
    cross += 2.0 * FAR * o_buf[1, :HALF] * o_buf[3, :HALF]
    cross += o_buf[9, HALF:] * (2.0 * NEAR * o_buf[10, HALF:] + 2.0 * FAR * o_buf[11, HALF:])
    cross += 2.0 * FAR * o_buf[10, HALF:] * o_buf[8, HALF:]
    top += jnp.sum(cross, 0, keepdims=True)
    e_y[core * columns + y] = jnp.where(
        lane_row < 64, top + pltpu.roll(top, 64, 1), bottom + pltpu.roll(bottom, 64, 1)
    )
    pl.semaphore_wait(token.at[3], 1)

    def to_hubs(steps):
        mine = e_y.at[core * columns + y]
        for d in steps:
            send(mine, mine, (ey_sem.at[0], ey_sem.at[1]), (on_column(d)[0], chip_states[1]))

    each_core(lambda: to_hubs((2, 1, 3, 0)), lambda: to_hubs((2, 1, 3)))

    with jax.named_scope("w_halo_b"):
        take(halo_recv.at[1], o_buf.at[pl.ds(0, 2)])
        take(halo_recv.at[2], g_in)
    h_buf[1] += NEAR * o_buf[1] + FAR * o_buf[0]
    h_buf[2] += FAR * o_buf[1]
    h_buf[8] += NEAR * o_buf[10] + FAR * o_buf[11]
    h_buf[7] += FAR * o_buf[10]
    r_buf[0] += K0 * o_buf[1]
    r_buf[7] += K0 * o_buf[10]
    for ghost, at, inner, outer, side in ((1, 0, 2, 0, 0), (10, 9, 9, 11, 1)):
        centre = o_buf[ghost]
        first = (o_buf[inner] + o_buf[outer]) + beside(centre)
        second = o_buf[2 * inner - ghost] + beside_two(centre)
        h_buf[at] = 3.75 * centre + g_in[side] + NEAR * first + FAR * second
    for q in range(PLANES // 2):
        both = None
        for p in (2 * q, 2 * q + 1):
            value = h_buf[p + 1]
            rest = value * THIRD + K0 * ((h_buf[p] + h_buf[p + 2]) + beside(value))
            a_buf[p] = C0 * (value + rest)
            b_buf[p] = C0 * (o_buf[p + 2] + r_buf[p])
            both = rest if both is None else both + rest
        pair_buf[q] = both
        pair_buf[q + 4] = r_buf[2 * q] + r_buf[2 * q + 1]
    halved = pair_buf[:, pl.ds(0, 32, 2), :] + pair_buf[:, pl.ds(1, 32, 2), :]
    halved = [halved[:4].reshape(LANES, LANES), halved[4:].reshape(LANES, LANES)]
    f1 = times(jnp.concatenate(halved, 1), mats[0:2].reshape(2 * LANES, LANES))
    f1 = f1.reshape(4, 32, LANES)
    f1_buf[2:6] = f1
    sems = (f1_sem.at[0], f1_sem.at[1])
    send(f1_buf.at[pl.ds(4, 2)], f1_buf.at[pl.ds(0, 2)], sems, right)
    send(f1_buf.at[pl.ds(2, 2)], f1_buf.at[pl.ds(6, 2)], sems, left)

    rest = []
    for p in range(4):
        total = beside(f1[p], 64)
        for q in (p - 1, p + 1):
            if 0 <= q < 4:
                total += f1[q]
        rest.append(f1[p] * THIRD + K1 * total)
    two_buf[0] = K1 * f1[0]
    two_buf[1] = rest[0] + rest[1]
    two_buf[2] = rest[2] + rest[3]
    two_buf[3] = K1 * f1[3]
    halved = two_buf[:, pl.ds(0, 16, 2), :] + two_buf[:, pl.ds(1, 16, 2), :]
    share = times(halved.reshape(64, LANES), mats[2]).reshape(4, 16, LANES)
    low = iota((8, LANES), 1) < 64
    for k in range(4):
        f2_out[k] = jnp.where(low, share[k][:8], share[k][8:])
    a, b, c, d = share[0], share[1], share[2], share[3]
    three_buf[0] = a * (K2 + THIRD) + K2 * (b + beside(a, 32))
    three_buf[1] = (b + c) * (THIRD + K2) + K2 * ((a + d) + (beside(b, 32) + beside(c, 32)))
    three_buf[2] = d * (K2 + THIRD) + K2 * (c + beside(d, 32))
    halved = three_buf[:, pl.ds(0, 8, 2), :] + three_buf[:, pl.ds(1, 8, 2), :]
    parts = times(halved.reshape(24, LANES), mats[3]).reshape(3, 8, LANES)
    lane = iota((8, LANES), 1)
    f3_in[REACH] = jnp.where(
        lane < 32, parts[0],
        jnp.where(lane < 64, parts[1], jnp.where(lane < 96, parts[2], 0.0)),
    )
    with jax.named_scope("w_t2"):
        pl.semaphore_wait(token.at[2], 2)
    sems = (f3_sem.at[0], f3_sem.at[1])
    for step in range(REACH, 0, -1):
        send(f3_in.at[REACH], f3_in.at[REACH - step], sems, slab(step))
        send(f3_in.at[REACH], f3_in.at[REACH + step], sems, slab(-step))
    sems = (f2_sem.at[0], f2_sem.at[1])
    send(f2_out.at[pl.ds(1, 3)], f2_in.at[pl.ds(0, 3)], sems, right)
    send(f2_out.at[pl.ds(0, 3)], f2_in.at[pl.ds(3, 3)], sems, left)
    send(f2_out.at[3], f2_in.at[6], sems, slab(2))
    send(f2_out.at[0], f2_in.at[7], sems, slab(-2))

    with jax.named_scope("w_t3"):
        pl.semaphore_wait(token.at[1], 2)
    far_first = sorted(range(1, RING), key=lambda d: abs(d - RING // 2))

    @pl.when(core == 0)
    def _():
        signal(token.at[4], [partner])

    @pl.when(hub)
    def _():
        pl.semaphore_wait(token.at[4], 1)
        take(ey_sem.at[1], e_y.at[pl.ds(0, 2 * columns - 1)])
        first = jnp.sum(e_y[:columns], axis=0)
        second = jnp.sum(e_y[columns:], axis=0)
        first, second = first + pltpu.roll(first, 96, 1), second + pltpu.roll(second, 96, 1)
        e_z[z] = jnp.where(
            lane_row < 64,
            jnp.where(lane_row < 32, first, pltpu.roll(first, 96, 1)),
            jnp.where(lane_row < 96, pltpu.roll(second, 64, 1), pltpu.roll(second, 32, 1)),
        )
        for state in chip_states:
            for d in far_first:
                send(e_z.at[z], e_z.at[z], (ez_sem.at[0], ez_sem.at[1]), (on_ring(d)[0], state))
        send(e_z.at[z], e_z.at[z], (ez_sem.at[0], ez_sem.at[1]), partner)

    with jax.named_scope("w_f"):
        take(f3_sem.at[1], f3_in.at[pl.ds(0, 2 * REACH)])
        take(f2_sem.at[1], f2_in)
        take(f1_sem.at[1], f1_buf.at[pl.ds(0, 4)])

    source = {}
    for p in range(1 - REACH, REACH):
        at = p + REACH
        total = jnp.where(lane < 32, f3_in[at + 1], jnp.where(lane < 64, f3_in[at], f3_in[at - 1]))
        total = total + pltpu.roll(total, 32, 1)
        source[p] = total + pltpu.roll(total, 64, 1)
    iterate = {p: C3 * source[p] for p in source}
    for reach in (2, 1):
        iterate = {
            p: iterate[p] * THIRD + C3 * source[p]
            + K3 * ((iterate[p - 1] + iterate[p + 1]) + beside(iterate[p], 16))
            for p in range(-reach, reach + 1)
        }
    spread = times(jnp.concatenate([iterate[p] for p in range(-1, 2)], 0), mats[4]).reshape(3, 8, LANES)
    up2_buf[:, pl.ds(0, 8, 2), :] = spread
    up2_buf[:, pl.ds(1, 8, 2), :] = spread

    def unfold(tile):
        turned = pltpu.roll(tile, 64, 1)
        return jnp.concatenate([jnp.where(low, tile, turned), jnp.where(low, turned, tile)], 0)

    f2 = {
        -2: unfold(f2_in[0] + f2_in[6]),
        -1: share[0] + unfold(f2_in[1]),
        0: share[1] + unfold(f2_in[2]),
        1: share[2] + unfold(f2_in[3]),
        2: share[3] + unfold(f2_in[4]),
        3: unfold(f2_in[5] + f2_in[7]),
    }
    fixed = {p: C2 * f2[p] + up2_buf[(p >> 1) + 1] for p in range(-2, 4)}
    value = [
        fixed[p] * THIRD + C2 * f2[p] + K2 * ((fixed[p - 1] + fixed[p + 1]) + beside(fixed[p], 32))
        for p in range(-1, 3)
    ]
    spread = times(jnp.concatenate(value, 0), mats[5]).reshape(4, 16, LANES)
    up1_buf[:, pl.ds(0, 16, 2), :] = spread
    up1_buf[:, pl.ds(1, 16, 2), :] = spread
    fixed = {p: C1 * f1_buf[p + 2] + up1_buf[(p >> 1) + 1] for p in range(-2, 6)}
    error = jnp.concatenate(
        [
            fixed[p] * THIRD + C1 * f1_buf[p + 2]
            + K1 * ((fixed[p - 1] + fixed[p + 1]) + beside(fixed[p], 64))
            for p in range(-1, 5)
        ],
        0,
    )

    spread = times(error, wide[...])
    for at, up_buf, last in ((0, uph_buf, a_buf), (LANES, upo_buf, b_buf)):
        part = spread[:, at : at + LANES].reshape(6, 32, LANES)
        up_buf[:, pl.ds(0, 32, 2), :] = part
        up_buf[:, pl.ds(1, 32, 2), :] = part
        for q in range(1, 5):
            value = up_buf[q]
            same = value * (THIRD + K0) + K0 * beside(value)
            last[2 * q - 2] += same + K0 * up_buf[q - 1]
            last[2 * q - 1] += same + K0 * up_buf[q + 1]
    each_core(
        lambda: take(ez_sem.at[1], e_z.at[pl.ds(0, RING)]),
        lambda: take(ez_sem.at[1], e_z.at[pl.ds(0, RING - 1)]),
    )
    with jax.named_scope("w_ez"):
        sums = jnp.sum(e_z[...], axis=0)
    part = lane_row >> 5
    numer = jnp.sum(jnp.where(part == 2 * core, sums, 0.0), axis=1, keepdims=True)
    denom = jnp.sum(jnp.where(part == 2 * core + 1, sums, 0.0), axis=1, keepdims=True)
    energy = numer / denom

    def finish(p):
        value = a_buf[p] - energy * b_buf[p]
        out_ref[0, p] = value
        return value.astype(jnp.bfloat16)

    def to_hub(step):
        chip = (x + step) & (CHIPS - 1)
        for plane in (0, 1):
            rounded[2 * chip + plane] = finish(2 * chip + plane)
        send(
            rounded.at[pl.ds(2 * chip, 2)], mixed.at[s], (x_sem.at[0], x_sem.at[1]), (g, 2 * chip + 1)
        )

    for step in (2, 1, -1):
        to_hub(step)

    @pl.when(core == 0)
    def _():
        to_hub(0)

    @pl.when(hub)
    def _():
        for plane in (0, 1):
            mixed[s, plane] = finish(2 * x + plane)
        take(x_sem.at[1], mixed.at[pl.ds(0, STATES - 1)])
        pairs = [(i, j) for i in range(STATES) for j in range(i, STATES)]
        held = {pair: None for pair in pairs}
        for at in range(2 * ROWS // 16):
            rows = slice(16 * at % ROWS, 16 * at % ROWS + 16)
            values = [mixed[i, 16 * at // ROWS, rows].astype(F32) for i in range(STATES)]
            for i, j in pairs:
                product = values[i] * values[j]
                product = product[:8] + product[8:]
                held[i, j] = product if held[i, j] is None else held[i, j] + product
        for i, j in pairs:
            row = jnp.sum(held[i, j], 0, keepdims=True)
            rows_buf[8 * i + j : 8 * i + j + 1] = row
            if i != j:
                rows_buf[8 * j + i : 8 * j + i + 1] = row
        flat = lax.dot_general(
            jnp.ones((8, LANES), F32), rows_buf[...], (((1,), (1,)), ((), ())),
            precision=HIGH, preferred_element_type=F32,
        )
        g_z[z] = flat[:1]
        for d in far_first:
            send(g_z.at[z], g_z.at[z], (gz_sem.at[0], gz_sem.at[1]), on_ring(d))
        take(gz_sem.at[1], g_z.at[pl.ds(0, RING - 1)])
        place = y * CHIPS + x
        g_xy[place] = jnp.sum(g_z[:RING], axis=0)
        order = {d: abs(d // STATES - 2) + abs(d % STATES - 4) / 2 - d % 2 for d in range(1, STATES * columns)}
        for d in sorted(order, key=order.get):
            send(g_xy.at[place], g_xy.at[place], (gx_sem.at[0], gx_sem.at[1]), on_face(d))

    with jax.named_scope("w_sends"):
        take(halo_send, o_buf.at[pl.ds(0, 6)])
        take(f1_sem.at[0], f1_buf.at[pl.ds(0, 4)])
        take(f2_sem.at[0], f2_in)
        take(f3_sem.at[0], f3_in.at[pl.ds(0, 2 * REACH)])

    @pl.when(core == 0)
    def _():
        take(ey_sem.at[0], g_z.at[pl.ds(0, columns)])
        take(x_sem.at[0], mixed.at[pl.ds(0, CHIPS)])
        take(gx_sem.at[1], g_xy)

    @pl.when(hub)
    def _():
        take(ey_sem.at[0], g_z.at[pl.ds(0, columns - 1)])
        take(ez_sem.at[0], g_z.at[pl.ds(0, 2 * RING - 1)])
        take(x_sem.at[0], mixed.at[pl.ds(0, CHIPS - 1)])
        take(gz_sem.at[0], g_z.at[pl.ds(0, RING - 1)])
        take(gx_sem.at[1], g_xy.at[pl.ds(0, CHIPS * columns - 1)])

    total = jnp.sum(g_xy[...], axis=0)
    picked = jnp.zeros((1, STATES), F32)
    for t in range(STATES):
        picked += jnp.where(s == t, total[:, STATES * t : STATES * t + STATES], 0.0)
    gram_ref[...] = picked / F32(PLANES * ROWS * LANES * slabs)
    pl.when(hub)(lambda: take(gx_sem.at[0], g_z.at[pl.ds(0, STATES * columns - 1)]))


def solution(mesh):
    slabs = mesh.shape["grid"]
    columns = slabs // RING
    dma = pltpu.SemaphoreType.DMA

    def vmem(*shape, dtype=F32):
        return pltpu.VMEM(shape, dtype)

    def write_out(values, gram, values_hbm, gram_hbm, sem):
        copies = [
            pltpu.make_async_copy(values, values_hbm, sem.at[0]),
            pltpu.make_async_copy(gram, gram_hbm, sem.at[1]),
        ]
        for copy in copies:
            copy.start()
        for copy in copies:
            copy.wait()

    def on_device(orbitals, potential):
        shapes = (
            jax.ShapeDtypeStruct((1, PLANES, ROWS, LANES), F32),
            jax.ShapeDtypeStruct((1, STATES), F32),
        )
        results = pl.pallas_call(
            functools.partial(kernel, slabs),
            out_shape=(
                jax.ShapeDtypeStruct((1, PLANES, ROWS, LANES), F32),
                jax.ShapeDtypeStruct((1, STATES), F32),
            ),
            in_specs=[pl.BlockSpec(memory_space=pltpu.HBM)] * 2,
            out_specs=(
                pl.BlockSpec(memory_space=pltpu.VMEM),
                pl.BlockSpec(memory_space=pltpu.VMEM),
            ),
            scratch_shapes=[
                vmem(PLANES + 4, ROWS, LANES),
                vmem(PLANES, ROWS, LANES),
                vmem(PLANES + 2, ROWS, LANES),
                vmem(PLANES, ROWS, LANES),
                vmem(2, ROWS, LANES),
                vmem(2, ROWS, LANES),
                vmem(PLANES, ROWS, LANES),
                vmem(6, LANES, LANES),
                vmem(8, 32, LANES),
                vmem(4, 32, LANES),
                vmem(4, 8, LANES),
                vmem(8, 8, LANES),
                vmem(3, 16, LANES),
                vmem(2 * REACH + 1, 8, LANES),
                vmem(3, 16, LANES),
                vmem(4, 32, LANES),
                vmem(6, ROWS, LANES),
                vmem(6, ROWS, LANES),
                vmem(PLANES, ROWS, LANES),
                vmem(PLANES, ROWS, LANES),
                vmem(2 * columns, 1, LANES),
                vmem(RING, 1, LANES),
                vmem(PLANES, ROWS, LANES, dtype=jnp.bfloat16),
                vmem(STATES, 2, ROWS, LANES, dtype=jnp.bfloat16),
                vmem(LANES, LANES),
                vmem(2 * RING, 1, LANES),
                vmem(CHIPS * columns, 1, LANES),
                vmem(LANES, 2 * LANES),
                dma((2,)), dma(()), dma((3,)), dma((2,)), dma((2,)), dma((2,)),
                dma((2,)), dma((2,)), dma((2,)), dma((2,)), dma((2,)),
                pltpu.SemaphoreType.REGULAR((5,)),
            ],
            compiler_params=pltpu.CompilerParams(
                collective_id=0, has_side_effects=True, vmem_limit_bytes=32 * 1024 * 1024
            ),
        )(*[pltpu.with_memory_space_constraint(v, pltpu.HBM) for v in (orbitals, potential)])

        return pl.pallas_call(
            write_out,
            out_shape=shapes,
            in_specs=[pl.BlockSpec(memory_space=pltpu.VMEM)] * 2,
            out_specs=(pl.BlockSpec(memory_space=pltpu.HBM), pl.BlockSpec(memory_space=pltpu.HBM)),
            scratch_shapes=[dma((2,))],
            compiler_params=pltpu.CompilerParams(vmem_limit_bytes=1024 * 1024),
        )(*results)

    return jax.shard_map(
        on_device,
        mesh=mesh,
        in_specs=(P("state", "grid", None, None), P("grid", None, None)),
        out_specs=(P("state", "grid", None, None), P("state", None)),
        check_vma=False,
    )
```
